32 devices in a mesh: groups: 2 (over y), frame: 4 (over z), tensor: 4 (over x, core).
Axes of the slice: x: 2, y: 2, z: 4, core: 2. Of those that a mesh axis runs over, the one named last changes fastest.
Arguments:
- latent: bfloat16 [6, 1024, 1024], P(None, ('groups', 'frame')), parts along dimension 1, may hold values from -17 to 17
- norm1_gain: float32 [1024], replicated, may hold values from 0.1 to 1.9
- conv1_weight: bfloat16 [3, 1024, 1024], P(None, None, 'tensor'), may hold values from -0.109375 to 0.109375
- time_bias: float32 [1024], P('tensor'), may hold values from -4 to 4
- norm2_gain: float32 [1024], P('tensor'), may hold values from 0.1 to 1.9
- conv2_weight: bfloat16 [3, 1024, 1024], P(None, 'tensor'), may hold values from -0.375 to 0.375
- attn_gain: float32 [1024], replicated, may hold values from 0.1 to 1.9
- qkv_weight: bfloat16 [1024, 3, 1024], P(None, None, 'tensor'), may hold values from -2 to 2
- out_weight: bfloat16 [1024, 1024], P('tensor'), may hold values from -0.1875 to 0.1875
Outputs:
- velocity: bfloat16 [6, 1024, 1024], P(None, ('groups', 'frame'), 'tensor'), parts along dimension 1
The draws below stay inside these ranges and needn't reach their ends.
There are 2 independent parts, one for each index of `groups`. The reference program is written for one: setup_inputs(seed, part) draws one part's arguments, and reference() takes and returns one part's arrays. A program takes and returns all parts, laid end to end along the dimension named above; an argument that names none is the same for every part. Nothing has to cross between parts.
All inputs are finite; a program needn't handle non-finite values.
Results may differ from the reference program's by a relative error of at most 0.014.
Values may be sent and summed in bfloat16 or wider, within the bound.
No kernel may reach another device: no remote copies, remote signals or barrier semaphores. Data moves between devices by JAX's collectives and lax.ppermute only.
A program may use at most 64 MiB of HBM per device.

```python
import math
import jax
import jax.numpy as jnp
from jax import lax

D = 1024
GROUPS = 32
HEADS = 16
HEAD_DIM = 64
STEMS = 6
WINDOW = 64
FRAMES = 512
N_TENSOR = 4


def draw_latent(key, part):
    key_base, key_rough = jax.random.split(key, 2)
    position = jnp.arange(FRAMES).astype(jnp.float32) / (FRAMES - 1)
    rising = 1.0 + 2.0 * position
    rough = jax.random.uniform(key_rough, (STEMS, FRAMES, 1), jnp.float32, 0.6, 1.4)
    base = jnp.clip(jax.random.normal(key_base, (STEMS, FRAMES, D), jnp.float32), -4.0, 4.0)
    return (base * rising[None, :, None] * rough).astype(jnp.bfloat16)


def draw_qkv_weight(key, part):
    key_base = jax.random.fold_in(key, 0)
    base = jnp.clip(jax.random.normal(key_base, (D, 3, D), jnp.float32), -4.0, 4.0) / math.sqrt(D)
    return base.astype(jnp.bfloat16)


def level_of(own_key, dims, shards, smallest, top_value):
    loudness = 1.0
    for dim, shards_of in shards:
        heights = jax.random.uniform(jax.random.fold_in(jax.random.fold_in(own_key, 6), dim), (shards_of,), jnp.float32, smallest / len(shards), top_value / len(shards))
        loudness = loudness * jnp.repeat(jnp.exp(heights), dims[dim] // shards_of).reshape((-1,) + (1,) * (len(dims) - 1 - dim))
    return loudness


def centred(stream_key, extent, scale, most, cuts=(), kind=jnp.bfloat16):
    values = scale * jax.random.normal(stream_key, extent, jnp.float32)
    if cuts:
        values = values * level_of(stream_key, extent, cuts, -0.22, 0.18)
    return jnp.clip(values, -most, most).astype(kind)


def setup_inputs(seed: int = 0, part: int = 0) -> dict:
    arg_keys = jax.random.split(jax.random.key(seed), 10)
    own_keys = jax.random.split(jax.random.fold_in(arg_keys[9], part), 10)
    return {
        "latent": draw_latent(jax.random.fold_in(jax.random.fold_in(arg_keys[9], part), 71), part),
        "norm1_gain": jnp.clip(1.0 + 0.18 * jax.random.normal(arg_keys[1], (D,), jnp.float32), 0.1, 1.9),
        "conv1_weight": centred(arg_keys[2], (3, D, D), (3 * D) ** -0.5, 0.109375, ((2, 4),)),
        "time_bias": centred(arg_keys[3], (D,), 1.0, 4.0, ((0, 4),), jnp.float32),
        "norm2_gain": jnp.clip(1.0 + 0.18 * jax.random.normal(arg_keys[4], (D,), jnp.float32), 0.1, 1.9),
        "conv2_weight": centred(arg_keys[5], (3, D, D), (D // 4) ** -0.5, 0.375, ((1, 4),)),
        "attn_gain": jnp.clip(1.0 + 0.18 * jax.random.normal(arg_keys[6], (D,), jnp.float32), 0.1, 1.9),
        "qkv_weight": draw_qkv_weight(jax.random.fold_in(arg_keys[9], 71), part),
        "out_weight": centred(arg_keys[8], (D, D), D ** -0.5, 0.1875, ((0, 4),)),
    }


norm_eps = 1e-05
rms_eps = 1e-06

def group_norm(hidden, gain_vec, group_count):
    stem_count, frame_count, channels = hidden.shape
    grouped = hidden.reshape(stem_count, frame_count, group_count, channels // group_count)
    centre = lax.optimization_barrier(jnp.mean(grouped, axis=(1, 3), keepdims=True))
    square = lax.optimization_barrier(jnp.mean(grouped * grouped, axis=(1, 3), keepdims=True))
    scaled = (grouped - centre) * lax.rsqrt(square - centre * centre + norm_eps)
    return scaled.reshape(stem_count, frame_count, channels) * gain_vec

def conv_three(inputs, kernel):
    stem_count, frame_count, channels = inputs.shape
    padded = jnp.pad(inputs, ((0, 0), (1, 1), (0, 0)))
    result = jnp.zeros((stem_count * frame_count, kernel.shape[2]), jnp.float32)
    for tap_index in range(3):
        tap_rows = padded[:, tap_index:tap_index + frame_count].reshape(stem_count * frame_count, channels)
        result = result + jnp.dot(tap_rows, kernel[tap_index], preferred_element_type=jnp.float32)
    return result.reshape(stem_count, frame_count, kernel.shape[2])

def bf16_term(value):
    rounded = value.astype(jnp.bfloat16)
    rounded = lax.optimization_barrier(rounded)
    return rounded.astype(jnp.float32)

def window_attention(queries, keys_all, values):
    stem_count, frame_count, head_count, head_dim = queries.shape

    def one_window(window_no):
        first_frame = window_no * WINDOW

        def tokens(source):
            window_slab = lax.dynamic_slice_in_dim(source, first_frame, WINDOW, 1)
            return window_slab.reshape(stem_count * WINDOW, head_count, head_dim).astype(jnp.float32)
        scores = jnp.einsum('qhd,khd->hqk', tokens(queries), tokens(keys_all), precision=lax.Precision.HIGHEST) / math.sqrt(head_dim)
        scores = scores - lax.optimization_barrier(jnp.max(scores, axis=2, keepdims=True))
        exp_scores = jnp.exp(scores)
        attn_probs = (exp_scores / lax.optimization_barrier(jnp.sum(exp_scores, axis=2, keepdims=True))).astype(jnp.bfloat16)
        context = jnp.einsum('hqk,khd->qhd', attn_probs.astype(jnp.float32), tokens(values))
        return context.astype(jnp.bfloat16)
    window_ids = jnp.arange(frame_count // WINDOW).astype(jnp.int32)
    stacked = lax.map(one_window, window_ids)
    stacked = stacked.reshape(frame_count // WINDOW, stem_count, WINDOW, head_count * head_dim)
    return stacked.transpose(1, 0, 2, 3).reshape(stem_count, frame_count, head_count * head_dim)

def reference(latent, norm1_gain, conv1_weight, time_bias, norm2_gain, conv2_weight, attn_gain, qkv_weight, out_weight):
    latent_f = latent.astype(jnp.float32)
    act_one = jax.nn.silu(group_norm(latent_f, norm1_gain, GROUPS)).astype(jnp.bfloat16)
    hid_one = conv_three(act_one, conv1_weight) + time_bias
    act_two = jax.nn.silu(group_norm(hid_one, norm2_gain, GROUPS)).astype(jnp.bfloat16)
    shard_width = D // N_TENSOR
    conv_total = jnp.zeros(latent.shape, jnp.float32)
    for shard_no in range(N_TENSOR):
        lo_edge = shard_no * shard_width
        partial_value = conv_three(act_two[:, :, lo_edge:lo_edge + shard_width], conv2_weight[:, lo_edge:lo_edge + shard_width, :])
        conv_total = conv_total + bf16_term(partial_value)
    residual = (latent_f + conv_total).astype(jnp.bfloat16)
    res_f = residual.astype(jnp.float32)
    mean_sq = lax.optimization_barrier(jnp.mean(res_f * res_f, axis=2, keepdims=True))
    normed = (res_f * lax.rsqrt(mean_sq + rms_eps) * attn_gain).astype(jnp.bfloat16)
    rows_all = normed.reshape(STEMS * FRAMES, D)

    def project(which):
        product = jnp.dot(rows_all, qkv_weight[:, which, :], preferred_element_type=jnp.float32)
        return product.reshape(STEMS, FRAMES, HEADS, HEAD_DIM)
    values = project(2).astype(jnp.bfloat16)
    context = window_attention(project(0), project(1), values)
    context_rows = context.reshape(STEMS * FRAMES, D)
    attn_total = jnp.zeros((STEMS * FRAMES, D), jnp.float32)
    for shard_no in range(N_TENSOR):
        lo_edge = shard_no * shard_width
        partial_value = jnp.dot(context_rows[:, lo_edge:lo_edge + shard_width], out_weight[lo_edge:lo_edge + shard_width], preferred_element_type=jnp.float32)
        attn_total = attn_total + bf16_term(partial_value)
    velocity = res_f + attn_total.reshape(STEMS, FRAMES, D)
    return velocity.astype(jnp.bfloat16)
```

```python
import functools
import math

import jax
import jax.numpy as jnp
from jax import lax
from jax.experimental import pallas as pl
from jax.experimental.pallas import tpu as pltpu
from jax.sharding import PartitionSpec as P

GROUPS = 32
HEAD_DIM = 64
WINDOW = 64
LANES = 128

norm_eps = 1e-05
rms_eps = 1e-06
HIGHEST = lax.Precision.HIGHEST
VMEM = pltpu.VMEM
bf16 = jnp.bfloat16
f32 = jnp.float32


def extended(block, sides, width):
    for axis, dim in sides:
        count = lax.axis_size(axis)
        forward = [(i, i + 1) for i in range(count - 1)]
        backward = [(target, source) for source, target in forward]
        low = lax.ppermute(
            lax.slice_in_dim(block, block.shape[dim] - width, None, axis=dim), axis, forward
        )
        high = lax.ppermute(lax.slice_in_dim(block, 0, width, axis=dim), axis, backward)
        block = jnp.concatenate([low, block, high], axis=dim)
    return block


def group_sums(hidden, group_count):
    stem_count, frame_count, channels = hidden.shape
    grouped = hidden.reshape(stem_count, frame_count, group_count, channels // group_count)
    return (jnp.sum(grouped, axis=(1, 3)), jnp.sum(grouped * grouped, axis=(1, 3)))


def apply_group(hidden, totals, squares, entries, gain_vec):
    stem_count, frame_count, channels = hidden.shape
    group_count = totals.shape[1]
    centre = totals / entries
    spread = squares / entries - centre * centre
    grouped = hidden.reshape(stem_count, frame_count, group_count, channels // group_count)
    scaled = (grouped - centre[:, None, :, None]) * lax.rsqrt(spread + norm_eps)[:, None, :, None]
    return scaled.reshape(stem_count, frame_count, channels) * gain_vec


def conv_padded(padded, kernel, frame_count):
    stem_count = padded.shape[0]
    channels = padded.shape[2]
    result = jnp.zeros((stem_count * frame_count, kernel.shape[2]), jnp.float32)
    for tap_index in range(3):
        tap_rows = padded[:, tap_index : tap_index + frame_count].reshape(
            stem_count * frame_count, channels
        )
        result = result + jnp.dot(tap_rows, kernel[tap_index], preferred_element_type=jnp.float32)
    return result.reshape(stem_count, frame_count, kernel.shape[2])


def attend(queries, keys_all, values):
    stem_count, frame_count, head_count, head_dim = queries.shape
    window_count = frame_count // WINDOW

    def arrange(source):
        shaped = source.reshape(stem_count, window_count, WINDOW, head_count, head_dim)
        return shaped.transpose(1, 3, 0, 2, 4).reshape(
            window_count, head_count, stem_count * WINDOW, head_dim
        )

    scores = jnp.einsum(
        "nhqd,nhkd->nhqk",
        arrange(queries),
        arrange(keys_all),
        precision=lax.Precision.HIGHEST,
        preferred_element_type=jnp.float32,
    ) / math.sqrt(head_dim)
    scores = scores - jnp.max(scores, axis=3, keepdims=True)
    exp_scores = jnp.exp(scores)
    attn_probs = (exp_scores / jnp.sum(exp_scores, axis=3, keepdims=True)).astype(jnp.bfloat16)
    context = jnp.einsum(
        "nhqk,nhkd->nhqd", attn_probs, arrange(values), preferred_element_type=jnp.float32
    ).astype(jnp.bfloat16)
    context = context.reshape(window_count, head_count, stem_count, WINDOW, head_dim).transpose(
        2, 0, 3, 1, 4
    )
    return context.reshape(stem_count * frame_count, head_count * head_dim)


def generic(
    latent,
    norm1_gain,
    conv1_weight,
    time_bias,
    norm2_gain,
    conv2_weight,
    attn_gain,
    qkv_weight,
    out_weight,
):
    stem_count, frame_count, channels = latent.shape
    tensor_size = lax.axis_size("tensor")
    shard_width = channels // tensor_size
    row_count = stem_count * frame_count
    group_entries = frame_count * lax.axis_size("frame") * (channels // GROUPS)
    latent_f = latent.astype(jnp.float32)
    sums_one, squares_one = group_sums(latent_f, GROUPS)
    sums_one, squares_one = lax.psum((sums_one, squares_one), "frame")
    act_one = jax.nn.silu(
        apply_group(latent_f, sums_one, squares_one, group_entries, norm1_gain)
    ).astype(jnp.bfloat16)
    padded_one = extended(act_one, (("frame", 1),), 1)
    hid_one = conv_padded(padded_one, conv1_weight, frame_count)
    hid_one = hid_one + time_bias
    local_groups = GROUPS // tensor_size
    sums_two, squares_two = group_sums(hid_one, local_groups)
    sums_two, squares_two = lax.psum((sums_two, squares_two), "frame")
    act_two = jax.nn.silu(
        apply_group(hid_one, sums_two, squares_two, group_entries, norm2_gain)
    ).astype(jnp.bfloat16)
    padded_two = extended(act_two, (("frame", 1),), 1)
    conv_term = conv_padded(padded_two, conv2_weight, frame_count)
    own_start = lax.axis_index("tensor") * shard_width
    qkv_flat = qkv_weight.reshape(channels, 3 * shard_width)
    conv_total = lax.psum(conv_term.astype(jnp.bfloat16), "tensor").astype(jnp.float32)
    residual = (latent_f + conv_total).astype(jnp.bfloat16)
    res_f = residual.astype(jnp.float32)
    mean_sq = jnp.mean(res_f * res_f, axis=2, keepdims=True)
    normed = (res_f * lax.rsqrt(mean_sq + rms_eps) * attn_gain).astype(jnp.bfloat16)
    projected = jnp.dot(
        normed.reshape(row_count, channels), qkv_flat, preferred_element_type=jnp.float32
    )
    res_own = lax.dynamic_slice_in_dim(res_f, own_start, shard_width, 2)
    head_local = shard_width // HEAD_DIM
    projected = projected.reshape(stem_count, frame_count, 3, head_local, HEAD_DIM)
    values = projected[:, :, 2].astype(jnp.bfloat16)
    context = attend(projected[:, :, 0], projected[:, :, 1], values)
    out_term = jnp.dot(context, out_weight, preferred_element_type=jnp.float32).reshape(
        stem_count, frame_count, channels
    )
    attn_share = lax.psum_scatter(
        out_term.astype(jnp.bfloat16), "tensor", scatter_dimension=2, tiled=True
    ).astype(jnp.float32)
    velocity = (res_own + attn_share).astype(jnp.bfloat16)
    return velocity


def silu(v):
    half = 0.5 * v
    return half + half * jnp.tanh(half)


def one_hot(rows, columns, width, by_row):
    row = lax.broadcasted_iota(jnp.int32, (rows, columns), 0)
    column = lax.broadcasted_iota(jnp.int32, (rows, columns), 1)
    if by_row:
        return (row // width == column).astype(f32)
    return (row == column // width).astype(f32)


def f32_dot(a, b):
    return jnp.dot(a, b, precision=HIGHEST, preferred_element_type=f32)


def group_totals(sums, squares, width):
    hot = one_hot(sums.shape[1], LANES, width, True)
    return f32_dot(sums, hot), f32_dot(squares, hot)


def channel_scale(refs, entries, channels, width):
    total = refs[0]
    for other in refs[1:]:
        total = total + other
    centre = total[:, :LANES] / entries
    spread = total[:, LANES:] / entries - centre * centre
    hot = one_hot(LANES, channels, width, False)
    return f32_dot(centre, hot), f32_dot(lax.rsqrt(spread + norm_eps), hot)


def stats_kernel(width, lat_ref, up_ref, down_ref, own_ref, sum_ref, square_ref):
    stems, frames, channels = lat_ref.shape
    for stem in range(stems):
        block = lat_ref[stem].astype(f32)
        sum_ref[stem : stem + 1, :] = jnp.sum(block, axis=0, keepdims=True)
        square_ref[stem : stem + 1, :] = jnp.sum(block * block, axis=0, keepdims=True)
        down_ref[stem : stem + 1, :channels] = block[:1]
        up_ref[stem : stem + 1, :channels] = block[frames - 1 :]
    sums, squares = group_totals(sum_ref[...], square_ref[...], width)
    for ref, start in ((up_ref, channels), (down_ref, channels), (own_ref, 0)):
        ref[:, start : start + LANES] = sums
        ref[:, start + LANES : start + 2 * LANES] = squares


def first_kernel(
    entries, width, frame_size,
    lat_ref, low_ref, high_ref, far_ref, own_ref, gain_ref, weight_ref, bias_ref,
    hid_ref, up_ref, down_ref, tot_ref, act_ref, edge_ref, sum_ref, square_ref,
):
    stems, frames, channels = lat_ref.shape
    shard = weight_ref.shape[2]
    place = lax.axis_index("frame")
    centre, scale = channel_scale(
        [own_ref[...], low_ref[:, channels:], high_ref[:, channels:], far_ref[...]],
        entries, channels, width,
    )
    scale = scale * gain_ref[...]
    edge_ref[...] = jnp.zeros_like(edge_ref)
    low = silu((low_ref[:, :channels] - centre) * scale)
    high = silu((high_ref[:, :channels] - centre) * scale)
    edge_ref[0:stems, :] = jnp.where(place > 0, low, 0.0)
    edge_ref[8 : 8 + stems, :] = jnp.where(place < frame_size - 1, high, 0.0)
    edge = edge_ref[...].astype(bf16)
    edge_low = jnp.dot(edge, weight_ref[0], preferred_element_type=f32)
    edge_high = jnp.dot(edge, weight_ref[2], preferred_element_type=f32)
    row = lax.broadcasted_iota(jnp.int32, (frames, shard), 0)
    bias = bias_ref[...]
    step = stems // 2
    for first in range(0, stems, step):
        for stem in range(first, first + step):
            block = lat_ref[stem].astype(f32)
            block = (block - centre[stem : stem + 1]) * scale[stem : stem + 1]
            act_ref[stem * frames : (stem + 1) * frames, :] = silu(block).astype(bf16)
        rows = act_ref[first * frames : (first + step) * frames, :]
        taps = [jnp.dot(rows, weight_ref[tap], preferred_element_type=f32) for tap in range(3)]
        for stem in range(first, first + step):
            lo = (stem - first) * frames
            before = pltpu.roll(taps[0][lo : lo + frames], 1, 0)
            after = pltpu.roll(taps[2][lo : lo + frames], frames - 1, 0)
            before = jnp.where(row == 0, edge_low[stem : stem + 1], before)
            after = jnp.where(row == frames - 1, edge_high[8 + stem : 9 + stem], after)
            hid = taps[1][lo : lo + frames] + before + after + bias
            hid_ref[stem] = hid
            sum_ref[stem : stem + 1, :] = jnp.sum(hid, axis=0, keepdims=True)
            square_ref[stem : stem + 1, :] = jnp.sum(hid * hid, axis=0, keepdims=True)
            down_ref[stem : stem + 1, :shard] = hid[:1]
            up_ref[stem : stem + 1, :shard] = hid[frames - 1 :]
    sums, squares = group_totals(sum_ref[...], square_ref[...], width)
    for ref, start in ((up_ref, shard), (down_ref, shard), (tot_ref, 0)):
        ref[:, start : start + LANES] = sums
        ref[:, start + LANES : start + 2 * LANES] = squares


def second_kernel(
    entries, width, frame_size, other,
    hid_ref, low_ref, high_ref, far_ref, own_ref, gain_ref, weight_ref,
    send_ref, keep_ref, act_ref,
):
    stems, frames, shard = hid_ref.shape
    place = lax.axis_index("frame")
    index = lax.axis_index("tensor")
    chip, core = index // 2, index % 2
    window = 1 - chip if other else chip
    centre, scale = channel_scale(
        [own_ref[...], low_ref[:, shard:], high_ref[:, shard:], far_ref[...]],
        entries, shard, width,
    )
    scale = scale * gain_ref[...]
    low = jnp.where(place > 0, silu((low_ref[:, :shard] - centre) * scale), 0.0)
    high = jnp.where(
        place < frame_size - 1, silu((high_ref[:, :shard] - centre) * scale), 0.0
    )
    row = lax.broadcasted_iota(jnp.int32, (WINDOW, shard), 0)
    half = stems // 2
    for stem in range(stems):
        start = pl.multiple_of(window * WINDOW, WINDOW)
        mean, factor = centre[stem : stem + 1], scale[stem : stem + 1]
        act = silu((hid_ref[stem, pl.ds(start, WINDOW), :] - mean) * factor)
        inner = silu((hid_ref[stem, WINDOW - 8 : WINDOW + 8, :] - mean) * factor)
        before = jnp.where(window == 0, low[stem : stem + 1], inner[7:8])
        after = jnp.where(window == 0, inner[8:9], high[stem : stem + 1])
        before = jnp.where(row == 0, before, pltpu.roll(act, 1, 0))
        after = jnp.where(row == WINDOW - 1, after, pltpu.roll(act, WINDOW - 1, 0))
        mine = core if stem < half else 1 - core
        base = jnp.where(mine == 0, half * WINDOW, 0) + (stem % half) * WINDOW
        at = pl.ds(pl.multiple_of(base, WINDOW), WINDOW)
        act_ref[at, 0:shard] = before.astype(bf16)
        act_ref[at, shard : 2 * shard] = act.astype(bf16)
        act_ref[at, 2 * shard : 3 * shard] = after.astype(bf16)
    total = jnp.dot(act_ref[...], weight_ref[...], preferred_element_type=f32)
    send_ref[...] = total[: half * WINDOW].astype(bf16)
    keep_ref[...] = total[half * WINDOW :].astype(bf16)


def split3(value):
    high = value.astype(bf16)
    rest = value - high.astype(f32)
    middle = rest.astype(bf16)
    return high, middle, (rest - middle.astype(f32)).astype(bf16)


def attention_kernel(
    mine_ref, theirs_ref, gain_ref, qkv_ref, qkv_far_ref, out_ref, out_far_ref,
    send_ref, keep_ref, res_ref, normed_ref, context_ref,
):
    rows, channels = mine_ref.shape
    shard = qkv_ref.shape[2]
    index = lax.axis_index("tensor")
    chip, core = index // 2, index % 2
    for first, ref in ((0, mine_ref), (rows, theirs_ref)):
        res = ref[...].astype(f32)
        res_ref[first : first + rows, :] = res
        mean_sq = jnp.mean(res * res, axis=1, keepdims=True)
        normed_ref[first : first + rows, :] = (
            res * lax.rsqrt(mean_sq + rms_eps) * gain_ref[...]
        ).astype(bf16)
    normed = normed_ref[...]
    lane = lax.broadcasted_iota(jnp.int32, (2 * rows, LANES), 1)
    per_tile = LANES // HEAD_DIM
    nt = (((1,), (1,)), ((), ()))
    for side, ref in enumerate((qkv_ref, qkv_far_ref)):
        queries, keys, values = [
            jnp.dot(normed, ref[which], preferred_element_type=f32) for which in range(3)
        ]
        queries = queries * (1.0 / math.sqrt(HEAD_DIM))
        values = values.astype(bf16)
        for tile in range(shard // LANES):
            at = slice(tile * LANES, (tile + 1) * LANES)
            q_high, q_mid, q_low = split3(queries[:, at])
            left = jnp.concatenate([q_high, q_mid, q_high, q_mid, q_high, q_low], axis=1)
            result = None
            for head in range(per_tile):
                inside = lane // HEAD_DIM == head
                k_high, k_mid, k_low = split3(jnp.where(inside, keys[:, at], 0.0))
                right = jnp.concatenate([k_high, k_high, k_mid, k_mid, k_low, k_high], axis=1)
                scores = lax.dot_general(left, right, nt, preferred_element_type=f32)
                scores = jnp.exp(scores - jnp.max(scores, axis=1, keepdims=True))
                total = jnp.sum(scores, axis=1, keepdims=True)
                probs = (scores / total).astype(bf16)
                part = jnp.dot(probs, values[:, at], preferred_element_type=f32)
                result = part if result is None else jnp.where(inside, part, result)
            base = side * shard + tile * LANES
            context_ref[:, base : base + LANES] = result.astype(bf16)
    context = context_ref[...]

    def term(block):
        at = pl.ds(pl.multiple_of(block * shard, shard), shard)
        near = jnp.dot(context[:, :shard], out_ref[:, at], preferred_element_type=f32)
        return near + jnp.dot(context[:, shard:], out_far_ref[:, at], preferred_element_type=f32)

    for place, goal in enumerate((1 - chip, chip)):
        at = slice(place * shard, (place + 1) * shard)
        value = term(2 * goal + 1 - core).astype(bf16)
        send_ref[:rows, at] = value[rows:]
        send_ref[rows:, at] = value[:rows]
        block = 2 * goal + core
        kept = term(block)
        keep_ref[:, at] = kept + res_ref[:, pl.ds(pl.multiple_of(block * shard, shard), shard)]


def place_kernel(own_ref, far_ref, out_ref):
    stems, frames, shard = out_ref.shape
    index = lax.axis_index("tensor")
    chip, core = index // 2, index % 2
    half = stems // 2
    for stem in range(stems):
        goal = (core if stem < half else 1 - core) * half + stem % half
        rows = slice(stem * WINDOW, (stem + 1) * WINDOW)
        near = pl.multiple_of(chip * WINDOW, WINDOW)
        away = pl.multiple_of((1 - chip) * WINDOW, WINDOW)
        out_ref[goal, pl.ds(near, WINDOW), :] = own_ref[rows, :]
        out_ref[goal, pl.ds(away, WINDOW), :] = far_ref[rows, :]


def call(kernel, name, outs, scratch, args, flops=0, moved=0):
    return pl.pallas_call(
        kernel,
        name=name,
        out_shape=[jax.ShapeDtypeStruct(shape, dtype) for shape, dtype in outs],
        in_specs=[pl.BlockSpec(memory_space=VMEM)] * len(args),
        out_specs=[pl.BlockSpec(memory_space=VMEM)] * len(outs),
        scratch_shapes=[VMEM(shape, dtype) for shape, dtype in scratch],
        compiler_params=pltpu.CompilerParams(vmem_limit_bytes=40 * 2**20),
        cost_estimate=pl.CostEstimate(flops=flops, bytes_accessed=moved, transcendentals=0),
    )(*args)


def swap_cores(value):
    return lax.ppermute(value, "tensor", [(0, 1), (1, 0), (2, 3), (3, 2)])


def swap_chips(value):
    return lax.ppermute(value, "tensor", [(0, 2), (2, 0), (1, 3), (3, 1)])


def shift_frames(value, by):
    count = lax.axis_size("frame")
    return lax.ppermute(value, "frame", [(i, (i + by) % count) for i in range(count)])


def exchange(up, down, own):
    return shift_frames(up, 1), shift_frames(down, -1), shift_frames(own, 2)


def fast(
    latent, norm1_gain, conv1_weight, time_bias, norm2_gain, conv2_weight,
    attn_gain, qkv_weight, out_weight,
):
    stems, frames, channels = latent.shape
    frame_size = lax.axis_size("frame")
    shard = conv1_weight.shape[2]
    width = channels // GROUPS
    entries = frames * frame_size * width
    half_rows = stems // 2 * WINDOW
    qkv = jnp.transpose(qkv_weight, (1, 0, 2))
    qkv_far = swap_chips(qkv)
    out_far = swap_chips(out_weight)
    wide = channels + 2 * LANES
    up, down, own = call(
        functools.partial(stats_kernel, width), "stats",
        [((stems, wide), f32), ((stems, wide), f32), ((stems, 2 * LANES), f32)],
        [((stems, channels), f32)] * 2,
        [latent],
    )
    low, high, far = exchange(up, down, own)
    narrow = shard + 2 * LANES
    hid, up2, down2, own2 = call(
        functools.partial(first_kernel, entries, width, frame_size), "first",
        [((stems, frames, shard), f32), ((stems, narrow), f32), ((stems, narrow), f32),
         ((stems, 2 * LANES), f32)],
        [((stems * frames, channels), bf16), ((16, channels), f32)] + [((stems, shard), f32)] * 2,
        [latent, low, high, far, own, norm1_gain[None], conv1_weight, time_bias[None]],
        flops=6 * stems * frames * channels * shard,
    )
    low2, high2, far2 = exchange(up2, down2, own2)
    weight2 = conv2_weight.reshape(3 * shard, channels)

    def second(other):
        return call(
            functools.partial(second_kernel, entries, width, frame_size, other),
            "second_other" if other else "second_own",
            [((half_rows, channels), bf16)] * 2,
            [((2 * half_rows, 3 * shard), bf16)],
            [hid, low2, high2, far2, own2, norm2_gain[None], weight2],
            flops=12 * half_rows * channels * shard,
        )

    send, keep = second(True)
    summed = (swap_cores(send).astype(f32) + keep.astype(f32)).astype(bf16)
    summed = swap_chips(summed)
    send_own, keep_own = second(False)
    got_own = swap_cores(send_own)
    index = lax.axis_index("tensor")
    chip, core = index // 2, index % 2
    latent_own = lax.dynamic_slice(
        latent, (core * (stems // 2), chip * WINDOW, 0), (stems // 2, WINDOW, channels)
    ).reshape(half_rows, channels)
    mine = (
        latent_own.astype(f32) + keep_own.astype(f32) + got_own.astype(f32) + summed.astype(f32)
    ).astype(bf16)
    theirs = swap_cores(mine)
    out_send, out_keep = call(
        attention_kernel, "attention",
        [((2 * half_rows, 2 * shard), bf16), ((2 * half_rows, 2 * shard), f32)],
        [((2 * half_rows, channels), f32), ((2 * half_rows, channels), bf16),
         ((2 * half_rows, 2 * shard), bf16)],
        [mine, theirs, attn_gain[None], qkv, qkv_far, out_weight, out_far],
        flops=24 * half_rows * channels * shard,
    )
    out_got = swap_cores(out_send)
    away = (out_keep[:, :shard] + out_got[:, :shard].astype(f32)).astype(bf16)
    stay = (out_keep[:, shard:] + out_got[:, shard:].astype(f32)).astype(bf16)
    arrived = swap_chips(away)
    return call(
        place_kernel, "place", [((stems, frames, shard), bf16)], [], [stay, arrived]
    )[0]


def local(*args):
    latent = args[0]
    stems, frames, channels = latent.shape
    tensor_size, frame_size = lax.axis_size("tensor"), lax.axis_size("frame")
    shard = channels // tensor_size
    suits = (
        tensor_size == 4
        and frame_size == 4
        and frames == 2 * WINDOW
        and stems % 2 == 0
        and stems <= 8
        and shard % (2 * LANES) == 0
    )
    return fast(*args) if suits else generic(*args)


def solution(mesh):
    return jax.shard_map(
        local,
        mesh=mesh,
        in_specs=(
            P(None, ("groups", "frame"), None),
            P(),
            P(None, None, "tensor"),
            P("tensor"),
            P("tensor"),
            P(None, "tensor", None),
            P(),
            P(None, None, "tensor"),
            P("tensor", None),
        ),
        out_specs=P(None, ("groups", "frame"), "tensor"),
        check_vma=False,
    )
```

```python
import functools
import math

import jax
import jax.numpy as jnp
from jax import lax
from jax.experimental import pallas as pl
from jax.experimental.pallas import tpu as pltpu
from jax.sharding import PartitionSpec as P


GROUPS = 32
HEAD_DIM = 64
WINDOW = 64
LANES = 128

norm_eps = 1e-05
rms_eps = 1e-06
HIGHEST = lax.Precision.HIGHEST
VMEM = pltpu.VMEM
bf16 = jnp.bfloat16
f32 = jnp.float32


def extended(block, sides, width):
    for axis, dim in sides:
        count = lax.axis_size(axis)
        forward = [(i, i + 1) for i in range(count - 1)]
        backward = [(target, source) for source, target in forward]
        low = lax.ppermute(
            lax.slice_in_dim(block, block.shape[dim] - width, None, axis=dim), axis, forward
        )
        high = lax.ppermute(lax.slice_in_dim(block, 0, width, axis=dim), axis, backward)
        block = jnp.concatenate([low, block, high], axis=dim)
    return block


def group_sums(hidden, group_count):
    stem_count, frame_count, channels = hidden.shape
    grouped = hidden.reshape(stem_count, frame_count, group_count, channels // group_count)
    return (jnp.sum(grouped, axis=(1, 3)), jnp.sum(grouped * grouped, axis=(1, 3)))


def apply_group(hidden, totals, squares, entries, gain_vec):
    stem_count, frame_count, channels = hidden.shape
    group_count = totals.shape[1]
    centre = totals / entries
    spread = squares / entries - centre * centre
    grouped = hidden.reshape(stem_count, frame_count, group_count, channels // group_count)
    scaled = (grouped - centre[:, None, :, None]) * lax.rsqrt(spread + norm_eps)[:, None, :, None]
    return scaled.reshape(stem_count, frame_count, channels) * gain_vec


def conv_padded(padded, kernel, frame_count):
    stem_count = padded.shape[0]
    channels = padded.shape[2]
    result = jnp.zeros((stem_count * frame_count, kernel.shape[2]), jnp.float32)
    for tap_index in range(3):
        tap_rows = padded[:, tap_index : tap_index + frame_count].reshape(
            stem_count * frame_count, channels
        )
        result = result + jnp.dot(tap_rows, kernel[tap_index], preferred_element_type=jnp.float32)
    return result.reshape(stem_count, frame_count, kernel.shape[2])


def attend(queries, keys_all, values):
    stem_count, frame_count, head_count, head_dim = queries.shape
    window_count = frame_count // WINDOW

    def arrange(source):
        shaped = source.reshape(stem_count, window_count, WINDOW, head_count, head_dim)
        return shaped.transpose(1, 3, 0, 2, 4).reshape(
            window_count, head_count, stem_count * WINDOW, head_dim
        )

    scores = jnp.einsum(
        "nhqd,nhkd->nhqk",
        arrange(queries),
        arrange(keys_all),
        precision=lax.Precision.HIGHEST,
        preferred_element_type=jnp.float32,
    ) / math.sqrt(head_dim)
    scores = scores - jnp.max(scores, axis=3, keepdims=True)
    exp_scores = jnp.exp(scores)
    attn_probs = (exp_scores / jnp.sum(exp_scores, axis=3, keepdims=True)).astype(jnp.bfloat16)
    context = jnp.einsum(
        "nhqk,nhkd->nhqd", attn_probs, arrange(values), preferred_element_type=jnp.float32
    ).astype(jnp.bfloat16)
    context = context.reshape(window_count, head_count, stem_count, WINDOW, head_dim).transpose(
        2, 0, 3, 1, 4
    )
    return context.reshape(stem_count * frame_count, head_count * head_dim)


def generic(
    latent,
    norm1_gain,
    conv1_weight,
    time_bias,
    norm2_gain,
    conv2_weight,
    attn_gain,
    qkv_weight,
    out_weight,
):
    stem_count, frame_count, channels = latent.shape
    tensor_size = lax.axis_size("tensor")
    shard_width = channels // tensor_size
    row_count = stem_count * frame_count
    group_entries = frame_count * lax.axis_size("frame") * (channels // GROUPS)
    latent_f = latent.astype(jnp.float32)
    sums_one, squares_one = group_sums(latent_f, GROUPS)
    sums_one, squares_one = lax.psum((sums_one, squares_one), "frame")
    act_one = jax.nn.silu(
        apply_group(latent_f, sums_one, squares_one, group_entries, norm1_gain)
    ).astype(jnp.bfloat16)
    padded_one = extended(act_one, (("frame", 1),), 1)
    hid_one = conv_padded(padded_one, conv1_weight, frame_count)
    hid_one = hid_one + time_bias
    local_groups = GROUPS // tensor_size
    sums_two, squares_two = group_sums(hid_one, local_groups)
    sums_two, squares_two = lax.psum((sums_two, squares_two), "frame")
    act_two = jax.nn.silu(
        apply_group(hid_one, sums_two, squares_two, group_entries, norm2_gain)
    ).astype(jnp.bfloat16)
    padded_two = extended(act_two, (("frame", 1),), 1)
    conv_term = conv_padded(padded_two, conv2_weight, frame_count)
    own_start = lax.axis_index("tensor") * shard_width
    qkv_flat = qkv_weight.reshape(channels, 3 * shard_width)
    conv_total = lax.psum(conv_term.astype(jnp.bfloat16), "tensor").astype(jnp.float32)
    residual = (latent_f + conv_total).astype(jnp.bfloat16)
    res_f = residual.astype(jnp.float32)
    mean_sq = jnp.mean(res_f * res_f, axis=2, keepdims=True)
    normed = (res_f * lax.rsqrt(mean_sq + rms_eps) * attn_gain).astype(jnp.bfloat16)
    projected = jnp.dot(
        normed.reshape(row_count, channels), qkv_flat, preferred_element_type=jnp.float32
    )
    res_own = lax.dynamic_slice_in_dim(res_f, own_start, shard_width, 2)
    head_local = shard_width // HEAD_DIM
    projected = projected.reshape(stem_count, frame_count, 3, head_local, HEAD_DIM)
    values = projected[:, :, 2].astype(jnp.bfloat16)
    context = attend(projected[:, :, 0], projected[:, :, 1], values)
    out_term = jnp.dot(context, out_weight, preferred_element_type=jnp.float32).reshape(
        stem_count, frame_count, channels
    )
    attn_share = lax.psum_scatter(
        out_term.astype(jnp.bfloat16), "tensor", scatter_dimension=2, tiled=True
    ).astype(jnp.float32)
    velocity = (res_own + attn_share).astype(jnp.bfloat16)
    return velocity


def silu(v):
    half = 0.5 * v
    return half + half * jnp.tanh(half)


def one_hot(rows, columns, width, by_row):
    row = lax.broadcasted_iota(jnp.int32, (rows, columns), 0)
    column = lax.broadcasted_iota(jnp.int32, (rows, columns), 1)
    if by_row:
        return (row // width == column).astype(f32)
    return (row == column // width).astype(f32)


def f32_dot(a, b):
    return jnp.dot(a, b, precision=HIGHEST, preferred_element_type=f32)


def group_totals(sums, squares, width):
    hot = one_hot(sums.shape[1], LANES, width, True)
    return f32_dot(sums, hot), f32_dot(squares, hot)


def channel_scale(refs, entries, channels, width):
    total = refs[0]
    for other in refs[1:]:
        total = total + other
    centre = total[:, :LANES] / entries
    spread = total[:, LANES:] / entries - centre * centre
    hot = one_hot(LANES, channels, width, False)
    return f32_dot(centre, hot), f32_dot(lax.rsqrt(spread + norm_eps), hot)


def stats_kernel(width, lat_ref, up_ref, down_ref, own_ref, sum_ref, square_ref):
    stems, frames, channels = lat_ref.shape
    for stem in range(stems):
        block = lat_ref[stem].astype(f32)
        sum_ref[stem : stem + 1, :] = jnp.sum(block, axis=0, keepdims=True)
        square_ref[stem : stem + 1, :] = jnp.sum(block * block, axis=0, keepdims=True)
        down_ref[stem : stem + 1, :channels] = block[:1]
        up_ref[stem : stem + 1, :channels] = block[frames - 1 :]
    sums, squares = group_totals(sum_ref[...], square_ref[...], width)
    for ref, start in ((up_ref, channels), (down_ref, channels), (own_ref, 0)):
        ref[:, start : start + LANES] = sums
        ref[:, start + LANES : start + 2 * LANES] = squares


def first_kernel(
    entries, width, frame_size,
    lat_ref, low_ref, high_ref, far_ref, own_ref, gain_ref, weight_ref, bias_ref,
    hid_ref, up_ref, down_ref, tot_ref, act_ref, edge_ref, sum_ref, square_ref,
):
    stems, frames, channels = lat_ref.shape
    shard = weight_ref.shape[2]
    place = lax.axis_index("frame")
    centre, scale = channel_scale(
        [own_ref[...], low_ref[:, channels:], high_ref[:, channels:], far_ref[...]],
        entries, channels, width,
    )
    scale = scale * gain_ref[...]
    edge_ref[...] = jnp.zeros_like(edge_ref)
    low = silu((low_ref[:, :channels] - centre) * scale)
    high = silu((high_ref[:, :channels] - centre) * scale)
    edge_ref[0:stems, :] = jnp.where(place > 0, low, 0.0)
    edge_ref[8 : 8 + stems, :] = jnp.where(place < frame_size - 1, high, 0.0)
    edge = edge_ref[...].astype(bf16)
    edge_low = jnp.dot(edge, weight_ref[0], preferred_element_type=f32)
    edge_high = jnp.dot(edge, weight_ref[2], preferred_element_type=f32)
    row = lax.broadcasted_iota(jnp.int32, (frames, shard), 0)
    bias = bias_ref[...]
    step = stems // 2
    for first in range(0, stems, step):
        for stem in range(first, first + step):
            block = lat_ref[stem].astype(f32)
            block = (block - centre[stem : stem + 1]) * scale[stem : stem + 1]
            act_ref[stem * frames : (stem + 1) * frames, :] = silu(block).astype(bf16)
        rows = act_ref[first * frames : (first + step) * frames, :]
        taps = [jnp.dot(rows, weight_ref[tap], preferred_element_type=f32) for tap in range(3)]
        for stem in range(first, first + step):
            lo = (stem - first) * frames
            before = pltpu.roll(taps[0][lo : lo + frames], 1, 0)
            after = pltpu.roll(taps[2][lo : lo + frames], frames - 1, 0)
            before = jnp.where(row == 0, edge_low[stem : stem + 1], before)
            after = jnp.where(row == frames - 1, edge_high[8 + stem : 9 + stem], after)
            hid = taps[1][lo : lo + frames] + before + after + bias
            hid_ref[stem] = hid
            sum_ref[stem : stem + 1, :] = jnp.sum(hid, axis=0, keepdims=True)
            square_ref[stem : stem + 1, :] = jnp.sum(hid * hid, axis=0, keepdims=True)
            down_ref[stem : stem + 1, :shard] = hid[:1]
            up_ref[stem : stem + 1, :shard] = hid[frames - 1 :]
    sums, squares = group_totals(sum_ref[...], square_ref[...], width)
    for ref, start in ((up_ref, shard), (down_ref, shard), (tot_ref, 0)):
        ref[:, start : start + LANES] = sums
        ref[:, start + LANES : start + 2 * LANES] = squares


def second_kernel(
    entries, width, frame_size, other,
    hid_ref, low_ref, high_ref, far_ref, own_ref, gain_ref, weight_ref,
    send_ref, keep_ref, act_ref,
):
    stems, _, shard = hid_ref.shape
    place = lax.axis_index("frame")
    index = lax.axis_index("tensor")
    chip, core = index // 2, index % 2
    window = 1 - chip if other else chip
    centre, scale = channel_scale(
        [own_ref[...], low_ref[:, shard:], high_ref[:, shard:], far_ref[...]],
        entries, shard, width,
    )
    scale = scale * gain_ref[...]
    low = jnp.where(place > 0, silu((low_ref[:, :shard] - centre) * scale), 0.0)
    high = jnp.where(
        place < frame_size - 1, silu((high_ref[:, :shard] - centre) * scale), 0.0
    )
    row = lax.broadcasted_iota(jnp.int32, (WINDOW, shard), 0)
    half = stems // 2
    for stem in range(stems):
        start = pl.multiple_of(window * WINDOW, WINDOW)
        mean, factor = centre[stem : stem + 1], scale[stem : stem + 1]
        act = silu((hid_ref[stem, pl.ds(start, WINDOW), :] - mean) * factor)
        inner = silu((hid_ref[stem, WINDOW - 8 : WINDOW + 8, :] - mean) * factor)
        before = jnp.where(window == 0, low[stem : stem + 1], inner[7:8])
        after = jnp.where(window == 0, inner[8:9], high[stem : stem + 1])
        before = jnp.where(row == 0, before, pltpu.roll(act, 1, 0))
        after = jnp.where(row == WINDOW - 1, after, pltpu.roll(act, WINDOW - 1, 0))
        mine = core if stem < half else 1 - core
        base = jnp.where(mine == 0, half * WINDOW, 0) + (stem % half) * WINDOW
        at = pl.ds(pl.multiple_of(base, WINDOW), WINDOW)
        act_ref[at, 0:shard] = before.astype(bf16)
        act_ref[at, shard : 2 * shard] = act.astype(bf16)
        act_ref[at, 2 * shard : 3 * shard] = after.astype(bf16)
    total = jnp.dot(act_ref[...], weight_ref[...], preferred_element_type=f32)
    send_ref[...] = total[: half * WINDOW].astype(bf16)
    keep_ref[...] = total[half * WINDOW :].astype(bf16)


def split3(value):
    high = value.astype(bf16)
    rest = value - high.astype(f32)
    middle = rest.astype(bf16)
    return high, middle, (rest - middle.astype(f32)).astype(bf16)


def attention_kernel(
    mine_ref, theirs_ref, gain_ref, qkv_ref, out_ref,
    heads_x_ref, rest_x_ref, heads_y_ref, rest_y_ref,
    send_ref, keep_ref, res_ref, normed_ref, context_ref,
):
    rows, channels = mine_ref.shape
    shard = qkv_ref.shape[2]
    depth = channels // 2
    part = shard // 2
    group = lax.axis_index("groups")
    index = lax.axis_index("tensor")
    chip, core = index // 2, index % 2
    for first, ref in ((0, mine_ref), (rows, theirs_ref)):
        res = ref[...].astype(f32)
        res_ref[first : first + rows, :] = res
        mean_sq = jnp.mean(res * res, axis=1, keepdims=True)
        normed_ref[first : first + rows, :] = (
            res * lax.rsqrt(mean_sq + rms_eps) * gain_ref[...]
        ).astype(bf16)
    normed = normed_ref[...]
    lane = lax.broadcasted_iota(jnp.int32, (2 * rows, LANES), 1)
    per_tile = LANES // HEAD_DIM
    nt = (((1,), (1,)), ((), ()))
    near_at = pl.ds(pl.multiple_of(group * depth, depth), depth)
    away_at = pl.ds(pl.multiple_of((1 - group) * depth, depth), depth)

    def project(side, which):
        if side == 0:
            return jnp.dot(normed, qkv_ref[which], preferred_element_type=f32)
        from_x = heads_x_ref[which] if which < 2 else rest_x_ref[0]
        from_y = heads_y_ref[which] if which < 2 else rest_y_ref[0]
        near = jnp.dot(normed_ref[:, near_at], from_x, preferred_element_type=f32)
        return near + jnp.dot(normed_ref[:, away_at], from_y, preferred_element_type=f32)

    for side in range(2):
        queries, keys, values = [project(side, which) for which in range(3)]
        queries = queries * (1.0 / math.sqrt(HEAD_DIM))
        values = values.astype(bf16)
        for tile in range(shard // LANES):
            at = slice(tile * LANES, (tile + 1) * LANES)
            q_high, q_mid, q_low = split3(queries[:, at])
            left = jnp.concatenate([q_high, q_mid, q_high, q_mid, q_high, q_low], axis=1)
            result = None
            for head in range(per_tile):
                inside = lane // HEAD_DIM == head
                k_high, k_mid, k_low = split3(jnp.where(inside, keys[:, at], 0.0))
                right = jnp.concatenate([k_high, k_high, k_mid, k_mid, k_low, k_high], axis=1)
                scores = lax.dot_general(left, right, nt, preferred_element_type=f32)
                scores = jnp.exp(scores - jnp.max(scores, axis=1, keepdims=True))
                total = jnp.sum(scores, axis=1, keepdims=True)
                probs = (scores / total).astype(bf16)
                mixed = jnp.dot(probs, values[:, at], preferred_element_type=f32)
                result = mixed if result is None else jnp.where(inside, mixed, result)
            base = side * shard + tile * LANES
            context_ref[:, base : base + LANES] = result.astype(bf16)
    context = context_ref[:, :shard]
    from_x = context_ref[:, pl.ds(pl.multiple_of(shard + group * part, part), part)]
    from_y = context_ref[:, pl.ds(pl.multiple_of(shard + (1 - group) * part, part), part)]

    def term(block):
        at = pl.ds(pl.multiple_of(block * shard, shard), shard)
        rows_at = pl.ds(pl.multiple_of(block * part, part), part)
        value = jnp.dot(context, out_ref[:, at], preferred_element_type=f32)
        value = value + jnp.dot(from_x, rest_x_ref[1, rows_at, :], preferred_element_type=f32)
        return value + jnp.dot(from_y, rest_y_ref[1, rows_at, :], preferred_element_type=f32)

    for place, goal in enumerate((1 - chip, chip)):
        at = slice(place * shard, (place + 1) * shard)
        value = term(2 * goal + 1 - core).astype(bf16)
        send_ref[:rows, at] = value[rows:]
        send_ref[rows:, at] = value[:rows]
        block = 2 * goal + core
        kept = term(block)
        keep_ref[:, at] = kept + res_ref[:, pl.ds(pl.multiple_of(block * shard, shard), shard)]


def pack_heads_kernel(qkv_ref, send_ref, sem):
    depth = send_ref.shape[1]
    start = pl.multiple_of(lax.axis_index("groups") * depth, depth)
    copy = pltpu.make_async_copy(qkv_ref.at[pl.ds(0, 2), pl.ds(start, depth), :], send_ref, sem)
    copy.start()
    copy.wait()


def pack_rest_kernel(qkv_ref, out_ref, send_ref, sems):
    depth, shard = send_ref.shape[1:]
    part = shard // 2
    group = lax.axis_index("groups")
    at = pl.ds(pl.multiple_of(group * depth, depth), depth)
    copies = [pltpu.make_async_copy(qkv_ref.at[2, at, :], send_ref.at[0], sems.at[0])]
    rows = pl.ds(pl.multiple_of(group * part, part), part)
    for block in range(depth // part):
        copies.append(
            pltpu.make_async_copy(
                out_ref.at[rows, pl.ds(block * shard, shard)],
                send_ref.at[1, pl.ds(block * part, part), :],
                sems.at[1 + block],
            )
        )
    for copy in copies:
        copy.start()
    for copy in copies:
        copy.wait()


def pack(kernel, shape, copies, args):
    return pl.pallas_call(
        kernel,
        out_shape=jax.ShapeDtypeStruct(shape, bf16),
        in_specs=[pl.BlockSpec(memory_space=pl.ANY)] * len(args),
        out_specs=pl.BlockSpec(memory_space=VMEM),
        scratch_shapes=[pltpu.SemaphoreType.DMA(copies)],
        cost_estimate=pl.CostEstimate(flops=0, bytes_accessed=2**20, transcendentals=0),
    )(*args)


def place_kernel(own_ref, far_ref, out_ref):
    stems, _, _ = out_ref.shape
    index = lax.axis_index("tensor")
    chip, core = index // 2, index % 2
    half = stems // 2
    for stem in range(stems):
        goal = (core if stem < half else 1 - core) * half + stem % half
        rows = slice(stem * WINDOW, (stem + 1) * WINDOW)
        near = pl.multiple_of(chip * WINDOW, WINDOW)
        away = pl.multiple_of((1 - chip) * WINDOW, WINDOW)
        out_ref[goal, pl.ds(near, WINDOW), :] = own_ref[rows, :]
        out_ref[goal, pl.ds(away, WINDOW), :] = far_ref[rows, :]


def call(kernel, outs, scratch, args, flops=0, moved=0):
    return pl.pallas_call(
        kernel,
        out_shape=[jax.ShapeDtypeStruct(shape, dtype) for shape, dtype in outs],
        in_specs=[pl.BlockSpec(memory_space=VMEM)] * len(args),
        out_specs=[pl.BlockSpec(memory_space=VMEM)] * len(outs),
        scratch_shapes=[VMEM(shape, dtype) for shape, dtype in scratch],
        compiler_params=pltpu.CompilerParams(vmem_limit_bytes=40 * 2**20),
        cost_estimate=pl.CostEstimate(flops=flops, bytes_accessed=moved, transcendentals=0),
    )(*args)


def swap_cores(value):
    return lax.ppermute(value, "tensor", [(0, 1), (1, 0), (2, 3), (3, 2)])


def swap_chips(value):
    return lax.ppermute(value, "tensor", [(0, 2), (2, 0), (1, 3), (3, 1)])


def swap_groups(value):
    return lax.ppermute(value, "groups", [(0, 1), (1, 0)])


def shift_frames(value, by):
    count = lax.axis_size("frame")
    return lax.ppermute(value, "frame", [(i, (i + by) % count) for i in range(count)])


def exchange(up, down, own):
    return (shift_frames(up, 1), shift_frames(down, -1), shift_frames(own, 2))


def fast(
    latent, norm1_gain, conv1_weight, time_bias, norm2_gain, conv2_weight,
    attn_gain, qkv_weight, out_weight,
):
    stems, frames, channels = latent.shape
    frame_size = lax.axis_size("frame")
    shard = conv1_weight.shape[2]
    width = channels // GROUPS
    entries = frames * frame_size * width
    half_rows = stems // 2 * WINDOW
    qkv = jnp.transpose(qkv_weight, (1, 0, 2))
    depth, part = channels // 2, shard // 2
    heads = pack(pack_heads_kernel, (2, depth, shard), (), [qkv])
    rest = pack(pack_rest_kernel, (2, depth, shard), (1 + depth // part,), [qkv, out_weight])
    heads_x = swap_chips(heads)
    rest_x = swap_chips(rest)
    heads_y = swap_groups(heads_x)
    rest_y = swap_groups(rest_x)
    wide = channels + 2 * LANES
    up, down, own = call(
        functools.partial(stats_kernel, width),
        [((stems, wide), f32), ((stems, wide), f32), ((stems, 2 * LANES), f32)],
        [((stems, channels), f32)] * 2,
        [latent],
    )
    low, high, far = exchange(up, down, own)
    narrow = shard + 2 * LANES
    hid, up2, down2, own2 = call(
        functools.partial(first_kernel, entries, width, frame_size),
        [((stems, frames, shard), f32), ((stems, narrow), f32), ((stems, narrow), f32),
         ((stems, 2 * LANES), f32)],
        [((stems * frames, channels), bf16), ((16, channels), f32)] + [((stems, shard), f32)] * 2,
        [latent, low, high, far, own, norm1_gain[None], conv1_weight, time_bias[None]],
        flops=6 * stems * frames * channels * shard,
    )
    low2, high2, far2 = exchange(up2, down2, own2)
    weight2 = conv2_weight.reshape(3 * shard, channels)

    def second(other):
        return call(
            functools.partial(second_kernel, entries, width, frame_size, other),
            [((half_rows, channels), bf16)] * 2,
            [((2 * half_rows, 3 * shard), bf16)],
            [hid, low2, high2, far2, own2, norm2_gain[None], weight2],
            flops=12 * half_rows * channels * shard,
        )

    send, keep = second(True)
    got = swap_cores(send)
    summed = (got.astype(f32) + keep.astype(f32)).astype(bf16)
    summed = swap_chips(summed)
    send_own, keep_own = second(False)
    got_own = swap_cores(send_own)
    index = lax.axis_index("tensor")
    chip, core = index // 2, index % 2
    latent_own = lax.dynamic_slice(
        latent, (core * (stems // 2), chip * WINDOW, 0), (stems // 2, WINDOW, channels)
    ).reshape(half_rows, channels)
    mine = (
        latent_own.astype(f32) + keep_own.astype(f32) + got_own.astype(f32) + summed.astype(f32)
    ).astype(bf16)
    theirs = swap_cores(mine)
    out_send, out_keep = call(
        attention_kernel,
        [((2 * half_rows, 2 * shard), bf16), ((2 * half_rows, 2 * shard), f32)],
        [((2 * half_rows, channels), f32), ((2 * half_rows, channels), bf16),
         ((2 * half_rows, 2 * shard), bf16)],
        [mine, theirs, attn_gain[None], qkv, out_weight, heads_x, rest_x, heads_y, rest_y],
        flops=24 * half_rows * channels * shard,
    )
    out_got = swap_cores(out_send)
    away = (out_keep[:, :shard] + out_got[:, :shard].astype(f32)).astype(bf16)
    stay = (out_keep[:, shard:] + out_got[:, shard:].astype(f32)).astype(bf16)
    arrived = swap_chips(away)
    return call(place_kernel, [((stems, frames, shard), bf16)], [], [stay, arrived])[0]


def local(*args):
    latent = args[0]
    stems, frames, channels = latent.shape
    tensor_size, frame_size = lax.axis_size("tensor"), lax.axis_size("frame")
    shard = channels // tensor_size
    suits = (
        tensor_size == 4
        and frame_size == 4
        and lax.axis_size("groups") == 2
        and frames == 2 * WINDOW
        and stems % 2 == 0
        and stems <= 8
        and shard % (2 * LANES) == 0
    )
    if not suits:
        return generic(*args)
    return fast(*args)


def solution(mesh):
    return jax.shard_map(
        local,
        mesh=mesh,
        in_specs=(
            P(None, ("groups", "frame"), None),
            P(),
            P(None, None, "tensor"),
            P("tensor"),
            P("tensor"),
            P(None, "tensor", None),
            P(),
            P(None, None, "tensor"),
            P("tensor", None),
        ),
        out_specs=P(None, ("groups", "frame"), "tensor"),
        check_vma=False,
    )
```

```python
import functools
import math

import jax
import jax.numpy as jnp
from jax import lax
from jax.experimental import pallas as pl
from jax.experimental.pallas import tpu as pltpu
from jax.sharding import PartitionSpec as P


GROUPS = 32
HEAD_DIM = 64
WINDOW = 64
LANES = 128
PIECES = 4

norm_eps = 1e-05
rms_eps = 1e-06
HIGHEST = lax.Precision.HIGHEST
VMEM = pltpu.VMEM
bf16 = jnp.bfloat16
f32 = jnp.float32


def extended(block, sides, width):
    for axis, dim in sides:
        count = lax.axis_size(axis)
        forward = [(i, i + 1) for i in range(count - 1)]
        backward = [(target, source) for source, target in forward]
        low = lax.ppermute(
            lax.slice_in_dim(block, block.shape[dim] - width, None, axis=dim), axis, forward
        )
        high = lax.ppermute(lax.slice_in_dim(block, 0, width, axis=dim), axis, backward)
        block = jnp.concatenate([low, block, high], axis=dim)
    return block


def group_sums(hidden, group_count):
    stem_count, frame_count, channels = hidden.shape
    grouped = hidden.reshape(stem_count, frame_count, group_count, channels // group_count)
    return (jnp.sum(grouped, axis=(1, 3)), jnp.sum(grouped * grouped, axis=(1, 3)))


def apply_group(hidden, totals, squares, entries, gain_vec):
    stem_count, frame_count, channels = hidden.shape
    group_count = totals.shape[1]
    centre = totals / entries
    spread = squares / entries - centre * centre
    grouped = hidden.reshape(stem_count, frame_count, group_count, channels // group_count)
    scaled = (grouped - centre[:, None, :, None]) * lax.rsqrt(spread + norm_eps)[:, None, :, None]
    return scaled.reshape(stem_count, frame_count, channels) * gain_vec


def conv_padded(padded, kernel, frame_count):
    stem_count = padded.shape[0]
    channels = padded.shape[2]
    result = jnp.zeros((stem_count * frame_count, kernel.shape[2]), jnp.float32)
    for tap_index in range(3):
        tap_rows = padded[:, tap_index : tap_index + frame_count].reshape(
            stem_count * frame_count, channels
        )
        result = result + jnp.dot(tap_rows, kernel[tap_index], preferred_element_type=jnp.float32)
    return result.reshape(stem_count, frame_count, kernel.shape[2])


def attend(queries, keys_all, values):
    stem_count, frame_count, head_count, head_dim = queries.shape
    window_count = frame_count // WINDOW

    def arrange(source):
        shaped = source.reshape(stem_count, window_count, WINDOW, head_count, head_dim)
        return shaped.transpose(1, 3, 0, 2, 4).reshape(
            window_count, head_count, stem_count * WINDOW, head_dim
        )

    scores = jnp.einsum(
        "nhqd,nhkd->nhqk",
        arrange(queries),
        arrange(keys_all),
        precision=lax.Precision.HIGHEST,
        preferred_element_type=jnp.float32,
    ) / math.sqrt(head_dim)
    scores = scores - jnp.max(scores, axis=3, keepdims=True)
    exp_scores = jnp.exp(scores)
    attn_probs = (exp_scores / jnp.sum(exp_scores, axis=3, keepdims=True)).astype(jnp.bfloat16)
    context = jnp.einsum(
        "nhqk,nhkd->nhqd", attn_probs, arrange(values), preferred_element_type=jnp.float32
    ).astype(jnp.bfloat16)
    context = context.reshape(window_count, head_count, stem_count, WINDOW, head_dim).transpose(
        2, 0, 3, 1, 4
    )
    return context.reshape(stem_count * frame_count, head_count * head_dim)


def generic(
    latent,
    norm1_gain,
    conv1_weight,
    time_bias,
    norm2_gain,
    conv2_weight,
    attn_gain,
    qkv_weight,
    out_weight,
):
    stem_count, frame_count, channels = latent.shape
    tensor_size = lax.axis_size("tensor")
    shard_width = channels // tensor_size
    row_count = stem_count * frame_count
    group_entries = frame_count * lax.axis_size("frame") * (channels // GROUPS)
    latent_f = latent.astype(jnp.float32)
    sums_one, squares_one = group_sums(latent_f, GROUPS)
    sums_one, squares_one = lax.psum((sums_one, squares_one), "frame")
    act_one = jax.nn.silu(
        apply_group(latent_f, sums_one, squares_one, group_entries, norm1_gain)
    ).astype(jnp.bfloat16)
    padded_one = extended(act_one, (("frame", 1),), 1)
    hid_one = conv_padded(padded_one, conv1_weight, frame_count)
    hid_one = hid_one + time_bias
    local_groups = GROUPS // tensor_size
    sums_two, squares_two = group_sums(hid_one, local_groups)
    sums_two, squares_two = lax.psum((sums_two, squares_two), "frame")
    act_two = jax.nn.silu(
        apply_group(hid_one, sums_two, squares_two, group_entries, norm2_gain)
    ).astype(jnp.bfloat16)
    padded_two = extended(act_two, (("frame", 1),), 1)
    conv_term = conv_padded(padded_two, conv2_weight, frame_count)
    own_start = lax.axis_index("tensor") * shard_width
    qkv_flat = qkv_weight.reshape(channels, 3 * shard_width)
    conv_total = lax.psum(conv_term.astype(jnp.bfloat16), "tensor").astype(jnp.float32)
    residual = (latent_f + conv_total).astype(jnp.bfloat16)
    res_f = residual.astype(jnp.float32)
    mean_sq = jnp.mean(res_f * res_f, axis=2, keepdims=True)
    normed = (res_f * lax.rsqrt(mean_sq + rms_eps) * attn_gain).astype(jnp.bfloat16)
    projected = jnp.dot(
        normed.reshape(row_count, channels), qkv_flat, preferred_element_type=jnp.float32
    )
    res_own = lax.dynamic_slice_in_dim(res_f, own_start, shard_width, 2)
    head_local = shard_width // HEAD_DIM
    projected = projected.reshape(stem_count, frame_count, 3, head_local, HEAD_DIM)
    values = projected[:, :, 2].astype(jnp.bfloat16)
    context = attend(projected[:, :, 0], projected[:, :, 1], values)
    out_term = jnp.dot(context, out_weight, preferred_element_type=jnp.float32).reshape(
        stem_count, frame_count, channels
    )
    attn_share = lax.psum_scatter(
        out_term.astype(jnp.bfloat16), "tensor", scatter_dimension=2, tiled=True
    ).astype(jnp.float32)
    velocity = (res_own + attn_share).astype(jnp.bfloat16)
    return velocity


def silu(v):
    half = 0.5 * v
    return half + half * jnp.tanh(half)


def one_hot(rows, columns, width, by_row):
    row = lax.broadcasted_iota(jnp.int32, (rows, columns), 0)
    column = lax.broadcasted_iota(jnp.int32, (rows, columns), 1)
    if by_row:
        return (row // width == column).astype(f32)
    return (row == column // width).astype(f32)


def f32_dot(a, b):
    return jnp.dot(a, b, precision=HIGHEST, preferred_element_type=f32)


def group_totals(sums, squares, width):
    hot = one_hot(sums.shape[1], LANES, width, True)
    return f32_dot(sums, hot), f32_dot(squares, hot)


def channel_scale(refs, entries, channels, width):
    total = refs[0]
    for other in refs[1:]:
        total = total + other
    centre = total[:, :LANES] / entries
    spread = total[:, LANES:] / entries - centre * centre
    hot = one_hot(LANES, channels, width, False)
    return f32_dot(centre, hot), f32_dot(lax.rsqrt(spread + norm_eps), hot)


def stats_kernel(width, lat_ref, up_ref, down_ref, own_ref, sum_ref, square_ref):
    stems, frames, channels = lat_ref.shape
    for stem in range(stems):
        block = lat_ref[stem].astype(f32)
        sum_ref[stem : stem + 1, :] = jnp.sum(block, axis=0, keepdims=True)
        square_ref[stem : stem + 1, :] = jnp.sum(block * block, axis=0, keepdims=True)
        down_ref[stem : stem + 1, :channels] = block[:1]
        up_ref[stem : stem + 1, :channels] = block[frames - 1 :]
    sums, squares = group_totals(sum_ref[...], square_ref[...], width)
    for ref, start in ((up_ref, channels), (down_ref, channels), (own_ref, 0)):
        ref[:, start : start + LANES] = sums
        ref[:, start + LANES : start + 2 * LANES] = squares


def first_kernel(
    entries, width, frame_size,
    lat_ref, low_ref, high_ref, far_ref, own_ref, gain_ref, weight_ref, bias_ref,
    hid_ref, up_ref, down_ref, tot_ref, act_ref, edge_ref, sum_ref, square_ref,
):
    stems, frames, channels = lat_ref.shape
    shard = weight_ref.shape[2]
    place = lax.axis_index("frame")
    centre, scale = channel_scale(
        [own_ref[...], low_ref[:, channels:], high_ref[:, channels:], far_ref[...]],
        entries, channels, width,
    )
    scale = scale * gain_ref[...]
    edge_ref[...] = jnp.zeros_like(edge_ref)
    low = silu((low_ref[:, :channels] - centre) * scale)
    high = silu((high_ref[:, :channels] - centre) * scale)
    edge_ref[0:stems, :] = jnp.where(place > 0, low, 0.0)
    edge_ref[8 : 8 + stems, :] = jnp.where(place < frame_size - 1, high, 0.0)
    edge = edge_ref[...].astype(bf16)
    edge_low = jnp.dot(edge, weight_ref[0], preferred_element_type=f32)
    edge_high = jnp.dot(edge, weight_ref[2], preferred_element_type=f32)
    row = lax.broadcasted_iota(jnp.int32, (frames, shard), 0)
    bias = bias_ref[...]
    step = stems // 2
    for first in range(0, stems, step):
        for stem in range(first, first + step):
            block = lat_ref[stem].astype(f32)
            block = (block - centre[stem : stem + 1]) * scale[stem : stem + 1]
            act_ref[stem * frames : (stem + 1) * frames, :] = silu(block).astype(bf16)
        rows = act_ref[first * frames : (first + step) * frames, :]
        taps = [jnp.dot(rows, weight_ref[tap], preferred_element_type=f32) for tap in range(3)]
        for stem in range(first, first + step):
            lo = (stem - first) * frames
            before = pltpu.roll(taps[0][lo : lo + frames], 1, 0)
            after = pltpu.roll(taps[2][lo : lo + frames], frames - 1, 0)
            before = jnp.where(row == 0, edge_low[stem : stem + 1], before)
            after = jnp.where(row == frames - 1, edge_high[8 + stem : 9 + stem], after)
            hid = taps[1][lo : lo + frames] + before + after + bias
            hid_ref[stem] = hid
            sum_ref[stem : stem + 1, :] = jnp.sum(hid, axis=0, keepdims=True)
            square_ref[stem : stem + 1, :] = jnp.sum(hid * hid, axis=0, keepdims=True)
            down_ref[stem : stem + 1, :shard] = hid[:1]
            up_ref[stem : stem + 1, :shard] = hid[frames - 1 :]
    sums, squares = group_totals(sum_ref[...], square_ref[...], width)
    for ref, start in ((up_ref, shard), (down_ref, shard), (tot_ref, 0)):
        ref[:, start : start + LANES] = sums
        ref[:, start + LANES : start + 2 * LANES] = squares


def second_kernel(
    entries, width, frame_size, other,
    hid_ref, low_ref, high_ref, far_ref, own_ref, gain_ref, weight_ref,
    send_ref, keep_ref, act_ref,
):
    stems, _, shard = hid_ref.shape
    place = lax.axis_index("frame")
    index = lax.axis_index("tensor")
    chip, core = index // 2, index % 2
    window = 1 - chip if other else chip
    centre, scale = channel_scale(
        [own_ref[...], low_ref[:, shard:], high_ref[:, shard:], far_ref[...]],
        entries, shard, width,
    )
    scale = scale * gain_ref[...]
    low = jnp.where(place > 0, silu((low_ref[:, :shard] - centre) * scale), 0.0)
    high = jnp.where(
        place < frame_size - 1, silu((high_ref[:, :shard] - centre) * scale), 0.0
    )
    row = lax.broadcasted_iota(jnp.int32, (WINDOW, shard), 0)
    half = stems // 2
    for stem in range(stems):
        start = pl.multiple_of(window * WINDOW, WINDOW)
        mean, factor = centre[stem : stem + 1], scale[stem : stem + 1]
        act = silu((hid_ref[stem, pl.ds(start, WINDOW), :] - mean) * factor)
        inner = silu((hid_ref[stem, WINDOW - 8 : WINDOW + 8, :] - mean) * factor)
        before = jnp.where(window == 0, low[stem : stem + 1], inner[7:8])
        after = jnp.where(window == 0, inner[8:9], high[stem : stem + 1])
        before = jnp.where(row == 0, before, pltpu.roll(act, 1, 0))
        after = jnp.where(row == WINDOW - 1, after, pltpu.roll(act, WINDOW - 1, 0))
        mine = core if stem < half else 1 - core
        base = jnp.where(mine == 0, half * WINDOW, 0) + (stem % half) * WINDOW
        at = pl.ds(pl.multiple_of(base, WINDOW), WINDOW)
        act_ref[at, 0:shard] = before.astype(bf16)
        act_ref[at, shard : 2 * shard] = act.astype(bf16)
        act_ref[at, 2 * shard : 3 * shard] = after.astype(bf16)
    total = jnp.dot(act_ref[...], weight_ref[...], preferred_element_type=f32)
    send_ref[...] = total[: half * WINDOW].astype(bf16)
    keep_ref[...] = total[half * WINDOW :].astype(bf16)


def split2(value):
    high = value.astype(bf16)
    return high, (value - high.astype(f32)).astype(bf16)


def attention_kernel(
    mine_ref, theirs_ref, gain_ref, qkv_ref, out_ref,
    heads_x_ref, values_x_ref, outs_x_ref, heads_y_ref, values_y_ref, outs_z_ref,
    send_ref, keep_ref, res_ref, normed_ref, context_ref,
):
    rows, channels = mine_ref.shape
    shard = qkv_ref.shape[2]
    depth = channels // 2
    part = shard // 2
    group = lax.axis_index("groups")
    index = lax.axis_index("tensor")
    chip, core = index // 2, index % 2
    for first, ref in ((0, mine_ref), (rows, theirs_ref)):
        res = ref[...].astype(f32)
        res_ref[first : first + rows, :] = res
        mean_sq = jnp.mean(res * res, axis=1, keepdims=True)
        normed_ref[first : first + rows, :] = (
            res * lax.rsqrt(mean_sq + rms_eps) * gain_ref[...]
        ).astype(bf16)
    normed = normed_ref[...]
    lane = lax.broadcasted_iota(jnp.int32, (2 * rows, LANES), 1)
    per_tile = LANES // HEAD_DIM
    ones = jnp.ones((2 * rows, LANES), bf16)
    zero = jnp.zeros((), bf16)
    nt = (((1,), (1,)), ((), ()))
    near_at = pl.ds(pl.multiple_of(group * depth, depth), depth)
    away_at = pl.ds(pl.multiple_of((1 - group) * depth, depth), depth)

    def project(side, which):
        if side == 0:
            return jnp.dot(normed, qkv_ref[which], preferred_element_type=f32)
        from_x = heads_x_ref[which] if which < 2 else values_x_ref[...]
        from_y = heads_y_ref[which] if which < 2 else values_y_ref[...]
        near = jnp.dot(normed_ref[:, near_at], from_x, preferred_element_type=f32)
        return near + jnp.dot(normed_ref[:, away_at], from_y, preferred_element_type=f32)

    for side in range(2):
        queries, keys, values = [project(side, which) for which in range(3)]
        queries = queries * (1.0 / math.sqrt(HEAD_DIM))
        values = values.astype(bf16)
        for tile in range(shard // LANES):
            at = slice(tile * LANES, (tile + 1) * LANES)
            q_high, q_low = split2(queries[:, at])
            left = jnp.concatenate([q_high, q_low, q_high, q_low], axis=1)
            k_high, k_low = split2(keys[:, at])
            mixing = jnp.concatenate([values[:, at], ones], axis=1)
            result = None
            for head in range(per_tile):
                inside = lane // HEAD_DIM == head
                own_high = jnp.where(inside, k_high, zero)
                own_low = jnp.where(inside, k_low, zero)
                right = jnp.concatenate([own_high, own_high, own_low, own_low], axis=1)
                scores = lax.dot_general(left, right, nt, preferred_element_type=f32)
                scores = jnp.exp(scores - jnp.max(scores, axis=1, keepdims=True)).astype(bf16)
                mixed = jnp.dot(scores, mixing, preferred_element_type=f32)
                mixed = mixed[:, :LANES] / mixed[:, LANES:]
                result = mixed if result is None else jnp.where(inside, mixed, result)
            base = side * shard + tile * LANES
            context_ref[:, base : base + LANES] = result.astype(bf16)
    context = context_ref[:, :shard]
    parity = lax.axis_index("frame") % 2
    from_x = context_ref[:, pl.ds(pl.multiple_of(shard + parity * part, part), part)]
    from_z = context_ref[:, pl.ds(pl.multiple_of(shard + (1 - parity) * part, part), part)]

    def term(block):
        at = pl.ds(pl.multiple_of(block * shard, shard), shard)
        rows_at = pl.ds(pl.multiple_of(block * part, part), part)
        value = jnp.dot(context, out_ref[:, at], preferred_element_type=f32)
        value = value + jnp.dot(from_x, outs_x_ref[rows_at, :], preferred_element_type=f32)
        return value + jnp.dot(from_z, outs_z_ref[rows_at, :], preferred_element_type=f32)

    for place, goal in enumerate((1 - chip, chip)):
        at = slice(place * shard, (place + 1) * shard)
        value = term(2 * goal + 1 - core).astype(bf16)
        send_ref[:rows, at] = value[rows:]
        send_ref[rows:, at] = value[:rows]
        block = 2 * goal + core
        kept = term(block)
        keep_ref[:, at] = kept + res_ref[:, pl.ds(pl.multiple_of(block * shard, shard), shard)]


def run_copies(pairs, sems):
    copies = [
        pltpu.make_async_copy(source, goal, sems.at[place])
        for place, (source, goal) in enumerate(pairs)
    ]
    for copy in copies:
        copy.start()
    for copy in copies:
        copy.wait()


def pack_heads_kernel(qkv_ref, send_ref, sems):
    depth = send_ref.shape[1]
    step = depth // PIECES
    start = lax.axis_index("groups") * depth
    pairs = []
    for which in range(2):
        for piece in range(PIECES):
            rows = pl.ds(pl.multiple_of(start + piece * step, step), step)
            goal = send_ref.at[which, pl.ds(piece * step, step), :]
            pairs.append((qkv_ref.at[which, rows, :], goal))
    run_copies(pairs, sems)


def pack_rest_kernel(qkv_ref, out_ref, send_ref, sems):
    depth, shard = send_ref.shape[1:]
    part = shard // 2
    step = depth // PIECES
    start = lax.axis_index("groups") * depth
    pairs = []
    for piece in range(PIECES):
        rows = pl.ds(pl.multiple_of(start + piece * step, step), step)
        pairs.append((qkv_ref.at[2, rows, :], send_ref.at[0, pl.ds(piece * step, step), :]))
    rows = pl.ds(pl.multiple_of(lax.axis_index("frame") % 2 * part, part), part)
    for block in range(depth // part):
        goal = send_ref.at[1, pl.ds(block * part, part), :]
        pairs.append((out_ref.at[rows, pl.ds(block * shard, shard)], goal))
    run_copies(pairs, sems)


def pack(kernel, shape, copies, args):
    return pl.pallas_call(
        kernel,
        out_shape=jax.ShapeDtypeStruct(shape, bf16),
        in_specs=[pl.BlockSpec(memory_space=pltpu.HBM)] * len(args),
        out_specs=pl.BlockSpec(memory_space=VMEM),
        scratch_shapes=[pltpu.SemaphoreType.DMA((copies,))],
        compiler_params=pltpu.CompilerParams(vmem_limit_bytes=4 * 2**20),
        cost_estimate=pl.CostEstimate(flops=0, bytes_accessed=2**20, transcendentals=0),
    )(*[pltpu.with_memory_space_constraint(arg, pltpu.HBM) for arg in args])


def residual_kernel(latent_ref, keep_ref, got_ref, far_ref, out_ref):
    stems = latent_ref.shape[0]
    index = lax.axis_index("tensor")
    chip, core = index // 2, index % 2
    start = pl.multiple_of(chip * WINDOW, WINDOW)
    for stem in range(stems // 2):
        rows = slice(stem * WINDOW, (stem + 1) * WINDOW)
        total = keep_ref[rows, :].astype(f32) + got_ref[rows, :].astype(f32)
        total = total + far_ref[rows, :].astype(f32)
        latent = latent_ref[core * (stems // 2) + stem, pl.ds(start, WINDOW), :]
        out_ref[rows, :] = (latent.astype(f32) + total).astype(bf16)


def place_kernel(own_ref, far_ref, out_ref):
    stems, _, _ = out_ref.shape
    index = lax.axis_index("tensor")
    chip, core = index // 2, index % 2
    half = stems // 2
    for stem in range(stems):
        goal = (core if stem < half else 1 - core) * half + stem % half
        rows = slice(stem * WINDOW, (stem + 1) * WINDOW)
        near = pl.multiple_of(chip * WINDOW, WINDOW)
        away = pl.multiple_of((1 - chip) * WINDOW, WINDOW)
        out_ref[goal, pl.ds(near, WINDOW), :] = own_ref[rows, :]
        out_ref[goal, pl.ds(away, WINDOW), :] = far_ref[rows, :]


def call(kernel, outs, scratch, args, flops=0, moved=0, limit=16):
    return pl.pallas_call(
        kernel,
        out_shape=[jax.ShapeDtypeStruct(shape, dtype) for shape, dtype in outs],
        in_specs=[pl.BlockSpec(memory_space=VMEM)] * len(args),
        out_specs=[pl.BlockSpec(memory_space=VMEM)] * len(outs),
        scratch_shapes=[VMEM(shape, dtype) for shape, dtype in scratch],
        compiler_params=pltpu.CompilerParams(vmem_limit_bytes=limit * 2**20),
        cost_estimate=pl.CostEstimate(flops=flops, bytes_accessed=moved, transcendentals=0),
    )(*args)


def swap_cores(value):
    return lax.ppermute(value, "tensor", [(0, 1), (1, 0), (2, 3), (3, 2)])


def swap_chips(value):
    return lax.ppermute(value, "tensor", [(0, 2), (2, 0), (1, 3), (3, 1)])


def swap_groups(value):
    return lax.ppermute(value, "groups", [(0, 1), (1, 0)])


def swap_frames(value):
    return lax.ppermute(value, "frame", [(0, 1), (1, 0), (2, 3), (3, 2)])


def shift_frames(value, by):
    count = lax.axis_size("frame")
    return lax.ppermute(value, "frame", [(i, (i + by) % count) for i in range(count)])


def exchange(up, down, own):
    return (shift_frames(up, 1), shift_frames(down, -1), shift_frames(own, 2))


def fast(
    latent, norm1_gain, conv1_weight, time_bias, norm2_gain, conv2_weight,
    attn_gain, qkv_weight, out_weight,
):
    stems, frames, channels = latent.shape
    frame_size = lax.axis_size("frame")
    shard = conv1_weight.shape[2]
    width = channels // GROUPS
    entries = frames * frame_size * width
    half_rows = stems // 2 * WINDOW
    qkv = jnp.transpose(qkv_weight, (1, 0, 2))
    depth, part = channels // 2, shard // 2
    heads = pack(pack_heads_kernel, (2, depth, shard), 2 * PIECES, [qkv])
    rest = pack(
        pack_rest_kernel, (2, depth, shard), PIECES + depth // part,
        [qkv, out_weight],
    )
    heads_x = swap_chips(heads)
    rest_x = swap_chips(rest)
    heads_y = swap_groups(heads_x)
    values_x, outs_x = rest_x[0], rest_x[1]
    values_y = swap_groups(values_x)
    outs_z = swap_frames(outs_x)
    wide = channels + 2 * LANES
    up, down, own = call(
        functools.partial(stats_kernel, width),
        [((stems, wide), f32), ((stems, wide), f32), ((stems, 2 * LANES), f32)],
        [((stems, channels), f32)] * 2,
        [latent],
    )
    low, high, far = exchange(up, down, own)
    narrow = shard + 2 * LANES
    hid, up2, down2, own2 = call(
        functools.partial(first_kernel, entries, width, frame_size),
        [((stems, frames, shard), f32), ((stems, narrow), f32), ((stems, narrow), f32),
         ((stems, 2 * LANES), f32)],
        [((stems * frames, channels), bf16), ((16, channels), f32)] + [((stems, shard), f32)] * 2,
        [latent, low, high, far, own, norm1_gain[None], conv1_weight, time_bias[None]],
        flops=6 * stems * frames * channels * shard,
    )
    low2, high2, far2 = exchange(up2, down2, own2)
    weight2 = conv2_weight.reshape(3 * shard, channels)

    def second(other):
        return call(
            functools.partial(second_kernel, entries, width, frame_size, other),
            [((half_rows, channels), bf16)] * 2,
            [((2 * half_rows, 3 * shard), bf16)],
            [hid, low2, high2, far2, own2, norm2_gain[None], weight2],
            flops=12 * half_rows * channels * shard,
        )

    send, keep = second(True)
    got = swap_cores(send)
    summed = (got.astype(f32) + keep.astype(f32)).astype(bf16)
    summed = swap_chips(summed)
    send_own, keep_own = second(False)
    got_own = swap_cores(send_own)
    mine = call(
        residual_kernel, [((half_rows, channels), bf16)], [],
        [latent, keep_own, got_own, summed],
    )[0]
    theirs = swap_cores(mine)
    out_send, out_keep = call(
        attention_kernel,
        [((2 * half_rows, 2 * shard), bf16), ((2 * half_rows, 2 * shard), f32)],
        [((2 * half_rows, channels), f32), ((2 * half_rows, channels), bf16),
         ((2 * half_rows, 2 * shard), bf16)],
        [mine, theirs, attn_gain[None], qkv, out_weight, heads_x, values_x, outs_x,
         heads_y, values_y, outs_z],
        flops=24 * half_rows * channels * shard, limit=24,
    )
    out_got = swap_cores(out_send)
    away = (out_keep[:, :shard] + out_got[:, :shard].astype(f32)).astype(bf16)
    stay = (out_keep[:, shard:] + out_got[:, shard:].astype(f32)).astype(bf16)
    arrived = swap_chips(away)
    return call(place_kernel, [((stems, frames, shard), bf16)], [], [stay, arrived])[0]


def local(*args):
    latent = args[0]
    stems, frames, channels = latent.shape
    tensor_size, frame_size = lax.axis_size("tensor"), lax.axis_size("frame")
    shard = channels // tensor_size
    suits = (
        tensor_size == 4
        and frame_size == 4
        and lax.axis_size("groups") == 2
        and frames == 2 * WINDOW
        and stems % 2 == 0
        and stems <= 8
        and shard % (2 * LANES) == 0
    )
    if not suits:
        return generic(*args)
    return fast(*args)


def solution(mesh):
    return jax.shard_map(
        local,
        mesh=mesh,
        in_specs=(
            P(None, ("groups", "frame"), None),
            P(),
            P(None, None, "tensor"),
            P("tensor"),
            P("tensor"),
            P(None, "tensor", None),
            P(),
            P(None, None, "tensor"),
            P("tensor", None),
        ),
        out_specs=P(None, ("groups", "frame"), "tensor"),
        check_vma=False,
    )
```

```python
import functools
import math

import jax
import jax.numpy as jnp
from jax import lax
from jax.experimental import pallas as pl
from jax.experimental.pallas import tpu as pltpu
from jax.sharding import PartitionSpec as P


GROUPS = 32
HEAD_DIM = 64
WINDOW = 64
LANES = 128
PIECES = 4

norm_eps = 1e-05
rms_eps = 1e-06
HIGHEST = lax.Precision.HIGHEST
VMEM = pltpu.VMEM
bf16 = jnp.bfloat16
f32 = jnp.float32


def extended(block, sides, width):
    for axis, dim in sides:
        count = lax.axis_size(axis)
        forward = [(i, i + 1) for i in range(count - 1)]
        backward = [(target, source) for source, target in forward]
        low = lax.ppermute(
            lax.slice_in_dim(block, block.shape[dim] - width, None, axis=dim), axis, forward
        )
        high = lax.ppermute(lax.slice_in_dim(block, 0, width, axis=dim), axis, backward)
        block = jnp.concatenate([low, block, high], axis=dim)
    return block


def group_sums(hidden, group_count):
    stem_count, frame_count, channels = hidden.shape
    grouped = hidden.reshape(stem_count, frame_count, group_count, channels // group_count)
    return (jnp.sum(grouped, axis=(1, 3)), jnp.sum(grouped * grouped, axis=(1, 3)))


def apply_group(hidden, totals, squares, entries, gain_vec):
    stem_count, frame_count, channels = hidden.shape
    group_count = totals.shape[1]
    centre = totals / entries
    spread = squares / entries - centre * centre
    grouped = hidden.reshape(stem_count, frame_count, group_count, channels // group_count)
    scaled = (grouped - centre[:, None, :, None]) * lax.rsqrt(spread + norm_eps)[:, None, :, None]
    return scaled.reshape(stem_count, frame_count, channels) * gain_vec


def conv_padded(padded, kernel, frame_count):
    stem_count = padded.shape[0]
    channels = padded.shape[2]
    result = jnp.zeros((stem_count * frame_count, kernel.shape[2]), jnp.float32)
    for tap_index in range(3):
        tap_rows = padded[:, tap_index : tap_index + frame_count].reshape(
            stem_count * frame_count, channels
        )
        result = result + jnp.dot(tap_rows, kernel[tap_index], preferred_element_type=jnp.float32)
    return result.reshape(stem_count, frame_count, kernel.shape[2])


def attend(queries, keys_all, values):
    stem_count, frame_count, head_count, head_dim = queries.shape
    window_count = frame_count // WINDOW

    def arrange(source):
        shaped = source.reshape(stem_count, window_count, WINDOW, head_count, head_dim)
        return shaped.transpose(1, 3, 0, 2, 4).reshape(
            window_count, head_count, stem_count * WINDOW, head_dim
        )

    scores = jnp.einsum(
        "nhqd,nhkd->nhqk",
        arrange(queries),
        arrange(keys_all),
        precision=lax.Precision.HIGHEST,
        preferred_element_type=jnp.float32,
    ) / math.sqrt(head_dim)
    scores = scores - jnp.max(scores, axis=3, keepdims=True)
    exp_scores = jnp.exp(scores)
    attn_probs = (exp_scores / jnp.sum(exp_scores, axis=3, keepdims=True)).astype(jnp.bfloat16)
    context = jnp.einsum(
        "nhqk,nhkd->nhqd", attn_probs, arrange(values), preferred_element_type=jnp.float32
    ).astype(jnp.bfloat16)
    context = context.reshape(window_count, head_count, stem_count, WINDOW, head_dim).transpose(
        2, 0, 3, 1, 4
    )
    return context.reshape(stem_count * frame_count, head_count * head_dim)


def generic(
    latent,
    norm1_gain,
    conv1_weight,
    time_bias,
    norm2_gain,
    conv2_weight,
    attn_gain,
    qkv_weight,
    out_weight,
):
    stem_count, frame_count, channels = latent.shape
    tensor_size = lax.axis_size("tensor")
    shard_width = channels // tensor_size
    row_count = stem_count * frame_count
    group_entries = frame_count * lax.axis_size("frame") * (channels // GROUPS)
    latent_f = latent.astype(jnp.float32)
    sums_one, squares_one = group_sums(latent_f, GROUPS)
    sums_one, squares_one = lax.psum((sums_one, squares_one), "frame")
    act_one = jax.nn.silu(
        apply_group(latent_f, sums_one, squares_one, group_entries, norm1_gain)
    ).astype(jnp.bfloat16)
    padded_one = extended(act_one, (("frame", 1),), 1)
    hid_one = conv_padded(padded_one, conv1_weight, frame_count)
    hid_one = hid_one + time_bias
    local_groups = GROUPS // tensor_size
    sums_two, squares_two = group_sums(hid_one, local_groups)
    sums_two, squares_two = lax.psum((sums_two, squares_two), "frame")
    act_two = jax.nn.silu(
        apply_group(hid_one, sums_two, squares_two, group_entries, norm2_gain)
    ).astype(jnp.bfloat16)
    padded_two = extended(act_two, (("frame", 1),), 1)
    conv_term = conv_padded(padded_two, conv2_weight, frame_count)
    own_start = lax.axis_index("tensor") * shard_width
    qkv_flat = qkv_weight.reshape(channels, 3 * shard_width)
    conv_total = lax.psum(conv_term.astype(jnp.bfloat16), "tensor").astype(jnp.float32)
    residual = (latent_f + conv_total).astype(jnp.bfloat16)
    res_f = residual.astype(jnp.float32)
    mean_sq = jnp.mean(res_f * res_f, axis=2, keepdims=True)
    normed = (res_f * lax.rsqrt(mean_sq + rms_eps) * attn_gain).astype(jnp.bfloat16)
    projected = jnp.dot(
        normed.reshape(row_count, channels), qkv_flat, preferred_element_type=jnp.float32
    )
    res_own = lax.dynamic_slice_in_dim(res_f, own_start, shard_width, 2)
    head_local = shard_width // HEAD_DIM
    projected = projected.reshape(stem_count, frame_count, 3, head_local, HEAD_DIM)
    values = projected[:, :, 2].astype(jnp.bfloat16)
    context = attend(projected[:, :, 0], projected[:, :, 1], values)
    out_term = jnp.dot(context, out_weight, preferred_element_type=jnp.float32).reshape(
        stem_count, frame_count, channels
    )
    attn_share = lax.psum_scatter(
        out_term.astype(jnp.bfloat16), "tensor", scatter_dimension=2, tiled=True
    ).astype(jnp.float32)
    velocity = (res_own + attn_share).astype(jnp.bfloat16)
    return velocity


def silu_of_half(half):
    return half + half * jnp.tanh(half)


def one_hot(rows, columns, width, by_row):
    row = lax.broadcasted_iota(jnp.int32, (rows, columns), 0)
    column = lax.broadcasted_iota(jnp.int32, (rows, columns), 1)
    if by_row:
        return (row // width == column).astype(f32)
    return (row == column // width).astype(f32)


def f32_dot(a, b):
    return jnp.dot(a, b, precision=HIGHEST, preferred_element_type=f32)


def group_totals(sums, squares, width):
    hot = one_hot(sums.shape[1], LANES, width, True)
    return f32_dot(sums, hot), f32_dot(squares, hot)


def channel_scale(refs, entries, channels, width):
    total = refs[0]
    for other in refs[1:]:
        total = total + other
    centre = total[:, :LANES] / entries
    spread = total[:, LANES:] / entries - centre * centre
    hot = one_hot(LANES, channels, width, False)
    return f32_dot(centre, hot), f32_dot(lax.rsqrt(spread + norm_eps), hot)


def stats_kernel(width, lat_ref, up_ref, down_ref, own_ref, sum_ref, square_ref):
    stems, frames, channels = lat_ref.shape
    for stem in range(stems):
        block = lat_ref[stem].astype(f32)
        sum_ref[stem : stem + 1, :] = jnp.sum(block, axis=0, keepdims=True)
        square_ref[stem : stem + 1, :] = jnp.sum(block * block, axis=0, keepdims=True)
        down_ref[stem : stem + 1, :channels] = block[:1]
        up_ref[stem : stem + 1, :channels] = block[frames - 1 :]
    sums, squares = group_totals(sum_ref[...], square_ref[...], width)
    for ref, start in ((up_ref, channels), (down_ref, channels), (own_ref, 0)):
        ref[:, start : start + LANES] = sums
        ref[:, start + LANES : start + 2 * LANES] = squares


def first_kernel(
    entries, width, frame_size,
    lat_ref, low_ref, high_ref, far_ref, own_ref, gain_ref, weight_ref, bias_ref,
    hid_ref, up_ref, down_ref, tot_ref, act_ref, edge_ref, sum_ref, square_ref,
):
    stems, frames, channels = lat_ref.shape
    shard = weight_ref.shape[2]
    place = lax.axis_index("frame")
    centre, scale = channel_scale(
        [own_ref[...], low_ref[:, channels:], high_ref[:, channels:], far_ref[...]],
        entries, channels, width,
    )
    scale = scale * (0.5 * gain_ref[...])
    edge_ref[...] = jnp.zeros_like(edge_ref)
    low = silu_of_half((low_ref[:, :channels] - centre) * scale)
    high = silu_of_half((high_ref[:, :channels] - centre) * scale)
    edge_ref[0:stems, :] = jnp.where(place > 0, low, 0.0)
    edge_ref[8 : 8 + stems, :] = jnp.where(place < frame_size - 1, high, 0.0)
    edge = edge_ref[...].astype(bf16)
    edge_low = jnp.dot(edge, weight_ref[0], preferred_element_type=f32)
    edge_high = jnp.dot(edge, weight_ref[2], preferred_element_type=f32)
    row = lax.broadcasted_iota(jnp.int32, (frames, shard), 0)
    bias = bias_ref[...]
    step = stems // 2
    for first in range(0, stems, step):
        for stem in range(first, first + step):
            block = lat_ref[stem].astype(f32)
            block = (block - centre[stem : stem + 1]) * scale[stem : stem + 1]
            act_ref[stem * frames : (stem + 1) * frames, :] = silu_of_half(block).astype(bf16)
        rows = act_ref[first * frames : (first + step) * frames, :]
        taps = [jnp.dot(rows, weight_ref[tap], preferred_element_type=f32) for tap in range(3)]
        for stem in range(first, first + step):
            lo = (stem - first) * frames
            before = pltpu.roll(taps[0][lo : lo + frames], 1, 0)
            after = pltpu.roll(taps[2][lo : lo + frames], frames - 1, 0)
            before = jnp.where(row == 0, edge_low[stem : stem + 1], before)
            after = jnp.where(row == frames - 1, edge_high[8 + stem : 9 + stem], after)
            hid = taps[1][lo : lo + frames] + before + after + bias
            hid_ref[stem] = hid
            sum_ref[stem : stem + 1, :] = jnp.sum(hid, axis=0, keepdims=True)
            square_ref[stem : stem + 1, :] = jnp.sum(hid * hid, axis=0, keepdims=True)
            down_ref[stem : stem + 1, :shard] = hid[:1]
            up_ref[stem : stem + 1, :shard] = hid[frames - 1 :]
    sums, squares = group_totals(sum_ref[...], square_ref[...], width)
    for ref, start in ((up_ref, shard), (down_ref, shard), (tot_ref, 0)):
        ref[:, start : start + LANES] = sums
        ref[:, start + LANES : start + 2 * LANES] = squares


def second_kernel(
    entries, width, frame_size, other,
    hid_ref, low_ref, high_ref, far_ref, own_ref, gain_ref, weight_ref,
    send_ref, keep_ref, act_ref,
):
    stems, _, shard = hid_ref.shape
    place = lax.axis_index("frame")
    index = lax.axis_index("tensor")
    chip, core = index // 2, index % 2
    window = 1 - chip if other else chip
    centre, scale = channel_scale(
        [own_ref[...], low_ref[:, shard:], high_ref[:, shard:], far_ref[...]],
        entries, shard, width,
    )
    scale = scale * (0.5 * gain_ref[...])
    low = jnp.where(place > 0, silu_of_half((low_ref[:, :shard] - centre) * scale), 0.0)
    high = jnp.where(
        place < frame_size - 1, silu_of_half((high_ref[:, :shard] - centre) * scale), 0.0
    )
    row = lax.broadcasted_iota(jnp.int32, (WINDOW, shard), 0)
    half = stems // 2
    for stem in range(stems):
        start = pl.multiple_of(window * WINDOW, WINDOW)
        mean, factor = centre[stem : stem + 1], scale[stem : stem + 1]
        act = silu_of_half((hid_ref[stem, pl.ds(start, WINDOW), :] - mean) * factor)
        inner = silu_of_half((hid_ref[stem, WINDOW - 8 : WINDOW + 8, :] - mean) * factor)
        before = jnp.where(window == 0, low[stem : stem + 1], inner[7:8])
        after = jnp.where(window == 0, inner[8:9], high[stem : stem + 1])
        before = jnp.where(row == 0, before, pltpu.roll(act, 1, 0))
        after = jnp.where(row == WINDOW - 1, after, pltpu.roll(act, WINDOW - 1, 0))
        mine = core if stem < half else 1 - core
        base = jnp.where(mine == 0, half * WINDOW, 0) + (stem % half) * WINDOW
        at = pl.ds(pl.multiple_of(base, WINDOW), WINDOW)
        act_ref[at, 0:shard] = before.astype(bf16)
        act_ref[at, shard : 2 * shard] = act.astype(bf16)
        act_ref[at, 2 * shard : 3 * shard] = after.astype(bf16)
    total = jnp.dot(act_ref[...], weight_ref[...], preferred_element_type=f32)
    send_ref[...] = total[: half * WINDOW].astype(bf16)
    keep_ref[...] = total[half * WINDOW :].astype(bf16)


def split2(value):
    high = value.astype(bf16)
    return high, (value - high.astype(f32)).astype(bf16)


def attention_kernel(
    mine_ref, theirs_ref, gain_ref, qkv_ref, out_ref,
    heads_x_ref, values_x_ref, outs_x_ref, heads_y_ref, values_y_ref, outs_z_ref,
    send_far_ref, keep_far_ref, send_near_ref, keep_near_ref,
    res_ref, normed_ref, context_ref,
):
    rows, channels = mine_ref.shape
    shard = qkv_ref.shape[2]
    depth = channels // 2
    part = shard // 2
    group = lax.axis_index("groups")
    index = lax.axis_index("tensor")
    chip, core = index // 2, index % 2
    for first, ref in ((0, mine_ref), (rows, theirs_ref)):
        res = ref[...].astype(f32)
        res_ref[first : first + rows, :] = res
        mean_sq = jnp.mean(res * res, axis=1, keepdims=True)
        normed_ref[first : first + rows, :] = (
            res * lax.rsqrt(mean_sq + rms_eps) * gain_ref[...]
        ).astype(bf16)
    normed = normed_ref[...]
    lane = lax.broadcasted_iota(jnp.int32, (2 * rows, LANES), 1)
    nt = (((1,), (1,)), ((), ()))
    near_at = pl.ds(pl.multiple_of(group * depth, depth), depth)
    away_at = pl.ds(pl.multiple_of((1 - group) * depth, depth), depth)

    def project(side, which):
        if side == 0:
            return jnp.dot(normed, qkv_ref[which], preferred_element_type=f32)
        from_x = heads_x_ref[which] if which < 2 else values_x_ref[...]
        from_y = heads_y_ref[which] if which < 2 else values_y_ref[...]
        near = jnp.dot(normed_ref[:, near_at], from_x, preferred_element_type=f32)
        return near + jnp.dot(normed_ref[:, away_at], from_y, preferred_element_type=f32)

    for side in range(2):
        queries, keys, values = [project(side, which) for which in range(3)]
        queries = queries * (1.0 / math.sqrt(HEAD_DIM))
        for tile in range(shard // LANES):
            at = slice(tile * LANES, (tile + 1) * LANES)
            q_high, q_low = split2(queries[:, at])
            q_low = pltpu.roll(q_low.astype(f32), HEAD_DIM, 1).astype(bf16)
            k_high, k_low = split2(keys[:, at])
            k_rolled = split2(pltpu.roll(keys[:, at], HEAD_DIM, 1))
            terms, mixing = [], []
            for head in range(LANES // HEAD_DIM):
                inside = lane // HEAD_DIM == head
                left = jnp.where(inside, q_high, q_low)
                left = jnp.concatenate([left, left], axis=1)
                right = [
                    jnp.where(inside, own, rolled)
                    for own, rolled in zip((k_high, k_low), k_rolled)
                ]
                right = jnp.concatenate(right, axis=1)
                scores = lax.dot_general(left, right, nt, preferred_element_type=f32)
                scores = jnp.exp(scores - jnp.max(scores, axis=1, keepdims=True))
                terms.append(scores.astype(bf16))
                mixing.append(
                    jnp.concatenate(
                        [jnp.where(inside, values[:, at], 0.0), jnp.where(inside, 1.0, 0.0)], axis=1
                    ).astype(bf16)
                )
            mixed = jnp.dot(
                jnp.concatenate(terms, axis=1), jnp.concatenate(mixing, axis=0),
                preferred_element_type=f32,
            )
            base = side * shard + tile * LANES
            context_ref[:, base : base + LANES] = (mixed[:, :LANES] / mixed[:, LANES:]).astype(bf16)
    context = context_ref[:, :shard]
    parity = lax.axis_index("frame") % 2
    from_x = context_ref[:, pl.ds(pl.multiple_of(shard + parity * part, part), part)]
    from_z = context_ref[:, pl.ds(pl.multiple_of(shard + (1 - parity) * part, part), part)]

    def term(block):
        at = pl.ds(pl.multiple_of(block * shard, shard), shard)
        rows_at = pl.ds(pl.multiple_of(block * part, part), part)
        value = jnp.dot(context, out_ref[:, at], preferred_element_type=f32)
        value = value + jnp.dot(from_x, outs_x_ref[rows_at, :], preferred_element_type=f32)
        return value + jnp.dot(from_z, outs_z_ref[rows_at, :], preferred_element_type=f32)

    sides = ((1 - chip, send_far_ref, keep_far_ref), (chip, send_near_ref, keep_near_ref))
    for goal, send_ref, keep_ref in sides:
        value = term(2 * goal + 1 - core).astype(bf16)
        send_ref[:rows, :] = value[rows:]
        send_ref[rows:, :] = value[:rows]
        block = 2 * goal + core
        at = pl.ds(pl.multiple_of(block * shard, shard), shard)
        keep_ref[...] = term(block) + res_ref[:, at]


def run_copies(pairs, sems):
    copies = [
        pltpu.make_async_copy(source, goal, sems.at[place])
        for place, (source, goal) in enumerate(pairs)
    ]
    for copy in copies:
        copy.start()
    for copy in copies:
        copy.wait()


def pack_heads_kernel(qkv_ref, send_ref, sems):
    depth = send_ref.shape[1]
    step = depth // PIECES
    start = lax.axis_index("groups") * depth
    pairs = []
    for which in range(2):
        for piece in range(PIECES):
            rows = pl.ds(pl.multiple_of(start + piece * step, step), step)
            goal = send_ref.at[which, pl.ds(piece * step, step), :]
            pairs.append((qkv_ref.at[which, rows, :], goal))
    run_copies(pairs, sems)


def pack_rest_kernel(qkv_ref, out_ref, send_ref, sems):
    depth, shard = send_ref.shape[1:]
    part = shard // 2
    step = depth // PIECES
    start = lax.axis_index("groups") * depth
    pairs = []
    for piece in range(PIECES):
        rows = pl.ds(pl.multiple_of(start + piece * step, step), step)
        pairs.append((qkv_ref.at[2, rows, :], send_ref.at[0, pl.ds(piece * step, step), :]))
    rows = pl.ds(pl.multiple_of(lax.axis_index("frame") % 2 * part, part), part)
    for block in range(depth // part):
        goal = send_ref.at[1, pl.ds(block * part, part), :]
        pairs.append((out_ref.at[rows, pl.ds(block * shard, shard)], goal))
    run_copies(pairs, sems)


def pack(kernel, shape, copies, args):
    return pl.pallas_call(
        kernel,
        out_shape=jax.ShapeDtypeStruct(shape, bf16),
        in_specs=[pl.BlockSpec(memory_space=pltpu.HBM)] * len(args),
        out_specs=pl.BlockSpec(memory_space=VMEM),
        scratch_shapes=[pltpu.SemaphoreType.DMA((copies,))],
        compiler_params=pltpu.CompilerParams(vmem_limit_bytes=4 * 2**20),
        cost_estimate=pl.CostEstimate(flops=0, bytes_accessed=2**20, transcendentals=0),
    )(*[pltpu.with_memory_space_constraint(arg, pltpu.HBM) for arg in args])


def residual_kernel(latent_ref, keep_ref, got_ref, far_ref, out_ref):
    stems = latent_ref.shape[0]
    index = lax.axis_index("tensor")
    chip, core = index // 2, index % 2
    start = pl.multiple_of(chip * WINDOW, WINDOW)
    for stem in range(stems // 2):
        rows = slice(stem * WINDOW, (stem + 1) * WINDOW)
        total = keep_ref[rows, :].astype(f32) + got_ref[rows, :].astype(f32)
        total = total + far_ref[rows, :].astype(f32)
        latent = latent_ref[core * (stems // 2) + stem, pl.ds(start, WINDOW), :]
        out_ref[rows, :] = (latent.astype(f32) + total).astype(bf16)


def place(value_ref, out_ref, window, sems):
    stems = out_ref.shape[0]
    core = lax.axis_index("tensor") % 2
    half = stems // 2
    at = pl.ds(pl.multiple_of(window * WINDOW, WINDOW), WINDOW)
    pairs = []
    for stem in range(stems):
        goal = (core if stem < half else 1 - core) * half + stem % half
        source = value_ref.at[pl.ds(stem * WINDOW, WINDOW), :]
        pairs.append((source, out_ref.at[goal, at, :]))
    run_copies(pairs, sems)


def place_near_kernel(keep_ref, got_ref, out_ref, value_ref, sems):
    value_ref[...] = (keep_ref[...] + got_ref[...].astype(f32)).astype(bf16)
    place(value_ref, out_ref, lax.axis_index("tensor") // 2, sems)


def place_far_kernel(value_ref, near_ref, out_ref, sems):
    del near_ref
    place(value_ref, out_ref, 1 - lax.axis_index("tensor") // 2, sems)


def call(kernel, outs, scratch, args, flops=0, moved=0, limit=16):
    return pl.pallas_call(
        kernel,
        out_shape=[jax.ShapeDtypeStruct(shape, dtype) for shape, dtype in outs],
        in_specs=[pl.BlockSpec(memory_space=VMEM)] * len(args),
        out_specs=[pl.BlockSpec(memory_space=VMEM)] * len(outs),
        scratch_shapes=[VMEM(shape, dtype) for shape, dtype in scratch],
        compiler_params=pltpu.CompilerParams(vmem_limit_bytes=limit * 2**20),
        cost_estimate=pl.CostEstimate(flops=flops, bytes_accessed=moved, transcendentals=0),
    )(*args)


def swap_cores(value):
    return lax.ppermute(value, "tensor", [(0, 1), (1, 0), (2, 3), (3, 2)])


def swap_chips(value):
    return lax.ppermute(value, "tensor", [(0, 2), (2, 0), (1, 3), (3, 1)])


def swap_groups(value):
    return lax.ppermute(value, "groups", [(0, 1), (1, 0)])


def swap_frames(value):
    return lax.ppermute(value, "frame", [(0, 1), (1, 0), (2, 3), (3, 2)])


def shift_frames(value, by):
    count = lax.axis_size("frame")
    return lax.ppermute(value, "frame", [(i, (i + by) % count) for i in range(count)])


def exchange(up, down, own):
    return (shift_frames(up, 1), shift_frames(down, -1), shift_frames(own, 2))


def fast(
    latent, norm1_gain, conv1_weight, time_bias, norm2_gain, conv2_weight,
    attn_gain, qkv_weight, out_weight,
):
    stems, frames, channels = latent.shape
    frame_size = lax.axis_size("frame")
    shard = conv1_weight.shape[2]
    width = channels // GROUPS
    entries = frames * frame_size * width
    half_rows = stems // 2 * WINDOW
    qkv = jnp.transpose(qkv_weight, (1, 0, 2))
    depth, part = channels // 2, shard // 2
    heads = pack(pack_heads_kernel, (2, depth, shard), 2 * PIECES, [qkv])
    rest = pack(
        pack_rest_kernel, (2, depth, shard), PIECES + depth // part,
        [qkv, out_weight],
    )
    heads_x = swap_chips(heads)
    rest_x = swap_chips(rest)
    heads_y = swap_groups(heads_x)
    values_x, outs_x = rest_x[0], rest_x[1]
    values_y = swap_groups(values_x)
    outs_z = swap_frames(outs_x)
    wide = channels + 2 * LANES
    up, down, own = call(
        functools.partial(stats_kernel, width),
        [((stems, wide), f32), ((stems, wide), f32), ((stems, 2 * LANES), f32)],
        [((stems, channels), f32)] * 2,
        [latent],
    )
    low, high, far = exchange(up, down, own)
    narrow = shard + 2 * LANES
    hid, up2, down2, own2 = call(
        functools.partial(first_kernel, entries, width, frame_size),
        [((stems, frames, shard), f32), ((stems, narrow), f32), ((stems, narrow), f32),
         ((stems, 2 * LANES), f32)],
        [((stems * frames, channels), bf16), ((16, channels), f32)] + [((stems, shard), f32)] * 2,
        [latent, low, high, far, own, norm1_gain[None], conv1_weight, time_bias[None]],
        flops=6 * stems * frames * channels * shard,
    )
    low2, high2, far2 = exchange(up2, down2, own2)
    weight2 = conv2_weight.reshape(3 * shard, channels)

    def second(other):
        return call(
            functools.partial(second_kernel, entries, width, frame_size, other),
            [((half_rows, channels), bf16)] * 2,
            [((2 * half_rows, 3 * shard), bf16)],
            [hid, low2, high2, far2, own2, norm2_gain[None], weight2],
            flops=12 * half_rows * channels * shard,
        )

    send, keep = second(True)
    got = swap_cores(send)
    summed = (got.astype(f32) + keep.astype(f32)).astype(bf16)
    summed = swap_chips(summed)
    send_own, keep_own = second(False)
    got_own = swap_cores(send_own)
    mine = call(
        residual_kernel, [((half_rows, channels), bf16)], [],
        [latent, keep_own, got_own, summed],
    )[0]
    theirs = swap_cores(mine)
    send_far, keep_far, send_near, keep_near = call(
        attention_kernel,
        [((2 * half_rows, shard), bf16), ((2 * half_rows, shard), f32)] * 2,
        [((2 * half_rows, channels), f32), ((2 * half_rows, channels), bf16),
         ((2 * half_rows, 2 * shard), bf16)],
        [mine, theirs, attn_gain[None], qkv, out_weight, heads_x, values_x, outs_x,
         heads_y, values_y, outs_z],
        flops=24 * half_rows * channels * shard, limit=24,
    )
    got_far = swap_cores(send_far)
    got_near = swap_cores(send_near)
    away = (keep_far + got_far.astype(f32)).astype(bf16)
    arrived = swap_chips(away)
    vmem, anywhere = pl.BlockSpec(memory_space=VMEM), pl.BlockSpec(memory_space=pl.ANY)
    shape = jax.ShapeDtypeStruct((stems, frames, shard), bf16)
    sems = pltpu.SemaphoreType.DMA((stems,))
    params = pltpu.CompilerParams(vmem_limit_bytes=4 * 2**20)
    near = pl.pallas_call(
        place_near_kernel, name="place_near", out_shape=shape,
        in_specs=[vmem, vmem], out_specs=anywhere, compiler_params=params,
        scratch_shapes=[VMEM((2 * half_rows, shard), bf16), sems],
    )(keep_near, got_near)
    return pl.pallas_call(
        place_far_kernel, name="place_far", out_shape=shape,
        in_specs=[vmem, anywhere], out_specs=anywhere, compiler_params=params,
        scratch_shapes=[sems], input_output_aliases={1: 0},
    )(arrived, near)


def local(*args):
    latent = args[0]
    stems, frames, channels = latent.shape
    tensor_size, frame_size = lax.axis_size("tensor"), lax.axis_size("frame")
    shard = channels // tensor_size
    suits = (
        tensor_size == 4
        and frame_size == 4
        and lax.axis_size("groups") == 2
        and frames == 2 * WINDOW
        and stems % 2 == 0
        and stems <= 8
        and shard % (2 * LANES) == 0
    )
    if not suits:
        return generic(*args)
    return fast(*args)


def solution(mesh):
    return jax.shard_map(
        local,
        mesh=mesh,
        in_specs=(
            P(None, ("groups", "frame"), None),
            P(),
            P(None, None, "tensor"),
            P("tensor"),
            P("tensor"),
            P(None, "tensor", None),
            P(),
            P(None, None, "tensor"),
            P("tensor", None),
        ),
        out_specs=P(None, ("groups", "frame"), "tensor"),
        check_vma=False,
    )
```

```python
import functools
import math

import jax
import jax.numpy as jnp
from jax import lax
from jax.experimental import pallas as pl
from jax.experimental.pallas import tpu as pltpu
from jax.sharding import PartitionSpec as P


GROUPS = 32
HEAD_DIM = 64
WINDOW = 64
LANES = 128
PIECES = 4

norm_eps = 1e-05
rms_eps = 1e-06
HIGHEST = lax.Precision.HIGHEST
VMEM = pltpu.VMEM
bf16 = jnp.bfloat16
f32 = jnp.float32


def extended(block, sides, width):
    for axis, dim in sides:
        count = lax.axis_size(axis)
        forward = [(i, i + 1) for i in range(count - 1)]
        backward = [(target, source) for source, target in forward]
        low = lax.ppermute(
            lax.slice_in_dim(block, block.shape[dim] - width, None, axis=dim), axis, forward
        )
        high = lax.ppermute(lax.slice_in_dim(block, 0, width, axis=dim), axis, backward)
        block = jnp.concatenate([low, block, high], axis=dim)
    return block


def group_sums(hidden, group_count):
    stem_count, frame_count, channels = hidden.shape
    grouped = hidden.reshape(stem_count, frame_count, group_count, channels // group_count)
    return (jnp.sum(grouped, axis=(1, 3)), jnp.sum(grouped * grouped, axis=(1, 3)))


def apply_group(hidden, totals, squares, entries, gain_vec):
    stem_count, frame_count, channels = hidden.shape
    group_count = totals.shape[1]
    centre = totals / entries
    spread = squares / entries - centre * centre
    grouped = hidden.reshape(stem_count, frame_count, group_count, channels // group_count)
    scaled = (grouped - centre[:, None, :, None]) * lax.rsqrt(spread + norm_eps)[:, None, :, None]
    return scaled.reshape(stem_count, frame_count, channels) * gain_vec


def conv_padded(padded, kernel, frame_count):
    stem_count = padded.shape[0]
    channels = padded.shape[2]
    result = jnp.zeros((stem_count * frame_count, kernel.shape[2]), jnp.float32)
    for tap_index in range(3):
        tap_rows = padded[:, tap_index : tap_index + frame_count].reshape(
            stem_count * frame_count, channels
        )
        result = result + jnp.dot(tap_rows, kernel[tap_index], preferred_element_type=jnp.float32)
    return result.reshape(stem_count, frame_count, kernel.shape[2])


def attend(queries, keys_all, values):
    stem_count, frame_count, head_count, head_dim = queries.shape
    window_count = frame_count // WINDOW

    def arrange(source):
        shaped = source.reshape(stem_count, window_count, WINDOW, head_count, head_dim)
        return shaped.transpose(1, 3, 0, 2, 4).reshape(
            window_count, head_count, stem_count * WINDOW, head_dim
        )

    scores = jnp.einsum(
        "nhqd,nhkd->nhqk",
        arrange(queries),
        arrange(keys_all),
        precision=lax.Precision.HIGHEST,
        preferred_element_type=jnp.float32,
    ) / math.sqrt(head_dim)
    scores = scores - jnp.max(scores, axis=3, keepdims=True)
    exp_scores = jnp.exp(scores)
    attn_probs = (exp_scores / jnp.sum(exp_scores, axis=3, keepdims=True)).astype(jnp.bfloat16)
    context = jnp.einsum(
        "nhqk,nhkd->nhqd", attn_probs, arrange(values), preferred_element_type=jnp.float32
    ).astype(jnp.bfloat16)
    context = context.reshape(window_count, head_count, stem_count, WINDOW, head_dim).transpose(
        2, 0, 3, 1, 4
    )
    return context.reshape(stem_count * frame_count, head_count * head_dim)


def generic(
    latent,
    norm1_gain,
    conv1_weight,
    time_bias,
    norm2_gain,
    conv2_weight,
    attn_gain,
    qkv_weight,
    out_weight,
):
    stem_count, frame_count, channels = latent.shape
    tensor_size = lax.axis_size("tensor")
    shard_width = channels // tensor_size
    row_count = stem_count * frame_count
    group_entries = frame_count * lax.axis_size("frame") * (channels // GROUPS)
    latent_f = latent.astype(jnp.float32)
    sums_one, squares_one = group_sums(latent_f, GROUPS)
    sums_one, squares_one = lax.psum((sums_one, squares_one), "frame")
    act_one = jax.nn.silu(
        apply_group(latent_f, sums_one, squares_one, group_entries, norm1_gain)
    ).astype(jnp.bfloat16)
    padded_one = extended(act_one, (("frame", 1),), 1)
    hid_one = conv_padded(padded_one, conv1_weight, frame_count)
    hid_one = hid_one + time_bias
    local_groups = GROUPS // tensor_size
    sums_two, squares_two = group_sums(hid_one, local_groups)
    sums_two, squares_two = lax.psum((sums_two, squares_two), "frame")
    act_two = jax.nn.silu(
        apply_group(hid_one, sums_two, squares_two, group_entries, norm2_gain)
    ).astype(jnp.bfloat16)
    padded_two = extended(act_two, (("frame", 1),), 1)
    conv_term = conv_padded(padded_two, conv2_weight, frame_count)
    own_start = lax.axis_index("tensor") * shard_width
    qkv_flat = qkv_weight.reshape(channels, 3 * shard_width)
    conv_total = lax.psum(conv_term.astype(jnp.bfloat16), "tensor").astype(jnp.float32)
    residual = (latent_f + conv_total).astype(jnp.bfloat16)
    res_f = residual.astype(jnp.float32)
    mean_sq = jnp.mean(res_f * res_f, axis=2, keepdims=True)
    normed = (res_f * lax.rsqrt(mean_sq + rms_eps) * attn_gain).astype(jnp.bfloat16)
    projected = jnp.dot(
        normed.reshape(row_count, channels), qkv_flat, preferred_element_type=jnp.float32
    )
    res_own = lax.dynamic_slice_in_dim(res_f, own_start, shard_width, 2)
    head_local = shard_width // HEAD_DIM
    projected = projected.reshape(stem_count, frame_count, 3, head_local, HEAD_DIM)
    values = projected[:, :, 2].astype(jnp.bfloat16)
    context = attend(projected[:, :, 0], projected[:, :, 1], values)
    out_term = jnp.dot(context, out_weight, preferred_element_type=jnp.float32).reshape(
        stem_count, frame_count, channels
    )
    attn_share = lax.psum_scatter(
        out_term.astype(jnp.bfloat16), "tensor", scatter_dimension=2, tiled=True
    ).astype(jnp.float32)
    velocity = (res_own + attn_share).astype(jnp.bfloat16)
    return velocity


def silu_of_half(half):
    return half + half * jnp.tanh(half)


def one_hot(rows, columns, width, by_row):
    row = lax.broadcasted_iota(jnp.int32, (rows, columns), 0)
    column = lax.broadcasted_iota(jnp.int32, (rows, columns), 1)
    if by_row:
        return (row // width == column).astype(f32)
    return (row == column // width).astype(f32)


def f32_dot(a, b):
    return jnp.dot(a, b, precision=HIGHEST, preferred_element_type=f32)


def even_place():
    return lax.axis_index("frame") % 2 == 0


def group_totals(sums, squares, width):
    hot = one_hot(sums.shape[1], LANES, width, True)
    return f32_dot(sums, hot), f32_dot(squares, hot)


def channel_scale(refs, entries, channels, width):
    total = refs[0]
    for other in refs[1:]:
        total = total + other
    centre = total[:, :LANES] / entries
    spread = total[:, LANES:] / entries - centre * centre
    hot = one_hot(LANES, channels, width, False)
    return f32_dot(centre, hot), f32_dot(lax.rsqrt(spread + norm_eps), hot)


def stats_kernel(width, lat_ref, one_ref, two_ref, own_ref, sum_ref, square_ref):
    stems, frames, channels = lat_ref.shape
    even = even_place()
    for stem in range(stems):
        block = lat_ref[stem].astype(f32)
        sum_ref[stem : stem + 1, :] = jnp.sum(block, axis=0, keepdims=True)
        square_ref[stem : stem + 1, :] = jnp.sum(block * block, axis=0, keepdims=True)
        down, up = block[:1], block[frames - 1 :]
        one_ref[stem : stem + 1, :channels] = jnp.where(even, up, down)
        two_ref[stem : stem + 1, :channels] = jnp.where(even, down, up)
    sums, squares = group_totals(sum_ref[...], square_ref[...], width)
    for ref, start in ((one_ref, channels), (two_ref, channels), (own_ref, 0)):
        ref[:, start : start + LANES] = sums
        ref[:, start + LANES : start + 2 * LANES] = squares


def first_kernel(
    entries, width, frame_size,
    lat_ref, got_ref, swapped_ref, far_ref, own_ref, gain_ref, weight_ref, bias_ref,
    hid_ref, one_ref, two_ref, tot_ref, act_ref, edge_ref, sum_ref, square_ref,
):
    stems, frames, channels = lat_ref.shape
    shard = weight_ref.shape[2]
    place = lax.axis_index("frame")
    centre, scale = channel_scale(
        [own_ref[...], got_ref[:, channels:], swapped_ref[:, channels:], far_ref[...]],
        entries, channels, width,
    )
    even = even_place()
    first_got = even == (lax.axis_index("tensor") % 2 == 0)
    got, swapped = got_ref[:, :channels], swapped_ref[:, :channels]
    high, low = jnp.where(first_got, got, swapped), jnp.where(first_got, swapped, got)
    scale = scale * (0.5 * gain_ref[...])
    edge_ref[...] = jnp.zeros_like(edge_ref)
    low = silu_of_half((low - centre) * scale)
    high = silu_of_half((high - centre) * scale)
    edge_ref[0:stems, :] = jnp.where(place > 0, low, 0.0)
    edge_ref[8 : 8 + stems, :] = jnp.where(place < frame_size - 1, high, 0.0)
    edge = edge_ref[...].astype(bf16)
    edge_low = jnp.dot(edge, weight_ref[0], preferred_element_type=f32)
    edge_high = jnp.dot(edge, weight_ref[2], preferred_element_type=f32)
    row = lax.broadcasted_iota(jnp.int32, (frames, shard), 0)
    bias = bias_ref[...]
    step = stems // 2
    for first in range(0, stems, step):
        for stem in range(first, first + step):
            block = lat_ref[stem].astype(f32)
            block = (block - centre[stem : stem + 1]) * scale[stem : stem + 1]
            act_ref[stem * frames : (stem + 1) * frames, :] = silu_of_half(block).astype(bf16)
        rows = act_ref[first * frames : (first + step) * frames, :]
        taps = [jnp.dot(rows, weight_ref[tap], preferred_element_type=f32) for tap in range(3)]
        for stem in range(first, first + step):
            lo = (stem - first) * frames
            before = pltpu.roll(taps[0][lo : lo + frames], 1, 0)
            after = pltpu.roll(taps[2][lo : lo + frames], frames - 1, 0)
            before = jnp.where(row == 0, edge_low[stem : stem + 1], before)
            after = jnp.where(row == frames - 1, edge_high[8 + stem : 9 + stem], after)
            hid = taps[1][lo : lo + frames] + before + after + bias
            hid_ref[stem] = hid
            sum_ref[stem : stem + 1, :] = jnp.sum(hid, axis=0, keepdims=True)
            square_ref[stem : stem + 1, :] = jnp.sum(hid * hid, axis=0, keepdims=True)
            down, up = hid[:1], hid[frames - 1 :]
            one_ref[stem : stem + 1, :shard] = jnp.where(even, up, down)
            two_ref[stem : stem + 1, :shard] = jnp.where(even, down, up)
    sums, squares = group_totals(sum_ref[...], square_ref[...], width)
    for ref, start in ((one_ref, shard), (two_ref, shard), (tot_ref, 0)):
        ref[:, start : start + LANES] = sums
        ref[:, start + LANES : start + 2 * LANES] = squares


def second_kernel(
    entries, width, frame_size, other,
    hid_ref, one_ref, two_ref, far_ref, own_ref, gain_ref, weight_ref,
    send_ref, keep_ref, act_ref,
):
    stems, _, shard = hid_ref.shape
    place = lax.axis_index("frame")
    index = lax.axis_index("tensor")
    chip, core = index // 2, index % 2
    window = 1 - chip if other else chip
    centre, scale = channel_scale(
        [own_ref[...], one_ref[:, shard:], two_ref[:, shard:], far_ref[...]],
        entries, shard, width,
    )
    even = even_place()
    one, two = one_ref[:, :shard], two_ref[:, :shard]
    high, low = jnp.where(even, one, two), jnp.where(even, two, one)
    scale = scale * (0.5 * gain_ref[...])
    low = jnp.where(place > 0, silu_of_half((low - centre) * scale), 0.0)
    high = jnp.where(place < frame_size - 1, silu_of_half((high - centre) * scale), 0.0)
    row = lax.broadcasted_iota(jnp.int32, (WINDOW, shard), 0)
    half = stems // 2
    for stem in range(stems):
        start = pl.multiple_of(window * WINDOW, WINDOW)
        mean, factor = centre[stem : stem + 1], scale[stem : stem + 1]
        act = silu_of_half((hid_ref[stem, pl.ds(start, WINDOW), :] - mean) * factor)
        inner = silu_of_half((hid_ref[stem, WINDOW - 8 : WINDOW + 8, :] - mean) * factor)
        before = jnp.where(window == 0, low[stem : stem + 1], inner[7:8])
        after = jnp.where(window == 0, inner[8:9], high[stem : stem + 1])
        before = jnp.where(row == 0, before, pltpu.roll(act, 1, 0))
        after = jnp.where(row == WINDOW - 1, after, pltpu.roll(act, WINDOW - 1, 0))
        mine = core if stem < half else 1 - core
        base = jnp.where(mine == 0, half * WINDOW, 0) + (stem % half) * WINDOW
        at = pl.ds(pl.multiple_of(base, WINDOW), WINDOW)
        act_ref[at, 0:shard] = before.astype(bf16)
        act_ref[at, shard : 2 * shard] = act.astype(bf16)
        act_ref[at, 2 * shard : 3 * shard] = after.astype(bf16)
    total = jnp.dot(act_ref[...], weight_ref[...], preferred_element_type=f32)
    send_ref[...] = total[: half * WINDOW].astype(bf16)
    keep_ref[...] = total[half * WINDOW :].astype(bf16)


def split2(value):
    high = value.astype(bf16)
    return high, (value - high.astype(f32)).astype(bf16)


def attention_kernel(
    mine_ref, theirs_ref, gain_ref, qkv_ref, out_ref,
    heads_x_ref, values_x_ref, outs_x_ref, heads_y_ref, values_y_ref, outs_z_ref,
    send_far_ref, keep_far_ref, send_near_ref, keep_near_ref,
    res_ref, normed_ref, context_ref,
):
    rows, channels = mine_ref.shape
    shard = qkv_ref.shape[2]
    depth = channels // 2
    part = shard // 2
    group = lax.axis_index("groups")
    index = lax.axis_index("tensor")
    chip, core = index // 2, index % 2
    for first, ref in ((0, mine_ref), (rows, theirs_ref)):
        res = ref[...].astype(f32)
        res_ref[first : first + rows, :] = res
        mean_sq = jnp.mean(res * res, axis=1, keepdims=True)
        normed_ref[first : first + rows, :] = (
            res * lax.rsqrt(mean_sq + rms_eps) * gain_ref[...]
        ).astype(bf16)
    normed = normed_ref[...]
    lane = lax.broadcasted_iota(jnp.int32, (2 * rows, LANES), 1)
    nt = (((1,), (1,)), ((), ()))
    near_at = pl.ds(pl.multiple_of(group * depth, depth), depth)
    away_at = pl.ds(pl.multiple_of((1 - group) * depth, depth), depth)

    def project(side, which):
        if side == 0:
            return jnp.dot(normed, qkv_ref[which], preferred_element_type=f32)
        from_x = heads_x_ref[which] if which < 2 else values_x_ref[...]
        from_y = heads_y_ref[which] if which < 2 else values_y_ref[...]
        near = jnp.dot(normed_ref[:, near_at], from_x, preferred_element_type=f32)
        return near + jnp.dot(normed_ref[:, away_at], from_y, preferred_element_type=f32)

    for side in range(2):
        queries, keys, values = [project(side, which) for which in range(3)]
        queries = queries * (1.0 / math.sqrt(HEAD_DIM))
        for tile in range(shard // LANES):
            at = slice(tile * LANES, (tile + 1) * LANES)
            q_high, q_low = split2(queries[:, at])
            q_low = pltpu.roll(q_low.astype(f32), HEAD_DIM, 1).astype(bf16)
            k_high, k_low = split2(keys[:, at])
            k_rolled = split2(pltpu.roll(keys[:, at], HEAD_DIM, 1))
            terms, mixing = [], []
            for head in range(LANES // HEAD_DIM):
                inside = lane // HEAD_DIM == head
                left = jnp.where(inside, q_high, q_low)
                left = jnp.concatenate([left, left], axis=1)
                right = [
                    jnp.where(inside, own, rolled)
                    for own, rolled in zip((k_high, k_low), k_rolled)
                ]
                right = jnp.concatenate(right, axis=1)
                scores = lax.dot_general(left, right, nt, preferred_element_type=f32)
                scores = jnp.exp(scores - jnp.max(scores, axis=1, keepdims=True))
                terms.append(scores.astype(bf16))
                mixing.append(
                    jnp.concatenate(
                        [jnp.where(inside, values[:, at], 0.0), jnp.where(inside, 1.0, 0.0)], axis=1
                    ).astype(bf16)
                )
            mixed = jnp.dot(
                jnp.concatenate(terms, axis=1), jnp.concatenate(mixing, axis=0),
                preferred_element_type=f32,
            )
            base = side * shard + tile * LANES
            context_ref[:, base : base + LANES] = (mixed[:, :LANES] / mixed[:, LANES:]).astype(bf16)
    context = context_ref[:, :shard]
    parity = lax.axis_index("frame") % 2
    from_x = context_ref[:, pl.ds(pl.multiple_of(shard + parity * part, part), part)]
    from_z = context_ref[:, pl.ds(pl.multiple_of(shard + (1 - parity) * part, part), part)]

    def term(block):
        at = pl.ds(pl.multiple_of(block * shard, shard), shard)
        rows_at = pl.ds(pl.multiple_of(block * part, part), part)
        value = jnp.dot(context, out_ref[:, at], preferred_element_type=f32)
        value = value + jnp.dot(from_x, outs_x_ref[rows_at, :], preferred_element_type=f32)
        return value + jnp.dot(from_z, outs_z_ref[rows_at, :], preferred_element_type=f32)

    sides = ((1 - chip, send_far_ref, keep_far_ref), (chip, send_near_ref, keep_near_ref))
    for goal, send_ref, keep_ref in sides:
        value = term(2 * goal + 1 - core).astype(bf16)
        send_ref[:rows, :] = value[rows:]
        send_ref[rows:, :] = value[:rows]
        block = 2 * goal + core
        at = pl.ds(pl.multiple_of(block * shard, shard), shard)
        keep_ref[...] = term(block) + res_ref[:, at]


def run_copies(pairs, sems):
    copies = [
        pltpu.make_async_copy(source, goal, sems.at[place])
        for place, (source, goal) in enumerate(pairs)
    ]
    for copy in copies:
        copy.start()
    for copy in copies:
        copy.wait()


def pack_heads_kernel(qkv_ref, send_ref, sems):
    depth = send_ref.shape[1]
    step = depth // PIECES
    start = lax.axis_index("groups") * depth
    pairs = []
    for which in range(2):
        for piece in range(PIECES):
            rows = pl.ds(pl.multiple_of(start + piece * step, step), step)
            goal = send_ref.at[which, pl.ds(piece * step, step), :]
            pairs.append((qkv_ref.at[which, rows, :], goal))
    run_copies(pairs, sems)


def pack_rest_kernel(qkv_ref, out_ref, send_ref, sems):
    depth, shard = send_ref.shape[1:]
    part = shard // 2
    step = depth // PIECES
    start = lax.axis_index("groups") * depth
    pairs = []
    for piece in range(PIECES):
        rows = pl.ds(pl.multiple_of(start + piece * step, step), step)
        pairs.append((qkv_ref.at[2, rows, :], send_ref.at[0, pl.ds(piece * step, step), :]))
    rows = pl.ds(pl.multiple_of(lax.axis_index("frame") % 2 * part, part), part)
    for block in range(depth // part):
        goal = send_ref.at[1, pl.ds(block * part, part), :]
        pairs.append((out_ref.at[rows, pl.ds(block * shard, shard)], goal))
    run_copies(pairs, sems)


def pack(kernel, shape, copies, args):
    return pl.pallas_call(
        kernel,
        out_shape=jax.ShapeDtypeStruct(shape, bf16),
        in_specs=[pl.BlockSpec(memory_space=pltpu.HBM)] * len(args),
        out_specs=pl.BlockSpec(memory_space=VMEM),
        scratch_shapes=[pltpu.SemaphoreType.DMA((copies,))],
        compiler_params=pltpu.CompilerParams(vmem_limit_bytes=4 * 2**20),
        cost_estimate=pl.CostEstimate(flops=0, bytes_accessed=2**20, transcendentals=0),
    )(*[pltpu.with_memory_space_constraint(arg, pltpu.HBM) for arg in args])


def residual_kernel(latent_ref, keep_ref, got_ref, far_ref, out_ref):
    stems = latent_ref.shape[0]
    index = lax.axis_index("tensor")
    chip, core = index // 2, index % 2
    start = pl.multiple_of(chip * WINDOW, WINDOW)
    for stem in range(stems // 2):
        rows = slice(stem * WINDOW, (stem + 1) * WINDOW)
        total = keep_ref[rows, :].astype(f32) + got_ref[rows, :].astype(f32)
        total = total + far_ref[rows, :].astype(f32)
        latent = latent_ref[core * (stems // 2) + stem, pl.ds(start, WINDOW), :]
        out_ref[rows, :] = (latent.astype(f32) + total).astype(bf16)


def place(value_ref, out_ref, window, sems):
    stems = out_ref.shape[0]
    core = lax.axis_index("tensor") % 2
    half = stems // 2
    at = pl.ds(pl.multiple_of(window * WINDOW, WINDOW), WINDOW)
    pairs = []
    for stem in range(stems):
        goal = (core if stem < half else 1 - core) * half + stem % half
        source = value_ref.at[pl.ds(stem * WINDOW, WINDOW), :]
        pairs.append((source, out_ref.at[goal, at, :]))
    run_copies(pairs, sems)


def place_near_kernel(keep_ref, got_ref, out_ref, value_ref, sems):
    value_ref[...] = (keep_ref[...] + got_ref[...].astype(f32)).astype(bf16)
    place(value_ref, out_ref, lax.axis_index("tensor") // 2, sems)


def place_far_kernel(value_ref, near_ref, out_ref, sems):
    del near_ref
    place(value_ref, out_ref, 1 - lax.axis_index("tensor") // 2, sems)


def call(kernel, outs, scratch, args, flops=0, moved=0, limit=16):
    return pl.pallas_call(
        kernel,
        out_shape=[jax.ShapeDtypeStruct(shape, dtype) for shape, dtype in outs],
        in_specs=[pl.BlockSpec(memory_space=VMEM)] * len(args),
        out_specs=[pl.BlockSpec(memory_space=VMEM)] * len(outs),
        scratch_shapes=[VMEM(shape, dtype) for shape, dtype in scratch],
        compiler_params=pltpu.CompilerParams(vmem_limit_bytes=limit * 2**20),
        cost_estimate=pl.CostEstimate(flops=flops, bytes_accessed=moved, transcendentals=0),
    )(*args)


def swap_cores(value):
    return lax.ppermute(value, "tensor", [(0, 1), (1, 0), (2, 3), (3, 2)])


def swap_chips(value):
    return lax.ppermute(value, "tensor", [(0, 2), (2, 0), (1, 3), (3, 1)])


def swap_groups(value):
    return lax.ppermute(value, "groups", [(0, 1), (1, 0)])


def swap_frames(value):
    return lax.ppermute(value, "frame", [(0, 1), (1, 0), (2, 3), (3, 2)])


ONE = ((0, 1), (1, 0), (2, 3), (3, 2))
TWO = ((0, 3), (3, 0), (1, 2), (2, 1))
FAR = ((0, 2), (2, 0), (1, 3), (3, 1))


def trade(value, pairs):
    return lax.ppermute(value, "frame", pairs)


def trade_by_core(one, two):
    count = lax.axis_size("tensor")
    pairs = [
        (source * count + index, goal * count + index)
        for index in range(count)
        for source, goal in (TWO if index % 2 else ONE)
    ]
    value = jnp.where(lax.axis_index("tensor") % 2 == 0, one, two)
    return lax.ppermute(value, ("frame", "tensor"), pairs)


def fast(
    latent, norm1_gain, conv1_weight, time_bias, norm2_gain, conv2_weight,
    attn_gain, qkv_weight, out_weight,
):
    stems, frames, channels = latent.shape
    frame_size = lax.axis_size("frame")
    shard = conv1_weight.shape[2]
    width = channels // GROUPS
    entries = frames * frame_size * width
    half_rows = stems // 2 * WINDOW
    qkv = jnp.transpose(qkv_weight, (1, 0, 2))
    depth, part = channels // 2, shard // 2
    heads = pack(pack_heads_kernel, (2, depth, shard), 2 * PIECES, [qkv])
    rest = pack(
        pack_rest_kernel, (2, depth, shard), PIECES + depth // part,
        [qkv, out_weight],
    )
    heads_x = swap_chips(heads)
    rest_x = swap_chips(rest)
    heads_y = swap_groups(heads_x)
    values_x, outs_x = rest_x[0], rest_x[1]
    values_y = swap_groups(values_x)
    outs_z = swap_frames(outs_x)
    wide = channels + 2 * LANES
    one, two, own = call(
        functools.partial(stats_kernel, width),
        [((stems, wide), f32), ((stems, wide), f32), ((stems, 2 * LANES), f32)],
        [((stems, channels), f32)] * 2,
        [latent],
    )
    far = trade(own, FAR)
    got = trade_by_core(one, two)
    swapped = swap_cores(got)
    narrow = shard + 2 * LANES
    hid, one2, two2, own2 = call(
        functools.partial(first_kernel, entries, width, frame_size),
        [((stems, frames, shard), f32), ((stems, narrow), f32), ((stems, narrow), f32),
         ((stems, 2 * LANES), f32)],
        [((stems * frames, channels), bf16), ((16, channels), f32)] + [((stems, shard), f32)] * 2,
        [latent, got, swapped, far, own, norm1_gain[None], conv1_weight, time_bias[None]],
        flops=6 * stems * frames * channels * shard,
    )
    far2 = trade(own2, FAR)
    got_two = trade(two2, TWO)
    got_one = trade(one2, ONE)
    weight2 = conv2_weight.reshape(3 * shard, channels)

    def second(other):
        return call(
            functools.partial(second_kernel, entries, width, frame_size, other),
            [((half_rows, channels), bf16)] * 2,
            [((2 * half_rows, 3 * shard), bf16)],
            [hid, got_one, got_two, far2, own2, norm2_gain[None], weight2],
            flops=12 * half_rows * channels * shard,
        )

    send, keep = second(True)
    got = swap_cores(send)
    summed = (got.astype(f32) + keep.astype(f32)).astype(bf16)
    summed = swap_chips(summed)
    send_own, keep_own = second(False)
    got_own = swap_cores(send_own)
    mine = call(
        residual_kernel, [((half_rows, channels), bf16)], [],
        [latent, keep_own, got_own, summed],
    )[0]
    theirs = swap_cores(mine)
    send_far, keep_far, send_near, keep_near = call(
        attention_kernel,
        [((2 * half_rows, shard), bf16), ((2 * half_rows, shard), f32)] * 2,
        [((2 * half_rows, channels), f32), ((2 * half_rows, channels), bf16),
         ((2 * half_rows, 2 * shard), bf16)],
        [mine, theirs, attn_gain[None], qkv, out_weight, heads_x, values_x, outs_x,
         heads_y, values_y, outs_z],
        flops=24 * half_rows * channels * shard, limit=24,
    )
    got_far = swap_cores(send_far)
    got_near = swap_cores(send_near)
    away = (keep_far + got_far.astype(f32)).astype(bf16)
    arrived = swap_chips(away)
    vmem, anywhere = pl.BlockSpec(memory_space=VMEM), pl.BlockSpec(memory_space=pl.ANY)
    shape = jax.ShapeDtypeStruct((stems, frames, shard), bf16)
    sems = pltpu.SemaphoreType.DMA((stems,))
    params = pltpu.CompilerParams(vmem_limit_bytes=4 * 2**20)
    near = pl.pallas_call(
        place_near_kernel, name="place_near", out_shape=shape,
        in_specs=[vmem, vmem], out_specs=anywhere, compiler_params=params,
        scratch_shapes=[VMEM((2 * half_rows, shard), bf16), sems],
    )(keep_near, got_near)
    return pl.pallas_call(
        place_far_kernel, name="place_far", out_shape=shape,
        in_specs=[vmem, anywhere], out_specs=anywhere, compiler_params=params,
        scratch_shapes=[sems], input_output_aliases={1: 0},
    )(arrived, near)


def local(*args):
    latent = args[0]
    stems, frames, channels = latent.shape
    tensor_size, frame_size = lax.axis_size("tensor"), lax.axis_size("frame")
    shard = channels // tensor_size
    suits = (
        tensor_size == 4
        and frame_size == 4
        and lax.axis_size("groups") == 2
        and frames == 2 * WINDOW
        and stems % 2 == 0
        and stems <= 8
        and shard % (2 * LANES) == 0
    )
    if not suits:
        return generic(*args)
    return fast(*args)


def solution(mesh):
    return jax.shard_map(
        local,
        mesh=mesh,
        in_specs=(
            P(None, ("groups", "frame"), None),
            P(),
            P(None, None, "tensor"),
            P("tensor"),
            P("tensor"),
            P(None, "tensor", None),
            P(),
            P(None, None, "tensor"),
            P("tensor", None),
        ),
        out_specs=P(None, ("groups", "frame"), "tensor"),
        check_vma=False,
    )
```

```python
import functools
import math

import jax
import jax.numpy as jnp
from jax import lax
from jax.experimental import pallas as pl
from jax.experimental.pallas import tpu as pltpu
from jax.sharding import PartitionSpec as P


GROUPS = 32
HEAD_DIM = 64
WINDOW = 64
LANES = 128
PIECES = 4
CHUNK = 2

norm_eps = 1e-05
rms_eps = 1e-06
HIGHEST = lax.Precision.HIGHEST
VMEM = pltpu.VMEM
bf16 = jnp.bfloat16
f32 = jnp.float32


def extended(block, sides, width):
    for axis, dim in sides:
        count = lax.axis_size(axis)
        forward = [(i, i + 1) for i in range(count - 1)]
        backward = [(target, source) for source, target in forward]
        low = lax.ppermute(
            lax.slice_in_dim(block, block.shape[dim] - width, None, axis=dim), axis, forward
        )
        high = lax.ppermute(lax.slice_in_dim(block, 0, width, axis=dim), axis, backward)
        block = jnp.concatenate([low, block, high], axis=dim)
    return block


def group_sums(hidden, group_count):
    stem_count, frame_count, channels = hidden.shape
    grouped = hidden.reshape(stem_count, frame_count, group_count, channels // group_count)
    return (jnp.sum(grouped, axis=(1, 3)), jnp.sum(grouped * grouped, axis=(1, 3)))


def apply_group(hidden, totals, squares, entries, gain_vec):
    stem_count, frame_count, channels = hidden.shape
    group_count = totals.shape[1]
    centre = totals / entries
    spread = squares / entries - centre * centre
    grouped = hidden.reshape(stem_count, frame_count, group_count, channels // group_count)
    scaled = (grouped - centre[:, None, :, None]) * lax.rsqrt(spread + norm_eps)[:, None, :, None]
    return scaled.reshape(stem_count, frame_count, channels) * gain_vec


def conv_padded(padded, kernel, frame_count):
    stem_count = padded.shape[0]
    channels = padded.shape[2]
    result = jnp.zeros((stem_count * frame_count, kernel.shape[2]), jnp.float32)
    for tap_index in range(3):
        tap_rows = padded[:, tap_index : tap_index + frame_count].reshape(
            stem_count * frame_count, channels
        )
        result = result + jnp.dot(tap_rows, kernel[tap_index], preferred_element_type=jnp.float32)
    return result.reshape(stem_count, frame_count, kernel.shape[2])


def attend(queries, keys_all, values):
    stem_count, frame_count, head_count, head_dim = queries.shape
    window_count = frame_count // WINDOW

    def arrange(source):
        shaped = source.reshape(stem_count, window_count, WINDOW, head_count, head_dim)
        return shaped.transpose(1, 3, 0, 2, 4).reshape(
            window_count, head_count, stem_count * WINDOW, head_dim
        )

    scores = jnp.einsum(
        "nhqd,nhkd->nhqk",
        arrange(queries),
        arrange(keys_all),
        precision=lax.Precision.HIGHEST,
        preferred_element_type=jnp.float32,
    ) / math.sqrt(head_dim)
    scores = scores - jnp.max(scores, axis=3, keepdims=True)
    exp_scores = jnp.exp(scores)
    attn_probs = (exp_scores / jnp.sum(exp_scores, axis=3, keepdims=True)).astype(jnp.bfloat16)
    context = jnp.einsum(
        "nhqk,nhkd->nhqd", attn_probs, arrange(values), preferred_element_type=jnp.float32
    ).astype(jnp.bfloat16)
    context = context.reshape(window_count, head_count, stem_count, WINDOW, head_dim).transpose(
        2, 0, 3, 1, 4
    )
    return context.reshape(stem_count * frame_count, head_count * head_dim)


def generic(
    latent,
    norm1_gain,
    conv1_weight,
    time_bias,
    norm2_gain,
    conv2_weight,
    attn_gain,
    qkv_weight,
    out_weight,
):
    stem_count, frame_count, channels = latent.shape
    tensor_size = lax.axis_size("tensor")
    shard_width = channels // tensor_size
    row_count = stem_count * frame_count
    group_entries = frame_count * lax.axis_size("frame") * (channels // GROUPS)
    latent_f = latent.astype(jnp.float32)
    sums_one, squares_one = group_sums(latent_f, GROUPS)
    sums_one, squares_one = lax.psum((sums_one, squares_one), "frame")
    act_one = jax.nn.silu(
        apply_group(latent_f, sums_one, squares_one, group_entries, norm1_gain)
    ).astype(jnp.bfloat16)
    padded_one = extended(act_one, (("frame", 1),), 1)
    hid_one = conv_padded(padded_one, conv1_weight, frame_count)
    hid_one = hid_one + time_bias
    local_groups = GROUPS // tensor_size
    sums_two, squares_two = group_sums(hid_one, local_groups)
    sums_two, squares_two = lax.psum((sums_two, squares_two), "frame")
    act_two = jax.nn.silu(
        apply_group(hid_one, sums_two, squares_two, group_entries, norm2_gain)
    ).astype(jnp.bfloat16)
    padded_two = extended(act_two, (("frame", 1),), 1)
    conv_term = conv_padded(padded_two, conv2_weight, frame_count)
    own_start = lax.axis_index("tensor") * shard_width
    qkv_flat = qkv_weight.reshape(channels, 3 * shard_width)
    conv_total = lax.psum(conv_term.astype(jnp.bfloat16), "tensor").astype(jnp.float32)
    residual = (latent_f + conv_total).astype(jnp.bfloat16)
    res_f = residual.astype(jnp.float32)
    mean_sq = jnp.mean(res_f * res_f, axis=2, keepdims=True)
    normed = (res_f * lax.rsqrt(mean_sq + rms_eps) * attn_gain).astype(jnp.bfloat16)
    projected = jnp.dot(
        normed.reshape(row_count, channels), qkv_flat, preferred_element_type=jnp.float32
    )
    res_own = lax.dynamic_slice_in_dim(res_f, own_start, shard_width, 2)
    head_local = shard_width // HEAD_DIM
    projected = projected.reshape(stem_count, frame_count, 3, head_local, HEAD_DIM)
    values = projected[:, :, 2].astype(jnp.bfloat16)
    context = attend(projected[:, :, 0], projected[:, :, 1], values)
    out_term = jnp.dot(context, out_weight, preferred_element_type=jnp.float32).reshape(
        stem_count, frame_count, channels
    )
    attn_share = lax.psum_scatter(
        out_term.astype(jnp.bfloat16), "tensor", scatter_dimension=2, tiled=True
    ).astype(jnp.float32)
    velocity = (res_own + attn_share).astype(jnp.bfloat16)
    return velocity


def silu_of_half(half):
    return half + half * jnp.tanh(half)


def one_hot(rows, columns, width, by_row):
    row = lax.broadcasted_iota(jnp.int32, (rows, columns), 0)
    column = lax.broadcasted_iota(jnp.int32, (rows, columns), 1)
    if by_row:
        return (row // width == column).astype(f32)
    return (row == column // width).astype(f32)


def f32_dot(a, b):
    return jnp.dot(a, b, precision=HIGHEST, preferred_element_type=f32)


def even_place():
    return lax.axis_index("frame") % 2 == 0


def group_totals(sums, squares, width):
    hot = one_hot(sums.shape[1], LANES, width, True)
    return f32_dot(sums, hot), f32_dot(squares, hot)


def channel_scale(refs, entries, channels, width):
    total = refs[0]
    for other in refs[1:]:
        total = total + other
    centre = total[:, :LANES] / entries
    spread = total[:, LANES:] / entries - centre * centre
    hot = one_hot(LANES, channels, width, False)
    return f32_dot(centre, hot), f32_dot(lax.rsqrt(spread + norm_eps), hot)


def stats_kernel(width, lat_ref, near_ref, own_ref, sum_ref, square_ref):
    stems, frames, channels = lat_ref.shape
    upward = even_place() == (lax.axis_index("tensor") % 2 == 0)
    for stem in range(stems):
        block = lat_ref[stem].astype(f32)
        sum_ref[stem : stem + 1, :] = jnp.sum(block, axis=0, keepdims=True)
        square_ref[stem : stem + 1, :] = jnp.sum(block * block, axis=0, keepdims=True)
        edge = jnp.where(upward, block[frames - 1 :], block[:1])
        near_ref[stem : stem + 1, :channels] = edge
    sums, squares = group_totals(sum_ref[...], square_ref[...], width)
    for ref, start in ((near_ref, channels), (own_ref, 0)):
        ref[:, start : start + LANES] = sums
        ref[:, start + LANES : start + 2 * LANES] = squares


def pick(value):
    half = value.shape[0] // 2
    return jnp.where(lax.axis_index("tensor") % 2 == 0, value[:half], value[half:])


def both_dots(rows, near, away):
    parts = [jnp.dot(rows, weight, preferred_element_type=f32) for weight in (near, away)]
    return jnp.concatenate(parts, axis=1)


def first_kernel(
    entries, width, frame_size,
    lat_ref, got_ref, swapped_ref, far_ref, own_ref, gain_ref, weight_ref, partner_ref,
    bias_ref, bias_far_ref,
    hid_ref, one_ref, two_ref, tot_ref, act_ref, edge_ref, sum_ref, square_ref,
):
    frames, channels = lat_ref.shape[1:]
    stems, _, span = hid_ref.shape
    place = lax.axis_index("frame")
    core = lax.axis_index("tensor") % 2
    centre, scale = channel_scale(
        [own_ref[...], got_ref[:, channels:], swapped_ref[:, channels:], far_ref[...]],
        entries, channels, width,
    )
    even = even_place()
    first_got = even == (core == 0)
    got, swapped = got_ref[:, :channels], swapped_ref[:, :channels]
    high, low = jnp.where(first_got, got, swapped), jnp.where(first_got, swapped, got)
    scale = scale * (0.5 * gain_ref[...])
    low, high = pick(silu_of_half((low - centre) * scale)), pick(silu_of_half((high - centre) * scale))
    centre, scale = pick(centre), pick(scale)
    edge_ref[...] = jnp.zeros_like(edge_ref)
    edge_ref[0:stems, :] = jnp.where(place > 0, low, 0.0)
    edge_ref[8 : 8 + stems, :] = jnp.where(place < frame_size - 1, high, 0.0)
    edge = edge_ref[...].astype(bf16)
    edge_low = both_dots(edge, weight_ref[0], partner_ref[0])
    edge_high = both_dots(edge, weight_ref[2], partner_ref[2])
    row = lax.broadcasted_iota(jnp.int32, (frames, span), 0)
    bias = jnp.concatenate([bias_ref[...], bias_far_ref[...]], axis=1)
    for stem in range(stems):
        if stem % CHUNK == 0:
            first, last = stem, min(stem + CHUNK, stems)
            for part in range(first, last):
                block = lat_ref[core * stems + part].astype(f32)
                block = (block - centre[part : part + 1]) * scale[part : part + 1]
                act_ref[part * frames : (part + 1) * frames, :] = silu_of_half(block).astype(bf16)
            rows = act_ref[first * frames : last * frames, :]
            taps = [both_dots(rows, weight_ref[tap], partner_ref[tap]) for tap in range(3)]
        lo = (stem - first) * frames
        before = pltpu.roll(taps[0][lo : lo + frames], 1, 0)
        after = pltpu.roll(taps[2][lo : lo + frames], frames - 1, 0)
        before = jnp.where(row == 0, edge_low[stem : stem + 1], before)
        after = jnp.where(row == frames - 1, edge_high[8 + stem : 9 + stem], after)
        hid = taps[1][lo : lo + frames] + before + after + bias
        hid_ref[stem] = hid
        sum_ref[stem : stem + 1, :] = jnp.sum(hid, axis=0, keepdims=True)
        square_ref[stem : stem + 1, :] = jnp.sum(hid * hid, axis=0, keepdims=True)
        down, up = hid[:1], hid[frames - 1 :]
        one_ref[stem : stem + 1, :span] = jnp.where(even, up, down)
        two_ref[stem : stem + 1, :span] = jnp.where(even, down, up)
    sums, squares = group_totals(sum_ref[...], square_ref[...], width)
    for ref, start in ((one_ref, span), (two_ref, span), (tot_ref, 0)):
        ref[:, start : start + LANES] = sums
        ref[:, start + LANES : start + 2 * LANES] = squares


def second_kernel(
    entries, width, frame_size, other,
    hid_ref, one_ref, two_ref, far_ref, own_ref, gain_ref, weight_ref, partner_ref,
    total_ref, act_ref,
):
    stems, _, span = hid_ref.shape
    shard = span // 2
    place = lax.axis_index("frame")
    chip = lax.axis_index("tensor") // 2
    window = 1 - chip if other else chip
    centre, scale = channel_scale(
        [own_ref[...], one_ref[:, span:], two_ref[:, span:], far_ref[...]],
        entries, span, width,
    )
    even = even_place()
    one, two = one_ref[:, :span], two_ref[:, :span]
    high, low = jnp.where(even, one, two), jnp.where(even, two, one)
    scale = scale * (0.5 * gain_ref[...])
    low = jnp.where(place > 0, silu_of_half((low - centre) * scale), 0.0)
    high = jnp.where(place < frame_size - 1, silu_of_half((high - centre) * scale), 0.0)
    row = lax.broadcasted_iota(jnp.int32, (WINDOW, span), 0)
    start = pl.multiple_of(window * WINDOW, WINDOW)
    for stem in range(stems):
        mean, factor = centre[stem : stem + 1], scale[stem : stem + 1]
        act = silu_of_half((hid_ref[stem, pl.ds(start, WINDOW), :] - mean) * factor)
        inner = silu_of_half((hid_ref[stem, WINDOW - 8 : WINDOW + 8, :] - mean) * factor)
        before = jnp.where(window == 0, low[stem : stem + 1], inner[7:8])
        after = jnp.where(window == 0, inner[8:9], high[stem : stem + 1])
        before = jnp.where(row == 0, before, pltpu.roll(act, 1, 0))
        after = jnp.where(row == WINDOW - 1, after, pltpu.roll(act, WINDOW - 1, 0))
        at = slice(stem * WINDOW, (stem + 1) * WINDOW)
        for tap, value in enumerate((before, act, after)):
            value = value.astype(bf16)
            act_ref[at, tap * shard : (tap + 1) * shard] = value[:, :shard]
            act_ref[at, (3 + tap) * shard : (4 + tap) * shard] = value[:, shard:]
    total = jnp.dot(act_ref[:, : 3 * shard], weight_ref[...], preferred_element_type=f32)
    total = total + jnp.dot(
        act_ref[:, 3 * shard :], partner_ref[...], preferred_element_type=f32
    )
    total_ref[...] = total.astype(total_ref.dtype)


def split2(value):
    high = value.astype(bf16)
    return high, (value - high.astype(f32)).astype(bf16)


def normed_rows(res, gain_ref):
    mean_sq = jnp.mean(res * res, axis=1, keepdims=True)
    return (res * lax.rsqrt(mean_sq + rms_eps) * gain_ref[...]).astype(bf16)


def projector(normed_ref, qkv_ref, first_x_ref, first_y_ref, q_x_ref, q_z_ref, v_refs=()):
    depth = normed_ref.shape[1] // 2
    group, parity = lax.axis_index("groups"), lax.axis_index("frame") % 2

    def half(place):
        return normed_ref[:, pl.ds(pl.multiple_of(place * depth, depth), depth)]

    def project(side, which):
        if side == 0:
            return jnp.dot(normed_ref[...], qkv_ref[which], preferred_element_type=f32)
        if which == 0:
            place, near, away = parity, q_x_ref[...], q_z_ref[...]
        elif which == 1:
            place, near, away = group, first_x_ref[:depth, :], first_y_ref[:depth, :]
        else:
            place, near, away = group, v_refs[0][...], v_refs[1][...]
        value = jnp.dot(half(place), near, preferred_element_type=f32)
        return value + jnp.dot(half(1 - place), away, preferred_element_type=f32)

    return project


def project_kernel(
    mine_ref, gain_ref, qkv_ref, first_x_ref, first_y_ref, q_x_ref, q_z_ref,
    queries_ref, keys_ref, normed_ref,
):
    shard = qkv_ref.shape[2]
    normed_ref[...] = normed_rows(mine_ref[...].astype(f32), gain_ref)
    project = projector(normed_ref, qkv_ref, first_x_ref, first_y_ref, q_x_ref, q_z_ref)
    for side in range(2):
        at = slice(side * shard, (side + 1) * shard)
        queries_ref[:, at] = project(side, 0)
        keys_ref[:, at] = project(side, 1)


def attention_kernel(
    theirs_ref, gain_ref, qkv_ref, first_x_ref, first_y_ref, q_x_ref, q_z_ref, v_x_ref, v_y_ref,
    queries_ref, keys_ref, mine_ref,
    context_ref, normed_ref,
):
    rows = theirs_ref.shape[0]
    shard = qkv_ref.shape[2]
    normed_ref[:rows, :] = mine_ref[...]
    normed_ref[rows:, :] = normed_rows(theirs_ref[...].astype(f32), gain_ref)
    weights = qkv_ref, first_x_ref, first_y_ref, q_x_ref, q_z_ref
    project = projector(normed_ref.at[pl.ds(rows, rows), :], *weights)
    project_all = projector(normed_ref, *weights, (v_x_ref, v_y_ref))
    lane = lax.broadcasted_iota(jnp.int32, (2 * rows, LANES), 1)
    nt = (((1,), (1,)), ((), ()))
    for side in range(2):
        span = slice(side * shard, (side + 1) * shard)
        queries, keys = [
            jnp.concatenate([ref[:, span], project(side, which)], axis=0)
            for which, ref in enumerate((queries_ref, keys_ref))
        ]
        values = project_all(side, 2)
        queries = queries * (1.0 / math.sqrt(HEAD_DIM))
        for tile in range(shard // LANES):
            at = slice(tile * LANES, (tile + 1) * LANES)
            q_high, q_low = split2(queries[:, at])
            q_low = pltpu.roll(q_low.astype(f32), HEAD_DIM, 1).astype(bf16)
            k_high, k_low = split2(keys[:, at])
            k_rolled = split2(pltpu.roll(keys[:, at], HEAD_DIM, 1))
            terms, mixing = [], []
            for head in range(LANES // HEAD_DIM):
                inside = lane // HEAD_DIM == head
                left = jnp.where(inside, q_high, q_low)
                left = jnp.concatenate([left, left], axis=1)
                right = [
                    jnp.where(inside, own, rolled)
                    for own, rolled in zip((k_high, k_low), k_rolled)
                ]
                right = jnp.concatenate(right, axis=1)
                scores = lax.dot_general(left, right, nt, preferred_element_type=f32)
                scores = jnp.exp(scores - jnp.max(scores, axis=1, keepdims=True))
                terms.append(scores.astype(bf16))
                mixing.append(
                    jnp.concatenate(
                        [jnp.where(inside, values[:, at], 0.0), jnp.where(inside, 1.0, 0.0)], axis=1
                    ).astype(bf16)
                )
            mixed = jnp.dot(
                jnp.concatenate(terms, axis=1), jnp.concatenate(mixing, axis=0),
                preferred_element_type=f32,
            )
            base = side * shard + tile * LANES
            context_ref[:, base : base + LANES] = (mixed[:, :LANES] / mixed[:, LANES:]).astype(bf16)


def output_kernel(
    context_ref, mine_ref, theirs_ref, out_ref, first_x_ref, first_y_ref, out_z_ref,
    send_far_ref, keep_far_ref, send_near_ref, keep_near_ref,
    out_far_ref,
):
    rows, channels = mine_ref.shape
    shard = out_ref.shape[0]
    index = lax.axis_index("tensor")
    chip, core = index // 2, index % 2
    depth = channels // 2
    group, parity = lax.axis_index("groups"), lax.axis_index("frame") % 2
    out_far_ref[2 * group + parity] = first_x_ref[depth:, :]
    out_far_ref[2 * (1 - group) + parity] = first_y_ref[depth:, :]
    out_far_ref[2 * group + 1 - parity] = out_z_ref[0]
    out_far_ref[2 * (1 - group) + 1 - parity] = out_z_ref[1]

    def term(block):
        at = pl.ds(pl.multiple_of(block * shard, shard), shard)
        value = jnp.dot(context_ref[:, :shard], out_ref[:, at], preferred_element_type=f32)
        far = jnp.dot(context_ref[:, shard:], out_far_ref[block], preferred_element_type=f32)
        return value + far

    sides = ((1 - chip, send_far_ref, keep_far_ref), (chip, send_near_ref, keep_near_ref))
    for goal, send_ref, keep_ref in sides:
        value = term(2 * goal + 1 - core).astype(bf16)
        send_ref[:rows, :] = value[rows:]
        send_ref[rows:, :] = value[:rows]
        block = 2 * goal + core
        at = pl.ds(pl.multiple_of(block * shard, shard), shard)
        value = term(block)
        keep_ref[:rows, :] = value[:rows] + mine_ref[:, at].astype(f32)
        keep_ref[rows:, :] = value[rows:] + theirs_ref[:, at].astype(f32)


def run_copies(pairs, sems):
    copies = [
        pltpu.make_async_copy(source, goal, sems.at[place])
        for place, (source, goal) in enumerate(pairs)
    ]
    for copy in copies:
        copy.start()
    for copy in copies:
        copy.wait()


def row_pieces(place, depth):
    step = depth // PIECES
    for piece in range(PIECES):
        start = pl.multiple_of(place * depth + piece * step, step)
        yield pl.ds(start, step), pl.ds(piece * step, step)


def pack_first_kernel(qkv_ref, out_ref, send_ref, sems):
    depth, shard = qkv_ref.shape[1] // 2, qkv_ref.shape[2]
    group, parity = lax.axis_index("groups"), lax.axis_index("frame") % 2
    pairs = []
    for which, place, base in ((1, group, 0), (0, parity, depth + shard)):
        for rows, goal in row_pieces(place, depth):
            pairs.append((qkv_ref.at[which, rows, :], send_ref.at[pl.ds(base + goal.start, goal.size), :]))
    block = pl.ds(pl.multiple_of((2 * group + parity) * shard, shard), shard)
    for piece in range(2):
        rows = pl.ds(piece * shard // 2, shard // 2)
        goal = pl.ds(depth + piece * shard // 2, shard // 2)
        pairs.append((out_ref.at[rows, block], send_ref.at[goal, :]))
    run_copies(pairs, sems)


def pack_rest_kernel(qkv_ref, values_ref, sems):
    pairs = [
        (qkv_ref.at[2, rows, :], values_ref.at[goal, :])
        for rows, goal in row_pieces(lax.axis_index("groups"), values_ref.shape[0])
    ]
    run_copies(pairs, sems)


def pack(kernel, shapes, copies, args):
    return pl.pallas_call(
        kernel,
        out_shape=[jax.ShapeDtypeStruct(shape, bf16) for shape in shapes],
        in_specs=[pl.BlockSpec(memory_space=pltpu.HBM)] * len(args),
        out_specs=[pl.BlockSpec(memory_space=VMEM)] * len(shapes),
        scratch_shapes=[pltpu.SemaphoreType.DMA((copies,))],
        compiler_params=pltpu.CompilerParams(vmem_limit_bytes=4 * 2**20),
        cost_estimate=pl.CostEstimate(flops=0, bytes_accessed=2**20, transcendentals=0),
    )(*[pltpu.with_memory_space_constraint(arg, pltpu.HBM) for arg in args])


def residual_kernel(latent_ref, keep_ref, far_ref, out_ref):
    stems = latent_ref.shape[0]
    index = lax.axis_index("tensor")
    chip, core = index // 2, index % 2
    start = pl.multiple_of(chip * WINDOW, WINDOW)
    for stem in range(stems // 2):
        rows = slice(stem * WINDOW, (stem + 1) * WINDOW)
        total = keep_ref[rows, :] + far_ref[rows, :].astype(f32)
        latent = latent_ref[core * (stems // 2) + stem, pl.ds(start, WINDOW), :]
        out_ref[rows, :] = (latent.astype(f32) + total).astype(bf16)


def place(value_ref, out_ref, window, sems):
    stems = out_ref.shape[0]
    core = lax.axis_index("tensor") % 2
    half = stems // 2
    at = pl.ds(pl.multiple_of(window * WINDOW, WINDOW), WINDOW)
    pairs = []
    for stem in range(stems):
        goal = (core if stem < half else 1 - core) * half + stem % half
        source = value_ref.at[pl.ds(stem * WINDOW, WINDOW), :]
        pairs.append((source, out_ref.at[goal, at, :]))
    run_copies(pairs, sems)


def place_near_kernel(keep_ref, got_ref, out_ref, value_ref, sems):
    value_ref[...] = (keep_ref[...] + got_ref[...].astype(f32)).astype(bf16)
    place(value_ref, out_ref, lax.axis_index("tensor") // 2, sems)


def place_far_kernel(value_ref, near_ref, out_ref, sems):
    del near_ref
    place(value_ref, out_ref, 1 - lax.axis_index("tensor") // 2, sems)


def call(kernel, outs, scratch, args, flops=0, moved=0, limit=16):
    return pl.pallas_call(
        kernel,
        out_shape=[jax.ShapeDtypeStruct(shape, dtype) for shape, dtype in outs],
        in_specs=[pl.BlockSpec(memory_space=VMEM)] * len(args),
        out_specs=[pl.BlockSpec(memory_space=VMEM)] * len(outs),
        scratch_shapes=[VMEM(shape, dtype) for shape, dtype in scratch],
        compiler_params=pltpu.CompilerParams(vmem_limit_bytes=limit * 2**20),
        cost_estimate=pl.CostEstimate(flops=flops, bytes_accessed=moved, transcendentals=0),
    )(*args)


def swap_cores(value):
    return lax.ppermute(value, "tensor", [(0, 1), (1, 0), (2, 3), (3, 2)])


def swap_chips(value):
    return lax.ppermute(value, "tensor", [(0, 2), (2, 0), (1, 3), (3, 1)])


def swap_groups(value):
    return lax.ppermute(value, "groups", [(0, 1), (1, 0)])


ONE = ((0, 1), (1, 0), (2, 3), (3, 2))
TWO = ((0, 3), (3, 0), (1, 2), (2, 1))
FAR = ((0, 2), (2, 0), (1, 3), (3, 1))


def trade(value, pairs):
    return lax.ppermute(value, "frame", pairs)


def trade_by_core(value):
    count = lax.axis_size("tensor")
    pairs = [
        (source * count + index, goal * count + index)
        for index in range(count)
        for source, goal in (TWO if index % 2 else ONE)
    ]
    return lax.ppermute(value, ("frame", "tensor"), pairs)


def fast(
    latent, norm1_gain, conv1_weight, time_bias, norm2_gain, conv2_weight,
    attn_gain, qkv_weight, out_weight,
):
    stems, frames, channels = latent.shape
    frame_size = lax.axis_size("frame")
    shard = conv1_weight.shape[2]
    width = channels // GROUPS
    entries = frames * frame_size * width
    half_rows = stems // 2 * WINDOW
    qkv = jnp.transpose(qkv_weight, (1, 0, 2))
    depth = channels // 2
    (first,) = pack(
        pack_first_kernel, [(2 * depth + shard, shard)], 2 * PIECES + 2,
        [qkv, out_weight],
    )
    (values,) = pack(pack_rest_kernel, [(depth, shard)], PIECES, [qkv])
    first_x = swap_chips(first)
    v_x = swap_chips(values)
    first_x, q_x = first_x[: depth + shard], first_x[depth + shard :]
    first_y = swap_groups(first_x)
    q_z = trade(q_x, ONE)
    v_y = swap_groups(v_x)
    out_z = trade(jnp.stack([first_x[depth:], first_y[depth:]]), ONE)
    weight1 = swap_cores(conv1_weight)
    weight2 = swap_cores(conv2_weight).reshape(3 * shard, channels)
    bias_far = swap_cores(time_bias)
    gain_far = swap_cores(norm2_gain)
    gain2 = jnp.concatenate([norm2_gain, gain_far])[None]
    wide = channels + 2 * LANES
    near, own = call(
        functools.partial(stats_kernel, width),
        [((stems, wide), f32), ((stems, 2 * LANES), f32)],
        [((stems, channels), f32)] * 2,
        [latent],
    )
    far = trade(own, FAR)
    got = trade_by_core(near)
    swapped = swap_cores(got)
    half, span = stems // 2, 2 * shard
    narrow = span + 2 * LANES
    hid, one2, two2, own2 = call(
        functools.partial(first_kernel, entries, width, frame_size),
        [((half, frames, span), f32), ((half, narrow), f32), ((half, narrow), f32),
         ((half, 2 * LANES), f32)],
        [((half * frames, channels), bf16), ((16, channels), f32)] + [((half, span), f32)] * 2,
        [latent, got, swapped, far, own, norm1_gain[None], conv1_weight, weight1,
         time_bias[None], bias_far[None]],
        flops=6 * stems * frames * channels * shard, limit=24,
    )
    far2 = trade(own2, FAR)
    got_two = trade(two2, TWO)
    got_one = trade(one2, ONE)

    def second(other):
        return call(
            functools.partial(second_kernel, entries, width, frame_size, other),
            [((half_rows, channels), bf16 if other else f32)],
            [((half_rows, 6 * shard), bf16)],
            [hid, got_one, got_two, far2, own2, gain2,
             conv2_weight.reshape(3 * shard, channels), weight2],
            flops=12 * half_rows * channels * shard,
        )[0]

    summed = swap_chips(second(True))
    mine = call(
        residual_kernel, [((half_rows, channels), bf16)], [],
        [latent, second(False), summed],
    )[0]
    theirs = swap_cores(mine)
    weights = [attn_gain[None], qkv, first_x, first_y, q_x, q_z]
    projected = call(
        project_kernel,
        [((half_rows, 2 * shard), f32)] * 2 + [((half_rows, channels), bf16)], [],
        [mine, *weights],
        flops=8 * half_rows * channels * shard,
    )
    context = call(
        attention_kernel, [((2 * half_rows, 2 * shard), bf16)],
        [((2 * half_rows, channels), bf16)],
        [theirs, *weights, v_x, v_y, *projected],
        flops=24 * half_rows * channels * shard, limit=24,
    )[0]
    send_far, keep_far, send_near, keep_near = call(
        output_kernel,
        [((2 * half_rows, shard), bf16), ((2 * half_rows, shard), f32)] * 2,
        [((4, shard, shard), bf16)],
        [context, mine, theirs, out_weight, first_x, first_y, out_z],
        flops=8 * half_rows * channels * shard,
    )
    got_far = swap_cores(send_far)
    got_near = swap_cores(send_near)
    away = (keep_far + got_far.astype(f32)).astype(bf16)
    arrived = swap_chips(away)
    vmem, anywhere = pl.BlockSpec(memory_space=VMEM), pl.BlockSpec(memory_space=pl.ANY)
    shape = jax.ShapeDtypeStruct((stems, frames, shard), bf16)
    sems = pltpu.SemaphoreType.DMA((stems,))
    params = pltpu.CompilerParams(vmem_limit_bytes=4 * 2**20)
    near = pl.pallas_call(
        place_near_kernel, name="place_near", out_shape=shape,
        in_specs=[vmem, vmem], out_specs=anywhere, compiler_params=params,
        scratch_shapes=[VMEM((2 * half_rows, shard), bf16), sems],
    )(keep_near, got_near)
    return pl.pallas_call(
        place_far_kernel, name="place_far", out_shape=shape,
        in_specs=[vmem, anywhere], out_specs=anywhere, compiler_params=params,
        scratch_shapes=[sems], input_output_aliases={1: 0},
    )(arrived, near)


def local(*args):
    latent = args[0]
    stems, frames, channels = latent.shape
    tensor_size, frame_size = lax.axis_size("tensor"), lax.axis_size("frame")
    shard = channels // tensor_size
    suits = (
        tensor_size == 4
        and frame_size == 4
        and lax.axis_size("groups") == 2
        and frames == 2 * WINDOW
        and stems % 2 == 0
        and stems <= 8
        and shard % (2 * LANES) == 0
    )
    if not suits:
        return generic(*args)
    return fast(*args)


def solution(mesh):
    return jax.shard_map(
        local,
        mesh=mesh,
        in_specs=(
            P(None, ("groups", "frame"), None),
            P(),
            P(None, None, "tensor"),
            P("tensor"),
            P("tensor"),
            P(None, "tensor", None),
            P(),
            P(None, None, "tensor"),
            P("tensor", None),
        ),
        out_specs=P(None, ("groups", "frame"), "tensor"),
        check_vma=False,
    )
```

```python
import functools
import math

import jax
import jax.numpy as jnp
from jax import lax
from jax.experimental import pallas as pl
from jax.experimental.pallas import tpu as pltpu
from jax.sharding import PartitionSpec as P


TENSOR, FRAME, SONGS = "tensor", "frame", "groups"
GROUPS = 32
HEAD_DIM = 64
WINDOW = 64
LANES = 128
PIECES = 4
CHUNK = 2

norm_eps = 1e-05
rms_eps = 1e-06
HIGHEST = lax.Precision.HIGHEST
VMEM = pltpu.VMEM
bf16 = jnp.bfloat16
f32 = jnp.float32


def extended(block, sides, width):
    for axis, dim in sides:
        count = lax.axis_size(axis)
        forward = [(i, i + 1) for i in range(count - 1)]
        backward = [(target, source) for source, target in forward]
        low = lax.ppermute(
            lax.slice_in_dim(block, block.shape[dim] - width, None, axis=dim), axis, forward
        )
        high = lax.ppermute(lax.slice_in_dim(block, 0, width, axis=dim), axis, backward)
        block = jnp.concatenate([low, block, high], axis=dim)
    return block


def group_sums(hidden, group_count):
    stem_count, frame_count, channels = hidden.shape
    grouped = hidden.reshape(stem_count, frame_count, group_count, channels // group_count)
    return (jnp.sum(grouped, axis=(1, 3)), jnp.sum(grouped * grouped, axis=(1, 3)))


def apply_group(hidden, totals, squares, entries, gain_vec):
    stem_count, frame_count, channels = hidden.shape
    group_count = totals.shape[1]
    centre = totals / entries
    spread = squares / entries - centre * centre
    grouped = hidden.reshape(stem_count, frame_count, group_count, channels // group_count)
    scaled = (grouped - centre[:, None, :, None]) * lax.rsqrt(spread + norm_eps)[:, None, :, None]
    return scaled.reshape(stem_count, frame_count, channels) * gain_vec


def conv_padded(padded, kernel, frame_count):
    stem_count = padded.shape[0]
    channels = padded.shape[2]
    result = jnp.zeros((stem_count * frame_count, kernel.shape[2]), jnp.float32)
    for tap_index in range(3):
        tap_rows = padded[:, tap_index : tap_index + frame_count].reshape(
            stem_count * frame_count, channels
        )
        result = result + jnp.dot(tap_rows, kernel[tap_index], preferred_element_type=jnp.float32)
    return result.reshape(stem_count, frame_count, kernel.shape[2])


def attend(queries, keys_all, values):
    stem_count, frame_count, head_count, head_dim = queries.shape
    window_count = frame_count // WINDOW

    def arrange(source):
        shaped = source.reshape(stem_count, window_count, WINDOW, head_count, head_dim)
        return shaped.transpose(1, 3, 0, 2, 4).reshape(
            window_count, head_count, stem_count * WINDOW, head_dim
        )

    scores = jnp.einsum(
        "nhqd,nhkd->nhqk",
        arrange(queries),
        arrange(keys_all),
        precision=lax.Precision.HIGHEST,
        preferred_element_type=jnp.float32,
    ) / math.sqrt(head_dim)
    scores = scores - jnp.max(scores, axis=3, keepdims=True)
    exp_scores = jnp.exp(scores)
    attn_probs = (exp_scores / jnp.sum(exp_scores, axis=3, keepdims=True)).astype(jnp.bfloat16)
    context = jnp.einsum(
        "nhqk,nhkd->nhqd", attn_probs, arrange(values), preferred_element_type=jnp.float32
    ).astype(jnp.bfloat16)
    context = context.reshape(window_count, head_count, stem_count, WINDOW, head_dim).transpose(
        2, 0, 3, 1, 4
    )
    return context.reshape(stem_count * frame_count, head_count * head_dim)


def generic(
    latent,
    norm1_gain,
    conv1_weight,
    time_bias,
    norm2_gain,
    conv2_weight,
    attn_gain,
    qkv_weight,
    out_weight,
):
    stem_count, frame_count, channels = latent.shape
    tensor_size = lax.axis_size(TENSOR)
    shard_width = channels // tensor_size
    row_count = stem_count * frame_count
    group_entries = frame_count * lax.axis_size(FRAME) * (channels // GROUPS)
    latent_f = latent.astype(jnp.float32)
    sums_one, squares_one = group_sums(latent_f, GROUPS)
    sums_one, squares_one = lax.psum((sums_one, squares_one), FRAME)
    act_one = jax.nn.silu(
        apply_group(latent_f, sums_one, squares_one, group_entries, norm1_gain)
    ).astype(jnp.bfloat16)
    padded_one = extended(act_one, ((FRAME, 1),), 1)
    hid_one = conv_padded(padded_one, conv1_weight, frame_count)
    hid_one = hid_one + time_bias
    local_groups = GROUPS // tensor_size
    sums_two, squares_two = group_sums(hid_one, local_groups)
    sums_two, squares_two = lax.psum((sums_two, squares_two), FRAME)
    act_two = jax.nn.silu(
        apply_group(hid_one, sums_two, squares_two, group_entries, norm2_gain)
    ).astype(jnp.bfloat16)
    padded_two = extended(act_two, ((FRAME, 1),), 1)
    conv_term = conv_padded(padded_two, conv2_weight, frame_count)
    own_start = lax.axis_index(TENSOR) * shard_width
    qkv_flat = qkv_weight.reshape(channels, 3 * shard_width)
    conv_total = lax.psum(conv_term.astype(jnp.bfloat16), TENSOR).astype(jnp.float32)
    residual = (latent_f + conv_total).astype(jnp.bfloat16)
    res_f = residual.astype(jnp.float32)
    mean_sq = jnp.mean(res_f * res_f, axis=2, keepdims=True)
    normed = (res_f * lax.rsqrt(mean_sq + rms_eps) * attn_gain).astype(jnp.bfloat16)
    projected = jnp.dot(
        normed.reshape(row_count, channels), qkv_flat, preferred_element_type=jnp.float32
    )
    res_own = lax.dynamic_slice_in_dim(res_f, own_start, shard_width, 2)
    head_local = shard_width // HEAD_DIM
    projected = projected.reshape(stem_count, frame_count, 3, head_local, HEAD_DIM)
    values = projected[:, :, 2].astype(jnp.bfloat16)
    context = attend(projected[:, :, 0], projected[:, :, 1], values)
    out_term = jnp.dot(context, out_weight, preferred_element_type=jnp.float32).reshape(
        stem_count, frame_count, channels
    )
    attn_share = lax.psum_scatter(
        out_term.astype(jnp.bfloat16), TENSOR, scatter_dimension=2, tiled=True
    ).astype(jnp.float32)
    velocity = (res_own + attn_share).astype(jnp.bfloat16)
    return velocity


def silu_of_half(half):
    return half + half * jnp.tanh(half)


def one_hot(rows, columns, width, by_row):
    row = lax.broadcasted_iota(jnp.int32, (rows, columns), 0)
    column = lax.broadcasted_iota(jnp.int32, (rows, columns), 1)
    if by_row:
        return (row // width == column).astype(f32)
    return (row == column // width).astype(f32)


def f32_dot(a, b):
    return jnp.dot(a, b, precision=HIGHEST, preferred_element_type=f32)


def even_place():
    return lax.axis_index(FRAME) % 2 == 0


def group_totals(sums, squares, width):
    hot = one_hot(sums.shape[1], LANES, width, True)
    return f32_dot(sums, hot), f32_dot(squares, hot)


def channel_scale(refs, entries, channels, width):
    total = refs[0]
    for other in refs[1:]:
        total = total + other
    centre = total[:, :LANES] / entries
    spread = total[:, LANES:] / entries - centre * centre
    hot = one_hot(LANES, channels, width, False)
    return f32_dot(centre, hot), f32_dot(lax.rsqrt(spread + norm_eps), hot)


def stats_kernel(width, lat_ref, near_ref, own_ref, sum_ref, square_ref):
    stems, frames, channels = lat_ref.shape
    upward = even_place() == (lax.axis_index(TENSOR) % 2 == 0)
    for stem in range(stems):
        block = lat_ref[stem].astype(f32)
        sum_ref[stem : stem + 1, :] = jnp.sum(block, axis=0, keepdims=True)
        square_ref[stem : stem + 1, :] = jnp.sum(block * block, axis=0, keepdims=True)
        edge = jnp.where(upward, block[frames - 1 :], block[:1])
        near_ref[stem : stem + 1, :channels] = edge
    sums, squares = group_totals(sum_ref[...], square_ref[...], width)
    for ref, start in ((near_ref, channels), (own_ref, 0)):
        ref[:, start : start + LANES] = sums
        ref[:, start + LANES : start + 2 * LANES] = squares


def pick(value):
    half = value.shape[0] // 2
    return jnp.where(lax.axis_index(TENSOR) % 2 == 0, value[:half], value[half:])


def both_dots(rows, near, away):
    parts = [jnp.dot(rows, weight, preferred_element_type=f32) for weight in (near, away)]
    return jnp.concatenate(parts, axis=1)


def first_kernel(
    entries, width, frame_size,
    lat_ref, got_ref, swapped_ref, far_ref, own_ref, gain_ref, weight_ref, partner_ref,
    bias_ref, bias_far_ref,
    hid_ref, one_ref, two_ref, tot_ref, act_ref, edge_ref, sum_ref, square_ref,
):
    frames, channels = lat_ref.shape[1:]
    stems, _, span = hid_ref.shape
    place = lax.axis_index(FRAME)
    core = lax.axis_index(TENSOR) % 2
    centre, scale = channel_scale(
        [own_ref[...], got_ref[:, channels:], swapped_ref[:, channels:], far_ref[...]],
        entries, channels, width,
    )
    even = even_place()
    first_got = even == (core == 0)
    got, swapped = got_ref[:, :channels], swapped_ref[:, :channels]
    high, low = jnp.where(first_got, got, swapped), jnp.where(first_got, swapped, got)
    scale = scale * (0.5 * gain_ref[...])
    low, high = pick(silu_of_half((low - centre) * scale)), pick(silu_of_half((high - centre) * scale))
    centre, scale = pick(centre), pick(scale)
    edge_ref[...] = jnp.zeros_like(edge_ref)
    edge_ref[0:stems, :] = jnp.where(place > 0, low, 0.0)
    edge_ref[8 : 8 + stems, :] = jnp.where(place < frame_size - 1, high, 0.0)
    edge = edge_ref[...].astype(bf16)
    edge_low = both_dots(edge, weight_ref[0], partner_ref[0])
    edge_high = both_dots(edge, weight_ref[2], partner_ref[2])
    row = lax.broadcasted_iota(jnp.int32, (frames, span), 0)
    bias = jnp.concatenate([bias_ref[...], bias_far_ref[...]], axis=1)
    for stem in range(stems):
        if stem % CHUNK == 0:
            first, last = stem, min(stem + CHUNK, stems)
            for part in range(first, last):
                block = lat_ref[core * stems + part].astype(f32)
                block = (block - centre[part : part + 1]) * scale[part : part + 1]
                act_ref[part * frames : (part + 1) * frames, :] = silu_of_half(block).astype(bf16)
            rows = act_ref[first * frames : last * frames, :]
            taps = [both_dots(rows, weight_ref[tap], partner_ref[tap]) for tap in range(3)]
        lo = (stem - first) * frames
        before = pltpu.roll(taps[0][lo : lo + frames], 1, 0)
        after = pltpu.roll(taps[2][lo : lo + frames], frames - 1, 0)
        before = jnp.where(row == 0, edge_low[stem : stem + 1], before)
        after = jnp.where(row == frames - 1, edge_high[8 + stem : 9 + stem], after)
        hid = taps[1][lo : lo + frames] + before + after + bias
        hid_ref[stem] = hid
        sum_ref[stem : stem + 1, :] = jnp.sum(hid, axis=0, keepdims=True)
        square_ref[stem : stem + 1, :] = jnp.sum(hid * hid, axis=0, keepdims=True)
        down, up = hid[:1], hid[frames - 1 :]
        one_ref[stem : stem + 1, :span] = jnp.where(even, up, down)
        two_ref[stem : stem + 1, :span] = jnp.where(even, down, up)
    sums, squares = group_totals(sum_ref[...], square_ref[...], width)
    for ref, start in ((one_ref, span), (two_ref, span), (tot_ref, 0)):
        ref[:, start : start + LANES] = sums
        ref[:, start + LANES : start + 2 * LANES] = squares


def second_kernel(
    entries, width, frame_size, other,
    hid_ref, one_ref, two_ref, far_ref, own_ref, gain_ref, weight_ref, partner_ref,
    total_ref, act_ref,
):
    stems, _, span = hid_ref.shape
    shard = span // 2
    place = lax.axis_index(FRAME)
    chip = lax.axis_index(TENSOR) // 2
    window = 1 - chip if other else chip
    centre, scale = channel_scale(
        [own_ref[...], one_ref[:, span:], two_ref[:, span:], far_ref[...]],
        entries, span, width,
    )
    even = even_place()
    one, two = one_ref[:, :span], two_ref[:, :span]
    high, low = jnp.where(even, one, two), jnp.where(even, two, one)
    scale = scale * (0.5 * gain_ref[...])
    low = jnp.where(place > 0, silu_of_half((low - centre) * scale), 0.0)
    high = jnp.where(place < frame_size - 1, silu_of_half((high - centre) * scale), 0.0)
    row = lax.broadcasted_iota(jnp.int32, (WINDOW, span), 0)
    start = pl.multiple_of(window * WINDOW, WINDOW)
    for stem in range(stems):
        mean, factor = centre[stem : stem + 1], scale[stem : stem + 1]
        act = silu_of_half((hid_ref[stem, pl.ds(start, WINDOW), :] - mean) * factor)
        inner = silu_of_half((hid_ref[stem, WINDOW - 8 : WINDOW + 8, :] - mean) * factor)
        before = jnp.where(window == 0, low[stem : stem + 1], inner[7:8])
        after = jnp.where(window == 0, inner[8:9], high[stem : stem + 1])
        before = jnp.where(row == 0, before, pltpu.roll(act, 1, 0))
        after = jnp.where(row == WINDOW - 1, after, pltpu.roll(act, WINDOW - 1, 0))
        at = slice(stem * WINDOW, (stem + 1) * WINDOW)
        for tap, value in enumerate((before, act, after)):
            value = value.astype(bf16)
            act_ref[at, tap * shard : (tap + 1) * shard] = value[:, :shard]
            act_ref[at, (3 + tap) * shard : (4 + tap) * shard] = value[:, shard:]
    total = jnp.dot(act_ref[:, : 3 * shard], weight_ref[...], preferred_element_type=f32)
    total = total + jnp.dot(
        act_ref[:, 3 * shard :], partner_ref[...], preferred_element_type=f32
    )
    total_ref[...] = total.astype(total_ref.dtype)


def split2(value):
    high = value.astype(bf16)
    return high, (value - high.astype(f32)).astype(bf16)


def normed_rows(res, gain_ref):
    mean_sq = jnp.mean(res * res, axis=1, keepdims=True)
    return (res * lax.rsqrt(mean_sq + rms_eps) * gain_ref[...]).astype(bf16)


def projector(normed_ref, qkv_ref, first_x_ref, first_y_ref, q_x_ref, q_z_ref, v_refs=()):
    depth = normed_ref.shape[1] // 2
    group, parity = lax.axis_index(SONGS), lax.axis_index(FRAME) % 2

    def half(place):
        return normed_ref[:, pl.ds(pl.multiple_of(place * depth, depth), depth)]

    def project(side, which):
        if side == 0:
            return jnp.dot(normed_ref[...], qkv_ref[which], preferred_element_type=f32)
        if which == 0:
            place, near, away = parity, q_x_ref[...], q_z_ref[...]
        elif which == 1:
            place, near, away = group, first_x_ref[:depth, :], first_y_ref[:depth, :]
        else:
            place, near, away = group, v_refs[0][...], v_refs[1][...]
        value = jnp.dot(half(place), near, preferred_element_type=f32)
        return value + jnp.dot(half(1 - place), away, preferred_element_type=f32)

    return project


def project_kernel(
    mine_ref, gain_ref, qkv_ref, first_x_ref, first_y_ref, q_x_ref, q_z_ref,
    queries_ref, keys_ref, normed_ref,
):
    shard = qkv_ref.shape[2]
    normed_ref[...] = normed_rows(mine_ref[...].astype(f32), gain_ref)
    project = projector(normed_ref, qkv_ref, first_x_ref, first_y_ref, q_x_ref, q_z_ref)
    for side in range(2):
        at = slice(side * shard, (side + 1) * shard)
        queries_ref[:, at] = project(side, 0)
        keys_ref[:, at] = project(side, 1)


def attention_kernel(
    theirs_ref, gain_ref, qkv_ref, first_x_ref, first_y_ref, q_x_ref, q_z_ref, v_x_ref, v_y_ref,
    queries_ref, keys_ref, mine_ref,
    context_ref, normed_ref,
):
    rows = theirs_ref.shape[0]
    shard = qkv_ref.shape[2]
    normed_ref[:rows, :] = mine_ref[...]
    normed_ref[rows:, :] = normed_rows(theirs_ref[...].astype(f32), gain_ref)
    weights = qkv_ref, first_x_ref, first_y_ref, q_x_ref, q_z_ref
    project = projector(normed_ref.at[pl.ds(rows, rows), :], *weights)
    project_all = projector(normed_ref, *weights, (v_x_ref, v_y_ref))
    lane = lax.broadcasted_iota(jnp.int32, (2 * rows, LANES), 1)
    nt = (((1,), (1,)), ((), ()))
    for side in range(2):
        span = slice(side * shard, (side + 1) * shard)
        queries, keys = [
            jnp.concatenate([ref[:, span], project(side, which)], axis=0)
            for which, ref in enumerate((queries_ref, keys_ref))
        ]
        values = project_all(side, 2)
        queries = queries * (1.0 / math.sqrt(HEAD_DIM))
        for tile in range(shard // LANES):
            at = slice(tile * LANES, (tile + 1) * LANES)
            q_high, q_low = split2(queries[:, at])
            q_low = pltpu.roll(q_low.astype(f32), HEAD_DIM, 1).astype(bf16)
            k_high, k_low = split2(keys[:, at])
            k_rolled = split2(pltpu.roll(keys[:, at], HEAD_DIM, 1))
            terms, mixing = [], []
            for head in range(LANES // HEAD_DIM):
                inside = lane // HEAD_DIM == head
                left = jnp.where(inside, q_high, q_low)
                left = jnp.concatenate([left, left], axis=1)
                right = [
                    jnp.where(inside, own, rolled)
                    for own, rolled in zip((k_high, k_low), k_rolled)
                ]
                right = jnp.concatenate(right, axis=1)
                scores = lax.dot_general(left, right, nt, preferred_element_type=f32)
                scores = jnp.exp(scores - jnp.max(scores, axis=1, keepdims=True))
                terms.append(scores.astype(bf16))
                mixing.append(
                    jnp.concatenate(
                        [jnp.where(inside, values[:, at], 0.0), jnp.where(inside, 1.0, 0.0)], axis=1
                    ).astype(bf16)
                )
            mixed = jnp.dot(
                jnp.concatenate(terms, axis=1), jnp.concatenate(mixing, axis=0),
                preferred_element_type=f32,
            )
            base = side * shard + tile * LANES
            context_ref[:, base : base + LANES] = (mixed[:, :LANES] / mixed[:, LANES:]).astype(bf16)


def output_kernel(
    context_ref, mine_ref, theirs_ref, out_ref, first_x_ref, first_y_ref, out_z_ref,
    send_far_ref, keep_far_ref, send_near_ref, keep_near_ref,
    out_far_ref,
):
    rows, channels = mine_ref.shape
    shard = out_ref.shape[0]
    index = lax.axis_index(TENSOR)
    chip, core = index // 2, index % 2
    depth = channels // 2
    group, parity = lax.axis_index(SONGS), lax.axis_index(FRAME) % 2
    out_far_ref[2 * group + parity] = first_x_ref[depth:, :]
    out_far_ref[2 * (1 - group) + parity] = first_y_ref[depth:, :]
    out_far_ref[2 * group + 1 - parity] = out_z_ref[0]
    out_far_ref[2 * (1 - group) + 1 - parity] = out_z_ref[1]

    def term(block):
        at = pl.ds(pl.multiple_of(block * shard, shard), shard)
        value = jnp.dot(context_ref[:, :shard], out_ref[:, at], preferred_element_type=f32)
        far = jnp.dot(context_ref[:, shard:], out_far_ref[block], preferred_element_type=f32)
        return value + far

    sides = ((1 - chip, send_far_ref, keep_far_ref), (chip, send_near_ref, keep_near_ref))
    for goal, send_ref, keep_ref in sides:
        value = term(2 * goal + 1 - core).astype(bf16)
        send_ref[:rows, :] = value[rows:]
        send_ref[rows:, :] = value[:rows]
        block = 2 * goal + core
        at = pl.ds(pl.multiple_of(block * shard, shard), shard)
        value = term(block)
        keep_ref[:rows, :] = value[:rows] + mine_ref[:, at].astype(f32)
        keep_ref[rows:, :] = value[rows:] + theirs_ref[:, at].astype(f32)


def run_copies(pairs, sems):
    copies = [
        pltpu.make_async_copy(source, goal, sems.at[place])
        for place, (source, goal) in enumerate(pairs)
    ]
    for copy in copies:
        copy.start()
    for copy in copies:
        copy.wait()


def row_pieces(place, depth):
    step = depth // PIECES
    for piece in range(PIECES):
        start = pl.multiple_of(place * depth + piece * step, step)
        yield pl.ds(start, step), pl.ds(piece * step, step)


def pack_first_kernel(qkv_ref, out_ref, send_ref, sems):
    depth, shard = qkv_ref.shape[1] // 2, qkv_ref.shape[2]
    group, parity = lax.axis_index(SONGS), lax.axis_index(FRAME) % 2
    pairs = []
    for which, place, base in ((1, group, 0), (0, parity, depth + shard)):
        for rows, goal in row_pieces(place, depth):
            pairs.append((qkv_ref.at[which, rows, :], send_ref.at[pl.ds(base + goal.start, goal.size), :]))
    block = pl.ds(pl.multiple_of((2 * group + parity) * shard, shard), shard)
    for piece in range(2):
        rows = pl.ds(piece * shard // 2, shard // 2)
        goal = pl.ds(depth + piece * shard // 2, shard // 2)
        pairs.append((out_ref.at[rows, block], send_ref.at[goal, :]))
    run_copies(pairs, sems)


def pack_rest_kernel(qkv_ref, values_ref, sems):
    pairs = [
        (qkv_ref.at[2, rows, :], values_ref.at[goal, :])
        for rows, goal in row_pieces(lax.axis_index(SONGS), values_ref.shape[0])
    ]
    run_copies(pairs, sems)


def pack(kernel, shapes, copies, args):
    return pl.pallas_call(
        kernel,
        out_shape=[jax.ShapeDtypeStruct(shape, bf16) for shape in shapes],
        in_specs=[pl.BlockSpec(memory_space=pltpu.HBM)] * len(args),
        out_specs=[pl.BlockSpec(memory_space=VMEM)] * len(shapes),
        scratch_shapes=[pltpu.SemaphoreType.DMA((copies,))],
        compiler_params=pltpu.CompilerParams(vmem_limit_bytes=4 * 2**20),
        cost_estimate=pl.CostEstimate(flops=0, bytes_accessed=2**20, transcendentals=0),
    )(*[pltpu.with_memory_space_constraint(arg, pltpu.HBM) for arg in args])


def residual_kernel(latent_ref, keep_ref, far_ref, out_ref):
    stems = latent_ref.shape[0]
    index = lax.axis_index(TENSOR)
    chip, core = index // 2, index % 2
    start = pl.multiple_of(chip * WINDOW, WINDOW)
    for stem in range(stems // 2):
        rows = slice(stem * WINDOW, (stem + 1) * WINDOW)
        total = keep_ref[rows, :] + far_ref[rows, :].astype(f32)
        latent = latent_ref[core * (stems // 2) + stem, pl.ds(start, WINDOW), :]
        out_ref[rows, :] = (latent.astype(f32) + total).astype(bf16)


def place(value_ref, out_ref, window, sems):
    stems = out_ref.shape[0]
    core = lax.axis_index(TENSOR) % 2
    half = stems // 2
    at = pl.ds(pl.multiple_of(window * WINDOW, WINDOW), WINDOW)
    pairs = []
    for stem in range(stems):
        goal = (core if stem < half else 1 - core) * half + stem % half
        source = value_ref.at[pl.ds(stem * WINDOW, WINDOW), :]
        pairs.append((source, out_ref.at[goal, at, :]))
    run_copies(pairs, sems)


def place_near_kernel(keep_ref, got_ref, out_ref, value_ref, sems):
    value_ref[...] = (keep_ref[...] + got_ref[...].astype(f32)).astype(bf16)
    place(value_ref, out_ref, lax.axis_index(TENSOR) // 2, sems)


def place_far_kernel(value_ref, near_ref, out_ref, sems):
    del near_ref
    place(value_ref, out_ref, 1 - lax.axis_index(TENSOR) // 2, sems)


def call(kernel, outs, scratch, args, flops=0, moved=0, limit=16):
    return pl.pallas_call(
        kernel,
        out_shape=[jax.ShapeDtypeStruct(shape, dtype) for shape, dtype in outs],
        in_specs=[pl.BlockSpec(memory_space=VMEM)] * len(args),
        out_specs=[pl.BlockSpec(memory_space=VMEM)] * len(outs),
        scratch_shapes=[VMEM(shape, dtype) for shape, dtype in scratch],
        compiler_params=pltpu.CompilerParams(vmem_limit_bytes=limit * 2**20),
        cost_estimate=pl.CostEstimate(flops=flops, bytes_accessed=moved, transcendentals=0),
    )(*args)


def swap_cores(value):
    return lax.ppermute(value, TENSOR, [(0, 1), (1, 0), (2, 3), (3, 2)])


def swap_chips(value):
    return lax.ppermute(value, TENSOR, [(0, 2), (2, 0), (1, 3), (3, 1)])


def swap_groups(value):
    return lax.ppermute(value, SONGS, [(0, 1), (1, 0)])


ONE = ((0, 1), (1, 0), (2, 3), (3, 2))
TWO = ((0, 3), (3, 0), (1, 2), (2, 1))
FAR = ((0, 2), (2, 0), (1, 3), (3, 1))


def trade(value, pairs):
    return lax.ppermute(value, FRAME, pairs)


def trade_by_core(value):
    count = lax.axis_size(TENSOR)
    pairs = [
        (source * count + index, goal * count + index)
        for index in range(count)
        for source, goal in (TWO if index % 2 else ONE)
    ]
    return lax.ppermute(value, (FRAME, TENSOR), pairs)


def fast(
    latent, norm1_gain, conv1_weight, time_bias, norm2_gain, conv2_weight,
    attn_gain, qkv_weight, out_weight,
):
    stems, frames, channels = latent.shape
    frame_size = lax.axis_size(FRAME)
    shard = conv1_weight.shape[2]
    width = channels // GROUPS
    entries = frames * frame_size * width
    half_rows = stems // 2 * WINDOW
    qkv = jnp.transpose(qkv_weight, (1, 0, 2))
    depth = channels // 2
    (first,) = pack(
        pack_first_kernel, [(2 * depth + shard, shard)], 2 * PIECES + 2,
        [qkv, out_weight],
    )
    (values,) = pack(pack_rest_kernel, [(depth, shard)], PIECES, [qkv])
    first_x = swap_chips(first)
    v_x = swap_chips(values)
    first_x, q_x = first_x[: depth + shard], first_x[depth + shard :]
    first_y = swap_groups(first_x)
    q_z = trade(q_x, ONE)
    v_y = swap_groups(v_x)
    out_z = trade(jnp.stack([first_x[depth:], first_y[depth:]]), ONE)
    weight1 = swap_cores(conv1_weight)
    weight2 = swap_cores(conv2_weight).reshape(3 * shard, channels)
    bias_far = swap_cores(time_bias)
    gain_far = swap_cores(norm2_gain)
    gain2 = jnp.concatenate([norm2_gain, gain_far])[None]
    wide = channels + 2 * LANES
    near, own = call(
        functools.partial(stats_kernel, width),
        [((stems, wide), f32), ((stems, 2 * LANES), f32)],
        [((stems, channels), f32)] * 2,
        [latent],
    )
    far = trade(own, FAR)
    got = trade_by_core(near)
    swapped = swap_cores(got)
    half, span = stems // 2, 2 * shard
    narrow = span + 2 * LANES
    hid, one2, two2, own2 = call(
        functools.partial(first_kernel, entries, width, frame_size),
        [((half, frames, span), f32), ((half, narrow), f32), ((half, narrow), f32),
         ((half, 2 * LANES), f32)],
        [((half * frames, channels), bf16), ((16, channels), f32)] + [((half, span), f32)] * 2,
        [latent, got, swapped, far, own, norm1_gain[None], conv1_weight, weight1,
         time_bias[None], bias_far[None]],
        flops=6 * stems * frames * channels * shard, limit=24,
    )
    far2 = trade(own2, FAR)
    got_two = trade(two2, TWO)
    got_one = trade(one2, ONE)

    def second(other):
        return call(
            functools.partial(second_kernel, entries, width, frame_size, other),
            [((half_rows, channels), bf16 if other else f32)],
            [((half_rows, 6 * shard), bf16)],
            [hid, got_one, got_two, far2, own2, gain2,
             conv2_weight.reshape(3 * shard, channels), weight2],
            flops=12 * half_rows * channels * shard,
        )[0]

    summed = swap_chips(second(True))
    mine = call(
        residual_kernel, [((half_rows, channels), bf16)], [],
        [latent, second(False), summed],
    )[0]
    theirs = swap_cores(mine)
    weights = [attn_gain[None], qkv, first_x, first_y, q_x, q_z]
    projected = call(
        project_kernel,
        [((half_rows, 2 * shard), f32)] * 2 + [((half_rows, channels), bf16)], [],
        [mine, *weights],
        flops=8 * half_rows * channels * shard,
    )
    context = call(
        attention_kernel, [((2 * half_rows, 2 * shard), bf16)],
        [((2 * half_rows, channels), bf16)],
        [theirs, *weights, v_x, v_y, *projected],
        flops=24 * half_rows * channels * shard, limit=24,
    )[0]
    send_far, keep_far, send_near, keep_near = call(
        output_kernel,
        [((2 * half_rows, shard), bf16), ((2 * half_rows, shard), f32)] * 2,
        [((4, shard, shard), bf16)],
        [context, mine, theirs, out_weight, first_x, first_y, out_z],
        flops=8 * half_rows * channels * shard,
    )
    got_far = swap_cores(send_far)
    got_near = swap_cores(send_near)
    away = (keep_far + got_far.astype(f32)).astype(bf16)
    arrived = swap_chips(away)
    vmem, anywhere = pl.BlockSpec(memory_space=VMEM), pl.BlockSpec(memory_space=pl.ANY)
    shape = jax.ShapeDtypeStruct((stems, frames, shard), bf16)
    sems = pltpu.SemaphoreType.DMA((stems,))
    params = pltpu.CompilerParams(vmem_limit_bytes=4 * 2**20)
    near = pl.pallas_call(
        place_near_kernel, name="place_near", out_shape=shape,
        in_specs=[vmem, vmem], out_specs=anywhere, compiler_params=params,
        scratch_shapes=[VMEM((2 * half_rows, shard), bf16), sems],
    )(keep_near, got_near)
    return pl.pallas_call(
        place_far_kernel, name="place_far", out_shape=shape,
        in_specs=[vmem, anywhere], out_specs=anywhere, compiler_params=params,
        scratch_shapes=[sems], input_output_aliases={1: 0},
    )(arrived, near)


def local(*args):
    latent = args[0]
    stems, frames, channels = latent.shape
    tensor_size, frame_size = lax.axis_size(TENSOR), lax.axis_size(FRAME)
    shard = channels // tensor_size
    suits = (
        tensor_size == 4
        and frame_size == 4
        and lax.axis_size(SONGS) == 2
        and frames == 2 * WINDOW
        and stems % 2 == 0
        and stems <= 8
        and shard % (2 * LANES) == 0
    )
    if not suits:
        return generic(*args)
    return fast(*args)


def solution(mesh):
    return jax.shard_map(
        local,
        mesh=mesh,
        in_specs=(
            P(None, (SONGS, FRAME), None),
            P(),
            P(None, None, TENSOR),
            P(TENSOR),
            P(TENSOR),
            P(None, TENSOR, None),
            P(),
            P(None, None, TENSOR),
            P(TENSOR, None),
        ),
        out_specs=P(None, (SONGS, FRAME), TENSOR),
        check_vma=False,
    )
```

```python
import functools
import math

import jax
import jax.numpy as jnp
from jax import lax
from jax.experimental import pallas as pl
from jax.experimental.pallas import tpu as pltpu
from jax.sharding import PartitionSpec as P


TENSOR, FRAME, SONGS = "tensor", "frame", "groups"
GROUPS = 32
HEAD_DIM = 64
WINDOW = 64
LANES = 128
PIECES = 4
CHUNK = 2

norm_eps = 1e-05
rms_eps = 1e-06
HIGHEST = lax.Precision.HIGHEST
VMEM = pltpu.VMEM
bf16 = jnp.bfloat16
f32 = jnp.float32


def extended(block, sides, width):
    for axis, dim in sides:
        count = lax.axis_size(axis)
        forward = [(i, i + 1) for i in range(count - 1)]
        backward = [(target, source) for source, target in forward]
        low = lax.ppermute(
            lax.slice_in_dim(block, block.shape[dim] - width, None, axis=dim), axis, forward
        )
        high = lax.ppermute(lax.slice_in_dim(block, 0, width, axis=dim), axis, backward)
        block = jnp.concatenate([low, block, high], axis=dim)
    return block


def group_sums(hidden, group_count):
    stem_count, frame_count, channels = hidden.shape
    grouped = hidden.reshape(stem_count, frame_count, group_count, channels // group_count)
    return (jnp.sum(grouped, axis=(1, 3)), jnp.sum(grouped * grouped, axis=(1, 3)))


def apply_group(hidden, totals, squares, entries, gain_vec):
    stem_count, frame_count, channels = hidden.shape
    group_count = totals.shape[1]
    centre = totals / entries
    spread = squares / entries - centre * centre
    grouped = hidden.reshape(stem_count, frame_count, group_count, channels // group_count)
    scaled = (grouped - centre[:, None, :, None]) * lax.rsqrt(spread + norm_eps)[:, None, :, None]
    return scaled.reshape(stem_count, frame_count, channels) * gain_vec


def conv_padded(padded, kernel, frame_count):
    stem_count = padded.shape[0]
    channels = padded.shape[2]
    result = jnp.zeros((stem_count * frame_count, kernel.shape[2]), jnp.float32)
    for tap_index in range(3):
        tap_rows = padded[:, tap_index : tap_index + frame_count].reshape(
            stem_count * frame_count, channels
        )
        result = result + jnp.dot(tap_rows, kernel[tap_index], preferred_element_type=jnp.float32)
    return result.reshape(stem_count, frame_count, kernel.shape[2])


def attend(queries, keys_all, values):
    stem_count, frame_count, head_count, head_dim = queries.shape
    window_count = frame_count // WINDOW

    def arrange(source):
        shaped = source.reshape(stem_count, window_count, WINDOW, head_count, head_dim)
        return shaped.transpose(1, 3, 0, 2, 4).reshape(
            window_count, head_count, stem_count * WINDOW, head_dim
        )

    scores = jnp.einsum(
        "nhqd,nhkd->nhqk",
        arrange(queries),
        arrange(keys_all),
        precision=lax.Precision.HIGHEST,
        preferred_element_type=jnp.float32,
    ) / math.sqrt(head_dim)
    scores = scores - jnp.max(scores, axis=3, keepdims=True)
    exp_scores = jnp.exp(scores)
    attn_probs = (exp_scores / jnp.sum(exp_scores, axis=3, keepdims=True)).astype(jnp.bfloat16)
    context = jnp.einsum(
        "nhqk,nhkd->nhqd", attn_probs, arrange(values), preferred_element_type=jnp.float32
    ).astype(jnp.bfloat16)
    context = context.reshape(window_count, head_count, stem_count, WINDOW, head_dim).transpose(
        2, 0, 3, 1, 4
    )
    return context.reshape(stem_count * frame_count, head_count * head_dim)


def generic(
    latent,
    norm1_gain,
    conv1_weight,
    time_bias,
    norm2_gain,
    conv2_weight,
    attn_gain,
    qkv_weight,
    out_weight,
):
    stem_count, frame_count, channels = latent.shape
    tensor_size = lax.axis_size(TENSOR)
    shard_width = channels // tensor_size
    row_count = stem_count * frame_count
    group_entries = frame_count * lax.axis_size(FRAME) * (channels // GROUPS)
    latent_f = latent.astype(jnp.float32)
    sums_one, squares_one = group_sums(latent_f, GROUPS)
    sums_one, squares_one = lax.psum((sums_one, squares_one), FRAME)
    act_one = jax.nn.silu(
        apply_group(latent_f, sums_one, squares_one, group_entries, norm1_gain)
    ).astype(jnp.bfloat16)
    padded_one = extended(act_one, ((FRAME, 1),), 1)
    hid_one = conv_padded(padded_one, conv1_weight, frame_count)
    hid_one = hid_one + time_bias
    local_groups = GROUPS // tensor_size
    sums_two, squares_two = group_sums(hid_one, local_groups)
    sums_two, squares_two = lax.psum((sums_two, squares_two), FRAME)
    act_two = jax.nn.silu(
        apply_group(hid_one, sums_two, squares_two, group_entries, norm2_gain)
    ).astype(jnp.bfloat16)
    padded_two = extended(act_two, ((FRAME, 1),), 1)
    conv_term = conv_padded(padded_two, conv2_weight, frame_count)
    own_start = lax.axis_index(TENSOR) * shard_width
    qkv_flat = qkv_weight.reshape(channels, 3 * shard_width)
    conv_total = lax.psum(conv_term.astype(jnp.bfloat16), TENSOR).astype(jnp.float32)
    residual = (latent_f + conv_total).astype(jnp.bfloat16)
    res_f = residual.astype(jnp.float32)
    mean_sq = jnp.mean(res_f * res_f, axis=2, keepdims=True)
    normed = (res_f * lax.rsqrt(mean_sq + rms_eps) * attn_gain).astype(jnp.bfloat16)
    projected = jnp.dot(
        normed.reshape(row_count, channels), qkv_flat, preferred_element_type=jnp.float32
    )
    res_own = lax.dynamic_slice_in_dim(res_f, own_start, shard_width, 2)
    head_local = shard_width // HEAD_DIM
    projected = projected.reshape(stem_count, frame_count, 3, head_local, HEAD_DIM)
    values = projected[:, :, 2].astype(jnp.bfloat16)
    context = attend(projected[:, :, 0], projected[:, :, 1], values)
    out_term = jnp.dot(context, out_weight, preferred_element_type=jnp.float32).reshape(
        stem_count, frame_count, channels
    )
    attn_share = lax.psum_scatter(
        out_term.astype(jnp.bfloat16), TENSOR, scatter_dimension=2, tiled=True
    ).astype(jnp.float32)
    velocity = (res_own + attn_share).astype(jnp.bfloat16)
    return velocity


def silu_of_half(half):
    return half + half * jnp.tanh(half)


def one_hot(rows, columns, width, by_row):
    row = lax.broadcasted_iota(jnp.int32, (rows, columns), 0)
    column = lax.broadcasted_iota(jnp.int32, (rows, columns), 1)
    if by_row:
        return (row // width == column).astype(f32)
    return (row == column // width).astype(f32)


def f32_dot(a, b):
    return jnp.dot(a, b, precision=HIGHEST, preferred_element_type=f32)


def even_place():
    return lax.axis_index(FRAME) % 2 == 0


def group_totals(sums, squares, width):
    hot = one_hot(sums.shape[1], LANES, width, True)
    return f32_dot(sums, hot), f32_dot(squares, hot)


def channel_scale(refs, entries, channels, width):
    total = refs[0]
    for other in refs[1:]:
        total = total + other
    centre = total[:, :LANES] / entries
    spread = total[:, LANES:] / entries - centre * centre
    hot = one_hot(LANES, channels, width, False)
    return f32_dot(centre, hot), f32_dot(lax.rsqrt(spread + norm_eps), hot)


def stats_kernel(width, lat_ref, near_ref, own_ref, sum_ref, square_ref):
    stems, frames, channels = lat_ref.shape
    upward = even_place() == (lax.axis_index(TENSOR) % 2 == 0)
    for stem in range(stems):
        block = lat_ref[stem].astype(f32)
        sum_ref[stem : stem + 1, :] = jnp.sum(block, axis=0, keepdims=True)
        square_ref[stem : stem + 1, :] = jnp.sum(block * block, axis=0, keepdims=True)
        edge = jnp.where(upward, block[frames - 1 :], block[:1])
        near_ref[stem : stem + 1, :channels] = edge
    sums, squares = group_totals(sum_ref[...], square_ref[...], width)
    for ref, start in ((near_ref, channels), (own_ref, 0)):
        ref[:, start : start + LANES] = sums
        ref[:, start + LANES : start + 2 * LANES] = squares


def pick(value):
    half = value.shape[0] // 2
    return jnp.where(lax.axis_index(TENSOR) % 2 == 0, value[:half], value[half:])


def both_dots(rows, near, away):
    parts = [jnp.dot(rows, weight, preferred_element_type=f32) for weight in (near, away)]
    return jnp.concatenate(parts, axis=1)


def first_kernel(
    entries, width, frame_size,
    lat_ref, got_ref, swapped_ref, far_ref, own_ref, gain_ref, weight_ref, partner_ref,
    bias_ref, bias_far_ref,
    hid_ref, one_ref, two_ref, tot_ref, act_ref, edge_ref, sum_ref, square_ref,
):
    frames, channels = lat_ref.shape[1:]
    stems, _, span = hid_ref.shape
    place = lax.axis_index(FRAME)
    core = lax.axis_index(TENSOR) % 2
    centre, scale = channel_scale(
        [own_ref[...], got_ref[:, channels:], swapped_ref[:, channels:], far_ref[...]],
        entries, channels, width,
    )
    even = even_place()
    first_got = even == (core == 0)
    got, swapped = got_ref[:, :channels], swapped_ref[:, :channels]
    high, low = jnp.where(first_got, got, swapped), jnp.where(first_got, swapped, got)
    scale = scale * (0.5 * gain_ref[...])
    low, high = pick(silu_of_half((low - centre) * scale)), pick(silu_of_half((high - centre) * scale))
    centre, scale = pick(centre), pick(scale)
    edge_ref[...] = jnp.zeros_like(edge_ref)
    edge_ref[0:stems, :] = jnp.where(place > 0, low, 0.0)
    edge_ref[8 : 8 + stems, :] = jnp.where(place < frame_size - 1, high, 0.0)
    edge = edge_ref[...].astype(bf16)
    edge_low = both_dots(edge, weight_ref[0], partner_ref[0])
    edge_high = both_dots(edge, weight_ref[2], partner_ref[2])
    row = lax.broadcasted_iota(jnp.int32, (frames, span), 0)
    bias = jnp.concatenate([bias_ref[...], bias_far_ref[...]], axis=1)
    for stem in range(stems):
        if stem % CHUNK == 0:
            first, last = stem, min(stem + CHUNK, stems)
            for part in range(first, last):
                block = lat_ref[core * stems + part].astype(f32)
                block = (block - centre[part : part + 1]) * scale[part : part + 1]
                act_ref[part * frames : (part + 1) * frames, :] = silu_of_half(block).astype(bf16)
            rows = act_ref[first * frames : last * frames, :]
            taps = [both_dots(rows, weight_ref[tap], partner_ref[tap]) for tap in range(3)]
        lo = (stem - first) * frames
        before = pltpu.roll(taps[0][lo : lo + frames], 1, 0)
        after = pltpu.roll(taps[2][lo : lo + frames], frames - 1, 0)
        before = jnp.where(row == 0, edge_low[stem : stem + 1], before)
        after = jnp.where(row == frames - 1, edge_high[8 + stem : 9 + stem], after)
        hid = taps[1][lo : lo + frames] + before + after + bias
        hid_ref[stem] = hid
        sum_ref[stem : stem + 1, :] = jnp.sum(hid, axis=0, keepdims=True)
        square_ref[stem : stem + 1, :] = jnp.sum(hid * hid, axis=0, keepdims=True)
        down, up = hid[:1], hid[frames - 1 :]
        one_ref[stem : stem + 1, :span] = jnp.where(even, up, down)
        two_ref[stem : stem + 1, :span] = jnp.where(even, down, up)
    sums, squares = group_totals(sum_ref[...], square_ref[...], width)
    for ref, start in ((one_ref, span), (two_ref, span), (tot_ref, 0)):
        ref[:, start : start + LANES] = sums
        ref[:, start + LANES : start + 2 * LANES] = squares


def second_kernel(
    entries, width, frame_size, other,
    hid_ref, one_ref, two_ref, far_ref, own_ref, gain_ref, weight_ref, partner_ref,
    total_ref, act_ref,
):
    stems, _, span = hid_ref.shape
    shard = span // 2
    place = lax.axis_index(FRAME)
    chip = lax.axis_index(TENSOR) // 2
    window = 1 - chip if other else chip
    centre, scale = channel_scale(
        [own_ref[...], one_ref[:, span:], two_ref[:, span:], far_ref[...]],
        entries, span, width,
    )
    even = even_place()
    one, two = one_ref[:, :span], two_ref[:, :span]
    high, low = jnp.where(even, one, two), jnp.where(even, two, one)
    scale = scale * (0.5 * gain_ref[...])
    low = jnp.where(place > 0, silu_of_half((low - centre) * scale), 0.0)
    high = jnp.where(place < frame_size - 1, silu_of_half((high - centre) * scale), 0.0)
    row = lax.broadcasted_iota(jnp.int32, (WINDOW, span), 0)
    start = pl.multiple_of(window * WINDOW, WINDOW)
    for stem in range(stems):
        mean, factor = centre[stem : stem + 1], scale[stem : stem + 1]
        act = silu_of_half((hid_ref[stem, pl.ds(start, WINDOW), :] - mean) * factor)
        inner = silu_of_half((hid_ref[stem, WINDOW - 8 : WINDOW + 8, :] - mean) * factor)
        before = jnp.where(window == 0, low[stem : stem + 1], inner[7:8])
        after = jnp.where(window == 0, inner[8:9], high[stem : stem + 1])
        before = jnp.where(row == 0, before, pltpu.roll(act, 1, 0))
        after = jnp.where(row == WINDOW - 1, after, pltpu.roll(act, WINDOW - 1, 0))
        at = slice(stem * WINDOW, (stem + 1) * WINDOW)
        for tap, value in enumerate((before, act, after)):
            value = value.astype(bf16)
            act_ref[at, tap * shard : (tap + 1) * shard] = value[:, :shard]
            act_ref[at, (3 + tap) * shard : (4 + tap) * shard] = value[:, shard:]
    total = jnp.dot(act_ref[:, : 3 * shard], weight_ref[...], preferred_element_type=f32)
    total = total + jnp.dot(
        act_ref[:, 3 * shard :], partner_ref[...], preferred_element_type=f32
    )
    total_ref[...] = total.astype(total_ref.dtype)


def split2(value):
    high = value.astype(bf16)
    return high, (value - high.astype(f32)).astype(bf16)


def normed_rows(res, gain_ref):
    mean_sq = jnp.mean(res * res, axis=1, keepdims=True)
    return (res * lax.rsqrt(mean_sq + rms_eps) * gain_ref[...]).astype(bf16)


def projector(normed_ref, qkv_ref, k_x_ref, k_y_ref, q_x_ref, q_z_ref, v_refs=()):
    depth = normed_ref.shape[1] // 2
    group, parity = lax.axis_index(SONGS), lax.axis_index(FRAME) % 2

    def half(place):
        return normed_ref[:, pl.ds(pl.multiple_of(place * depth, depth), depth)]

    def project(side, which):
        if side == 0:
            return jnp.dot(normed_ref[...], qkv_ref[which], preferred_element_type=f32)
        if which == 0:
            place, near, away = parity, q_x_ref[...], q_z_ref[...]
        elif which == 1:
            place, near, away = group, k_x_ref[...], k_y_ref[...]
        else:
            place, near, away = group, v_refs[0][...], v_refs[1][...]
        value = jnp.dot(half(place), near, preferred_element_type=f32)
        return value + jnp.dot(half(1 - place), away, preferred_element_type=f32)

    return project


def project_kernel(
    mine_ref, gain_ref, qkv_ref, k_x_ref, k_y_ref, q_x_ref, q_z_ref,
    queries_ref, keys_ref, normed_ref,
):
    shard = qkv_ref.shape[2]
    normed_ref[...] = normed_rows(mine_ref[...].astype(f32), gain_ref)
    project = projector(normed_ref, qkv_ref, k_x_ref, k_y_ref, q_x_ref, q_z_ref)
    for side in range(2):
        at = slice(side * shard, (side + 1) * shard)
        queries_ref[:, at] = project(side, 0)
        keys_ref[:, at] = project(side, 1)


def attention_kernel(
    theirs_ref, gain_ref, qkv_ref, k_x_ref, k_y_ref, q_x_ref, q_z_ref, v_x_ref, v_y_ref,
    queries_ref, keys_ref, mine_ref,
    context_ref, normed_ref,
):
    rows = theirs_ref.shape[0]
    shard = qkv_ref.shape[2]
    normed_ref[:rows, :] = mine_ref[...]
    normed_ref[rows:, :] = normed_rows(theirs_ref[...].astype(f32), gain_ref)
    weights = qkv_ref, k_x_ref, k_y_ref, q_x_ref, q_z_ref
    project = projector(normed_ref.at[pl.ds(rows, rows), :], *weights)
    project_all = projector(normed_ref, *weights, (v_x_ref, v_y_ref))
    lane = lax.broadcasted_iota(jnp.int32, (2 * rows, LANES), 1)
    nt = (((1,), (1,)), ((), ()))
    for side in range(2):
        span = slice(side * shard, (side + 1) * shard)
        queries, keys = [
            jnp.concatenate([ref[:, span], project(side, which)], axis=0)
            for which, ref in enumerate((queries_ref, keys_ref))
        ]
        values = project_all(side, 2)
        queries = queries * (1.0 / math.sqrt(HEAD_DIM))
        for tile in range(shard // LANES):
            at = slice(tile * LANES, (tile + 1) * LANES)
            q_high, q_low = split2(queries[:, at])
            q_low = pltpu.roll(q_low.astype(f32), HEAD_DIM, 1).astype(bf16)
            k_high, k_low = split2(keys[:, at])
            k_rolled = split2(pltpu.roll(keys[:, at], HEAD_DIM, 1))
            terms, mixing = [], []
            for head in range(LANES // HEAD_DIM):
                inside = lane // HEAD_DIM == head
                left = jnp.where(inside, q_high, q_low)
                left = jnp.concatenate([left, left], axis=1)
                right = [
                    jnp.where(inside, own, rolled)
                    for own, rolled in zip((k_high, k_low), k_rolled)
                ]
                right = jnp.concatenate(right, axis=1)
                scores = lax.dot_general(left, right, nt, preferred_element_type=f32)
                scores = jnp.exp(scores - jnp.max(scores, axis=1, keepdims=True))
                terms.append(scores.astype(bf16))
                mixing.append(
                    jnp.concatenate(
                        [jnp.where(inside, values[:, at], 0.0), jnp.where(inside, 1.0, 0.0)], axis=1
                    ).astype(bf16)
                )
            mixed = jnp.dot(
                jnp.concatenate(terms, axis=1), jnp.concatenate(mixing, axis=0),
                preferred_element_type=f32,
            )
            base = side * shard + tile * LANES
            context_ref[:, base : base + LANES] = (mixed[:, :LANES] / mixed[:, LANES:]).astype(bf16)


def output_kernel(
    away, context_ref, mine_ref, theirs_ref, out_ref, out_x_ref, out_y_ref, out_z_ref,
    send_ref, keep_ref, out_far_ref,
):
    rows = mine_ref.shape[0]
    shard = out_ref.shape[0]
    index = lax.axis_index(TENSOR)
    chip, core = index // 2, index % 2
    group, parity = lax.axis_index(SONGS), lax.axis_index(FRAME) % 2
    out_far_ref[2 * group + parity] = out_x_ref[...]
    out_far_ref[2 * (1 - group) + parity] = out_y_ref[...]
    out_far_ref[2 * group + 1 - parity] = out_z_ref[0]
    out_far_ref[2 * (1 - group) + 1 - parity] = out_z_ref[1]

    def term(block):
        at = pl.ds(pl.multiple_of(block * shard, shard), shard)
        value = jnp.dot(context_ref[:, :shard], out_ref[:, at], preferred_element_type=f32)
        far = jnp.dot(context_ref[:, shard:], out_far_ref[block], preferred_element_type=f32)
        return value + far

    goal = 1 - chip if away else chip
    value = term(2 * goal + 1 - core).astype(bf16)
    send_ref[:rows, :] = value[rows:]
    send_ref[rows:, :] = value[:rows]
    block = 2 * goal + core
    at = pl.ds(pl.multiple_of(block * shard, shard), shard)
    value = term(block)
    keep_ref[:rows, :] = value[:rows] + mine_ref[:, at].astype(f32)
    keep_ref[rows:, :] = value[rows:] + theirs_ref[:, at].astype(f32)


def run_copies(pairs, sems):
    copies = [
        pltpu.make_async_copy(source, goal, sems.at[place])
        for place, (source, goal) in enumerate(pairs)
    ]
    for copy in copies:
        copy.start()
    for copy in copies:
        copy.wait()


def row_pieces(place, depth):
    step = depth // PIECES
    for piece in range(PIECES):
        start = pl.multiple_of(place * depth + piece * step, step)
        yield pl.ds(start, step), pl.ds(piece * step, step)


def pack_first_kernel(qkv_ref, out_ref, send_ref, sems):
    depth, shard = qkv_ref.shape[1] // 2, qkv_ref.shape[2]
    group, parity = lax.axis_index(SONGS), lax.axis_index(FRAME) % 2
    pairs = [
        (qkv_ref.at[1, rows, :], send_ref.at[goal, :]) for rows, goal in row_pieces(group, depth)
    ]
    block = pl.ds(pl.multiple_of((2 * group + parity) * shard, shard), shard)
    for piece in range(2):
        rows = pl.ds(piece * shard // 2, shard // 2)
        goal = pl.ds(depth + piece * shard // 2, shard // 2)
        pairs.append((out_ref.at[rows, block], send_ref.at[goal, :]))
    run_copies(pairs, sems)


def pack_rest_kernel(qkv_ref, send_ref, sems):
    depth = send_ref.shape[1]
    group, parity = lax.axis_index(SONGS), lax.axis_index(FRAME) % 2
    pairs = []
    for slot, which, place in ((0, 0, parity), (1, 2, group)):
        for rows, goal in row_pieces(place, depth):
            pairs.append((qkv_ref.at[which, rows, :], send_ref.at[slot, goal, :]))
    run_copies(pairs, sems)


def pack(kernel, shapes, copies, args):
    return pl.pallas_call(
        kernel,
        out_shape=[jax.ShapeDtypeStruct(shape, bf16) for shape in shapes],
        in_specs=[pl.BlockSpec(memory_space=pltpu.HBM)] * len(args),
        out_specs=[pl.BlockSpec(memory_space=VMEM)] * len(shapes),
        scratch_shapes=[pltpu.SemaphoreType.DMA((copies,))],
        compiler_params=pltpu.CompilerParams(vmem_limit_bytes=4 * 2**20),
        cost_estimate=pl.CostEstimate(flops=0, bytes_accessed=2**20, transcendentals=0),
    )(*[pltpu.with_memory_space_constraint(arg, pltpu.HBM) for arg in args])


def residual_kernel(latent_ref, keep_ref, far_ref, out_ref):
    stems = latent_ref.shape[0]
    index = lax.axis_index(TENSOR)
    chip, core = index // 2, index % 2
    start = pl.multiple_of(chip * WINDOW, WINDOW)
    for stem in range(stems // 2):
        rows = slice(stem * WINDOW, (stem + 1) * WINDOW)
        total = keep_ref[rows, :] + far_ref[rows, :].astype(f32)
        latent = latent_ref[core * (stems // 2) + stem, pl.ds(start, WINDOW), :]
        out_ref[rows, :] = (latent.astype(f32) + total).astype(bf16)


def place(value_ref, out_ref, window, sems):
    stems = out_ref.shape[0]
    core = lax.axis_index(TENSOR) % 2
    half = stems // 2
    at = pl.ds(pl.multiple_of(window * WINDOW, WINDOW), WINDOW)
    pairs = []
    for stem in range(stems):
        goal = (core if stem < half else 1 - core) * half + stem % half
        source = value_ref.at[pl.ds(stem * WINDOW, WINDOW), :]
        pairs.append((source, out_ref.at[goal, at, :]))
    run_copies(pairs, sems)


def place_near_kernel(keep_ref, got_ref, out_ref, value_ref, sems):
    value_ref[...] = (keep_ref[...] + got_ref[...].astype(f32)).astype(bf16)
    place(value_ref, out_ref, lax.axis_index(TENSOR) // 2, sems)


def place_far_kernel(value_ref, near_ref, out_ref, sems):
    del near_ref
    place(value_ref, out_ref, 1 - lax.axis_index(TENSOR) // 2, sems)


def call(kernel, outs, scratch, args, flops=0, moved=0, limit=16):
    return pl.pallas_call(
        kernel,
        out_shape=[jax.ShapeDtypeStruct(shape, dtype) for shape, dtype in outs],
        in_specs=[pl.BlockSpec(memory_space=VMEM)] * len(args),
        out_specs=[pl.BlockSpec(memory_space=VMEM)] * len(outs),
        scratch_shapes=[VMEM(shape, dtype) for shape, dtype in scratch],
        compiler_params=pltpu.CompilerParams(vmem_limit_bytes=limit * 2**20),
        cost_estimate=pl.CostEstimate(flops=flops, bytes_accessed=moved, transcendentals=0),
    )(*args)


def swap_cores(value):
    return lax.ppermute(value, TENSOR, [(0, 1), (1, 0), (2, 3), (3, 2)])


def swap_chips(value):
    return lax.ppermute(value, TENSOR, [(0, 2), (2, 0), (1, 3), (3, 1)])


def swap_groups(value):
    return lax.ppermute(value, SONGS, [(0, 1), (1, 0)])


ONE = ((0, 1), (1, 0), (2, 3), (3, 2))
TWO = ((0, 3), (3, 0), (1, 2), (2, 1))
FAR = ((0, 2), (2, 0), (1, 3), (3, 1))


def trade(value, pairs):
    return lax.ppermute(value, FRAME, pairs)


def trade_by_core(value):
    count = lax.axis_size(TENSOR)
    pairs = [
        (source * count + index, goal * count + index)
        for index in range(count)
        for source, goal in (TWO if index % 2 else ONE)
    ]
    return lax.ppermute(value, (FRAME, TENSOR), pairs)


def fast(
    latent, norm1_gain, conv1_weight, time_bias, norm2_gain, conv2_weight,
    attn_gain, qkv_weight, out_weight,
):
    stems, frames, channels = latent.shape
    frame_size = lax.axis_size(FRAME)
    shard = conv1_weight.shape[2]
    width = channels // GROUPS
    entries = frames * frame_size * width
    half_rows = stems // 2 * WINDOW
    qkv = jnp.transpose(qkv_weight, (1, 0, 2))
    depth = channels // 2
    (first,) = pack(pack_first_kernel, [(depth + shard, shard)], PIECES + 2, [qkv, out_weight])
    (rest,) = pack(pack_rest_kernel, [(2, depth, shard)], 2 * PIECES, [qkv])
    first_x = swap_chips(first)
    rest_x = swap_chips(rest)
    k_x, out_x = first_x[:depth], first_x[depth:]
    q_x, v_x = rest_x[0], rest_x[1]
    out_y = swap_groups(out_x)
    k_y = swap_groups(k_x)
    q_z = trade(q_x, ONE)
    v_y = swap_groups(v_x)
    out_z = trade(jnp.stack([out_x, out_y]), ONE)
    weight1 = swap_cores(conv1_weight)
    weight2 = swap_cores(conv2_weight).reshape(3 * shard, channels)
    bias_far = swap_cores(time_bias)
    gain_far = swap_cores(norm2_gain)
    gain2 = jnp.concatenate([norm2_gain, gain_far])[None]
    wide = channels + 2 * LANES
    near, own = call(
        functools.partial(stats_kernel, width),
        [((stems, wide), f32), ((stems, 2 * LANES), f32)],
        [((stems, channels), f32)] * 2,
        [latent],
    )
    far = trade(own, FAR)
    got = trade_by_core(near)
    swapped = swap_cores(got)
    half, span = stems // 2, 2 * shard
    narrow = span + 2 * LANES
    hid, one2, two2, own2 = call(
        functools.partial(first_kernel, entries, width, frame_size),
        [((half, frames, span), f32), ((half, narrow), f32), ((half, narrow), f32),
         ((half, 2 * LANES), f32)],
        [((half * frames, channels), bf16), ((16, channels), f32)] + [((half, span), f32)] * 2,
        [latent, got, swapped, far, own, norm1_gain[None], conv1_weight, weight1,
         time_bias[None], bias_far[None]],
        flops=6 * stems * frames * channels * shard, limit=24,
    )
    far2 = trade(own2, FAR)
    got_two = trade(two2, TWO)
    got_one = trade(one2, ONE)

    def second(other):
        return call(
            functools.partial(second_kernel, entries, width, frame_size, other),
            [((half_rows, channels), bf16 if other else f32)],
            [((half_rows, 6 * shard), bf16)],
            [hid, got_one, got_two, far2, own2, gain2,
             conv2_weight.reshape(3 * shard, channels), weight2],
            flops=12 * half_rows * channels * shard,
        )[0]

    summed = swap_chips(second(True))
    mine = call(
        residual_kernel, [((half_rows, channels), bf16)], [],
        [latent, second(False), summed],
    )[0]
    theirs = swap_cores(mine)
    weights = [attn_gain[None], qkv, k_x, k_y, q_x, q_z]
    projected = call(
        project_kernel,
        [((half_rows, 2 * shard), f32)] * 2 + [((half_rows, channels), bf16)], [],
        [mine, *weights],
        flops=8 * half_rows * channels * shard,
    )
    context = call(
        attention_kernel, [((2 * half_rows, 2 * shard), bf16)],
        [((2 * half_rows, channels), bf16)],
        [theirs, *weights, v_x, v_y, *projected],
        flops=24 * half_rows * channels * shard, limit=24,
    )[0]

    def output(away):
        return call(
            functools.partial(output_kernel, away),
            [((2 * half_rows, shard), bf16), ((2 * half_rows, shard), f32)],
            [((4, shard, shard), bf16)],
            [context, mine, theirs, out_weight, out_x, out_y, out_z],
            flops=4 * half_rows * channels * shard,
        )

    send_far, keep_far = output(True)
    send_near, keep_near = output(False)
    got_far = swap_cores(send_far)
    got_near = swap_cores(send_near)
    away = (keep_far + got_far.astype(f32)).astype(bf16)
    arrived = swap_chips(away)
    vmem, anywhere = pl.BlockSpec(memory_space=VMEM), pl.BlockSpec(memory_space=pl.ANY)
    shape = jax.ShapeDtypeStruct((stems, frames, shard), bf16)
    sems = pltpu.SemaphoreType.DMA((stems,))
    params = pltpu.CompilerParams(vmem_limit_bytes=4 * 2**20)
    near = pl.pallas_call(
        place_near_kernel, name="place_near", out_shape=shape,
        in_specs=[vmem, vmem], out_specs=anywhere, compiler_params=params,
        scratch_shapes=[VMEM((2 * half_rows, shard), bf16), sems],
    )(keep_near, got_near)
    return pl.pallas_call(
        place_far_kernel, name="place_far", out_shape=shape,
        in_specs=[vmem, anywhere], out_specs=anywhere, compiler_params=params,
        scratch_shapes=[sems], input_output_aliases={1: 0},
    )(arrived, near)


def local(*args):
    latent = args[0]
    stems, frames, channels = latent.shape
    tensor_size, frame_size = lax.axis_size(TENSOR), lax.axis_size(FRAME)
    shard = channels // tensor_size
    suits = (
        tensor_size == 4
        and frame_size == 4
        and lax.axis_size(SONGS) == 2
        and frames == 2 * WINDOW
        and stems % 2 == 0
        and stems <= 8
        and shard % (2 * LANES) == 0
    )
    if not suits:
        return generic(*args)
    return fast(*args)


def solution(mesh):
    return jax.shard_map(
        local,
        mesh=mesh,
        in_specs=(
            P(None, (SONGS, FRAME), None),
            P(),
            P(None, None, TENSOR),
            P(TENSOR),
            P(TENSOR),
            P(None, TENSOR, None),
            P(),
            P(None, None, TENSOR),
            P(TENSOR, None),
        ),
        out_specs=P(None, (SONGS, FRAME), TENSOR),
        check_vma=False,
    )
```

```python
import functools
import math

import jax
import jax.numpy as jnp
from jax import lax
from jax.experimental import pallas as pl
from jax.experimental.pallas import tpu as pltpu
from jax.sharding import PartitionSpec as P


TENSOR, FRAME, SONGS = "tensor", "frame", "groups"
GROUPS = 32
HEAD_DIM = 64
WINDOW = 64
LANES = 128
PIECES = 4
CHUNK = 2

norm_eps = 1e-05
rms_eps = 1e-06
HIGHEST = lax.Precision.HIGHEST
VMEM = pltpu.VMEM
bf16 = jnp.bfloat16
f32 = jnp.float32


def extended(block, sides, width):
    for axis, dim in sides:
        count = lax.axis_size(axis)
        forward = [(i, i + 1) for i in range(count - 1)]
        backward = [(target, source) for source, target in forward]
        low = lax.ppermute(
            lax.slice_in_dim(block, block.shape[dim] - width, None, axis=dim), axis, forward
        )
        high = lax.ppermute(lax.slice_in_dim(block, 0, width, axis=dim), axis, backward)
        block = jnp.concatenate([low, block, high], axis=dim)
    return block


def group_sums(hidden, group_count):
    stem_count, frame_count, channels = hidden.shape
    grouped = hidden.reshape(stem_count, frame_count, group_count, channels // group_count)
    return (jnp.sum(grouped, axis=(1, 3)), jnp.sum(grouped * grouped, axis=(1, 3)))


def apply_group(hidden, totals, squares, entries, gain_vec):
    stem_count, frame_count, channels = hidden.shape
    group_count = totals.shape[1]
    centre = totals / entries
    spread = squares / entries - centre * centre
    grouped = hidden.reshape(stem_count, frame_count, group_count, channels // group_count)
    scaled = (grouped - centre[:, None, :, None]) * lax.rsqrt(spread + norm_eps)[:, None, :, None]
    return scaled.reshape(stem_count, frame_count, channels) * gain_vec


def conv_padded(padded, kernel, frame_count):
    stem_count = padded.shape[0]
    channels = padded.shape[2]
    result = jnp.zeros((stem_count * frame_count, kernel.shape[2]), jnp.float32)
    for tap_index in range(3):
        tap_rows = padded[:, tap_index : tap_index + frame_count].reshape(
            stem_count * frame_count, channels
        )
        result = result + jnp.dot(tap_rows, kernel[tap_index], preferred_element_type=jnp.float32)
    return result.reshape(stem_count, frame_count, kernel.shape[2])


def attend(queries, keys_all, values):
    stem_count, frame_count, head_count, head_dim = queries.shape
    window_count = frame_count // WINDOW

    def arrange(source):
        shaped = source.reshape(stem_count, window_count, WINDOW, head_count, head_dim)
        return shaped.transpose(1, 3, 0, 2, 4).reshape(
            window_count, head_count, stem_count * WINDOW, head_dim
        )

    scores = jnp.einsum(
        "nhqd,nhkd->nhqk",
        arrange(queries),
        arrange(keys_all),
        precision=lax.Precision.HIGHEST,
        preferred_element_type=jnp.float32,
    ) / math.sqrt(head_dim)
    scores = scores - jnp.max(scores, axis=3, keepdims=True)
    exp_scores = jnp.exp(scores)
    attn_probs = (exp_scores / jnp.sum(exp_scores, axis=3, keepdims=True)).astype(jnp.bfloat16)
    context = jnp.einsum(
        "nhqk,nhkd->nhqd", attn_probs, arrange(values), preferred_element_type=jnp.float32
    ).astype(jnp.bfloat16)
    context = context.reshape(window_count, head_count, stem_count, WINDOW, head_dim).transpose(
        2, 0, 3, 1, 4
    )
    return context.reshape(stem_count * frame_count, head_count * head_dim)


def generic(
    latent,
    norm1_gain,
    conv1_weight,
    time_bias,
    norm2_gain,
    conv2_weight,
    attn_gain,
    qkv_weight,
    out_weight,
):
    stem_count, frame_count, channels = latent.shape
    tensor_size = lax.axis_size(TENSOR)
    shard_width = channels // tensor_size
    row_count = stem_count * frame_count
    group_entries = frame_count * lax.axis_size(FRAME) * (channels // GROUPS)
    latent_f = latent.astype(jnp.float32)
    sums_one, squares_one = group_sums(latent_f, GROUPS)
    sums_one, squares_one = lax.psum((sums_one, squares_one), FRAME)
    act_one = jax.nn.silu(
        apply_group(latent_f, sums_one, squares_one, group_entries, norm1_gain)
    ).astype(jnp.bfloat16)
    padded_one = extended(act_one, ((FRAME, 1),), 1)
    hid_one = conv_padded(padded_one, conv1_weight, frame_count)
    hid_one = hid_one + time_bias
    local_groups = GROUPS // tensor_size
    sums_two, squares_two = group_sums(hid_one, local_groups)
    sums_two, squares_two = lax.psum((sums_two, squares_two), FRAME)
    act_two = jax.nn.silu(
        apply_group(hid_one, sums_two, squares_two, group_entries, norm2_gain)
    ).astype(jnp.bfloat16)
    padded_two = extended(act_two, ((FRAME, 1),), 1)
    conv_term = conv_padded(padded_two, conv2_weight, frame_count)
    own_start = lax.axis_index(TENSOR) * shard_width
    qkv_flat = qkv_weight.reshape(channels, 3 * shard_width)
    conv_total = lax.psum(conv_term.astype(jnp.bfloat16), TENSOR).astype(jnp.float32)
    residual = (latent_f + conv_total).astype(jnp.bfloat16)
    res_f = residual.astype(jnp.float32)
    mean_sq = jnp.mean(res_f * res_f, axis=2, keepdims=True)
    normed = (res_f * lax.rsqrt(mean_sq + rms_eps) * attn_gain).astype(jnp.bfloat16)
    projected = jnp.dot(
        normed.reshape(row_count, channels), qkv_flat, preferred_element_type=jnp.float32
    )
    res_own = lax.dynamic_slice_in_dim(res_f, own_start, shard_width, 2)
    head_local = shard_width // HEAD_DIM
    projected = projected.reshape(stem_count, frame_count, 3, head_local, HEAD_DIM)
    values = projected[:, :, 2].astype(jnp.bfloat16)
    context = attend(projected[:, :, 0], projected[:, :, 1], values)
    out_term = jnp.dot(context, out_weight, preferred_element_type=jnp.float32).reshape(
        stem_count, frame_count, channels
    )
    attn_share = lax.psum_scatter(
        out_term.astype(jnp.bfloat16), TENSOR, scatter_dimension=2, tiled=True
    ).astype(jnp.float32)
    velocity = (res_own + attn_share).astype(jnp.bfloat16)
    return velocity


def silu_of_half(half):
    return half + half * jnp.tanh(half)


def one_hot(rows, columns, width, by_row):
    row = lax.broadcasted_iota(jnp.int32, (rows, columns), 0)
    column = lax.broadcasted_iota(jnp.int32, (rows, columns), 1)
    if by_row:
        return (row // width == column).astype(f32)
    return (row == column // width).astype(f32)


def f32_dot(a, b):
    return jnp.dot(a, b, precision=HIGHEST, preferred_element_type=f32)


def even_place():
    return lax.axis_index(FRAME) % 2 == 0


def group_totals(sums, squares, width):
    hot = one_hot(sums.shape[1], LANES, width, True)
    return f32_dot(sums, hot), f32_dot(squares, hot)


def channel_scale(refs, entries, channels, width):
    total = refs[0]
    for other in refs[1:]:
        total = total + other
    centre = total[:, :LANES] / entries
    spread = total[:, LANES:] / entries - centre * centre
    hot = one_hot(LANES, channels, width, False)
    return f32_dot(centre, hot), f32_dot(lax.rsqrt(spread + norm_eps), hot)


def stats_kernel(width, lat_ref, near_ref, own_ref, sum_ref, square_ref):
    stems, frames, channels = lat_ref.shape
    upward = even_place() == (lax.axis_index(TENSOR) % 2 == 0)
    for stem in range(stems):
        block = lat_ref[stem].astype(f32)
        sum_ref[stem : stem + 1, :] = jnp.sum(block, axis=0, keepdims=True)
        square_ref[stem : stem + 1, :] = jnp.sum(block * block, axis=0, keepdims=True)
        edge = jnp.where(upward, block[frames - 1 :], block[:1])
        near_ref[stem : stem + 1, :channels] = edge
    sums, squares = group_totals(sum_ref[...], square_ref[...], width)
    for ref, start in ((near_ref, channels), (own_ref, 0)):
        ref[:, start : start + LANES] = sums
        ref[:, start + LANES : start + 2 * LANES] = squares


def pick(value):
    half = value.shape[0] // 2
    return jnp.where(lax.axis_index(TENSOR) % 2 == 0, value[:half], value[half:])


def both_dots(rows, near, away):
    parts = [jnp.dot(rows, weight, preferred_element_type=f32) for weight in (near, away)]
    return jnp.concatenate(parts, axis=1)


def first_kernel(
    entries, width, frame_size,
    lat_ref, got_ref, swapped_ref, far_ref, own_ref, gain_ref, weight_ref, partner_ref,
    bias_ref, bias_far_ref,
    hid_ref, one_ref, two_ref, tot_ref, act_ref, edge_ref, sum_ref, square_ref,
):
    frames, channels = lat_ref.shape[1:]
    stems, _, span = hid_ref.shape
    place = lax.axis_index(FRAME)
    core = lax.axis_index(TENSOR) % 2
    centre, scale = channel_scale(
        [own_ref[...], got_ref[:, channels:], swapped_ref[:, channels:], far_ref[...]],
        entries, channels, width,
    )
    even = even_place()
    first_got = even == (core == 0)
    got, swapped = got_ref[:, :channels], swapped_ref[:, :channels]
    high, low = jnp.where(first_got, got, swapped), jnp.where(first_got, swapped, got)
    scale = scale * (0.5 * gain_ref[...])
    low, high = pick(silu_of_half((low - centre) * scale)), pick(silu_of_half((high - centre) * scale))
    centre, scale = pick(centre), pick(scale)
    edge_ref[...] = jnp.zeros_like(edge_ref)
    edge_ref[0:stems, :] = jnp.where(place > 0, low, 0.0)
    edge_ref[8 : 8 + stems, :] = jnp.where(place < frame_size - 1, high, 0.0)
    edge = edge_ref[...].astype(bf16)
    edge_low = both_dots(edge, weight_ref[0], partner_ref[0])
    edge_high = both_dots(edge, weight_ref[2], partner_ref[2])
    row = lax.broadcasted_iota(jnp.int32, (frames, span), 0)
    bias = jnp.concatenate([bias_ref[...], bias_far_ref[...]], axis=1)
    for stem in range(stems):
        if stem % CHUNK == 0:
            first, last = stem, min(stem + CHUNK, stems)
            for part in range(first, last):
                block = lat_ref[core * stems + part].astype(f32)
                block = (block - centre[part : part + 1]) * scale[part : part + 1]
                act_ref[part * frames : (part + 1) * frames, :] = silu_of_half(block).astype(bf16)
            rows = act_ref[first * frames : last * frames, :]
            taps = [both_dots(rows, weight_ref[tap], partner_ref[tap]) for tap in range(3)]
        lo = (stem - first) * frames
        before = pltpu.roll(taps[0][lo : lo + frames], 1, 0)
        after = pltpu.roll(taps[2][lo : lo + frames], frames - 1, 0)
        before = jnp.where(row == 0, edge_low[stem : stem + 1], before)
        after = jnp.where(row == frames - 1, edge_high[8 + stem : 9 + stem], after)
        hid = taps[1][lo : lo + frames] + before + after + bias
        hid_ref[stem] = hid
        sum_ref[stem : stem + 1, :] = jnp.sum(hid, axis=0, keepdims=True)
        square_ref[stem : stem + 1, :] = jnp.sum(hid * hid, axis=0, keepdims=True)
        down, up = hid[:1], hid[frames - 1 :]
        one_ref[stem : stem + 1, :span] = jnp.where(even, up, down)
        two_ref[stem : stem + 1, :span] = jnp.where(even, down, up)
    sums, squares = group_totals(sum_ref[...], square_ref[...], width)
    for ref, start in ((one_ref, span), (two_ref, span), (tot_ref, 0)):
        ref[:, start : start + LANES] = sums
        ref[:, start + LANES : start + 2 * LANES] = squares


def second_kernel(
    entries, width, frame_size, other,
    hid_ref, one_ref, two_ref, far_ref, own_ref, gain_ref, weight_ref, partner_ref,
    total_ref, act_ref,
):
    stems, _, span = hid_ref.shape
    shard = span // 2
    place = lax.axis_index(FRAME)
    chip = lax.axis_index(TENSOR) // 2
    window = 1 - chip if other else chip
    centre, scale = channel_scale(
        [own_ref[...], one_ref[:, span:], two_ref[:, span:], far_ref[...]],
        entries, span, width,
    )
    even = even_place()
    one, two = one_ref[:, :span], two_ref[:, :span]
    high, low = jnp.where(even, one, two), jnp.where(even, two, one)
    scale = scale * (0.5 * gain_ref[...])
    low = jnp.where(place > 0, silu_of_half((low - centre) * scale), 0.0)
    high = jnp.where(place < frame_size - 1, silu_of_half((high - centre) * scale), 0.0)
    row = lax.broadcasted_iota(jnp.int32, (WINDOW, span), 0)
    start = pl.multiple_of(window * WINDOW, WINDOW)
    for stem in range(stems):
        mean, factor = centre[stem : stem + 1], scale[stem : stem + 1]
        act = silu_of_half((hid_ref[stem, pl.ds(start, WINDOW), :] - mean) * factor)
        inner = silu_of_half((hid_ref[stem, WINDOW - 8 : WINDOW + 8, :] - mean) * factor)
        before = jnp.where(window == 0, low[stem : stem + 1], inner[7:8])
        after = jnp.where(window == 0, inner[8:9], high[stem : stem + 1])
        before = jnp.where(row == 0, before, pltpu.roll(act, 1, 0))
        after = jnp.where(row == WINDOW - 1, after, pltpu.roll(act, WINDOW - 1, 0))
        at = slice(stem * WINDOW, (stem + 1) * WINDOW)
        for tap, value in enumerate((before, act, after)):
            value = value.astype(bf16)
            act_ref[at, tap * shard : (tap + 1) * shard] = value[:, :shard]
            act_ref[at, (3 + tap) * shard : (4 + tap) * shard] = value[:, shard:]
    total = jnp.dot(act_ref[:, : 3 * shard], weight_ref[...], preferred_element_type=f32)
    total = total + jnp.dot(
        act_ref[:, 3 * shard :], partner_ref[...], preferred_element_type=f32
    )
    total_ref[...] = total.astype(total_ref.dtype)


def split2(value):
    high = value.astype(bf16)
    return high, (value - high.astype(f32)).astype(bf16)


def normed_rows(res, gain_ref):
    mean_sq = jnp.mean(res * res, axis=1, keepdims=True)
    return (res * lax.rsqrt(mean_sq + rms_eps) * gain_ref[...]).astype(bf16)


def projector(normed_ref, qkv_ref, k_x_ref, k_y_ref, q_x_ref, q_z_ref, v_refs=()):
    depth = normed_ref.shape[1] // 2
    group, parity = lax.axis_index(SONGS), lax.axis_index(FRAME) % 2

    def half(place):
        return normed_ref[:, pl.ds(pl.multiple_of(place * depth, depth), depth)]

    def project(side, which):
        if side == 0:
            return jnp.dot(normed_ref[...], qkv_ref[which], preferred_element_type=f32)
        if which == 0:
            place, near, away = parity, q_x_ref[...], q_z_ref[...]
        elif which == 1:
            place, near, away = group, k_x_ref[...], k_y_ref[...]
        else:
            place, near, away = group, v_refs[0][...], v_refs[1][...]
        value = jnp.dot(half(place), near, preferred_element_type=f32)
        return value + jnp.dot(half(1 - place), away, preferred_element_type=f32)

    return project


def project_kernel(
    mine_ref, gain_ref, qkv_ref, k_x_ref, k_y_ref,
    queries_ref, keys_ref, normed_ref,
):
    shard = qkv_ref.shape[2]
    normed_ref[...] = normed_rows(mine_ref[...].astype(f32), gain_ref)
    project = projector(normed_ref, qkv_ref, k_x_ref, k_y_ref, None, None)
    queries_ref[...] = project(0, 0)
    for side in range(2):
        keys_ref[:, side * shard : (side + 1) * shard] = project(side, 1)


def attention_kernel(
    theirs_ref, gain_ref, qkv_ref, k_x_ref, k_y_ref, q_x_ref, q_z_ref, v_x_ref, v_y_ref,
    queries_ref, keys_ref, mine_ref,
    context_ref, normed_ref,
):
    rows = theirs_ref.shape[0]
    shard = qkv_ref.shape[2]
    normed_ref[:rows, :] = mine_ref[...]
    normed_ref[rows:, :] = normed_rows(theirs_ref[...].astype(f32), gain_ref)
    weights = qkv_ref, k_x_ref, k_y_ref, q_x_ref, q_z_ref
    project = projector(normed_ref.at[pl.ds(rows, rows), :], *weights)
    project_all = projector(normed_ref, *weights, (v_x_ref, v_y_ref))
    lane = lax.broadcasted_iota(jnp.int32, (2 * rows, LANES), 1)
    nt = (((1,), (1,)), ((), ()))
    for side in range(2):
        span = slice(side * shard, (side + 1) * shard)
        if side == 0:
            queries = jnp.concatenate([queries_ref[...], project(0, 0)], axis=0)
        else:
            queries = project_all(1, 0)
        keys = jnp.concatenate([keys_ref[:, span], project(side, 1)], axis=0)
        values = project_all(side, 2)
        queries = queries * (math.log2(math.e) / math.sqrt(HEAD_DIM))
        for tile in range(shard // LANES):
            at = slice(tile * LANES, (tile + 1) * LANES)
            q_high, q_low = split2(queries[:, at])
            q_low = pltpu.roll(q_low.astype(f32), HEAD_DIM, 1).astype(bf16)
            k_high, k_low = split2(keys[:, at])
            k_rolled = split2(pltpu.roll(keys[:, at], HEAD_DIM, 1))
            terms, mixing = [], []
            for head in range(LANES // HEAD_DIM):
                inside = lane // HEAD_DIM == head
                left = jnp.where(inside, q_high, q_low)
                left = jnp.concatenate([left, left], axis=1)
                right = [
                    jnp.where(inside, own, rolled)
                    for own, rolled in zip((k_high, k_low), k_rolled)
                ]
                right = jnp.concatenate(right, axis=1)
                scores = lax.dot_general(left, right, nt, preferred_element_type=f32)
                scores = jnp.exp2(scores - jnp.max(scores, axis=1, keepdims=True))
                terms.append(scores.astype(bf16))
                mixing.append(
                    jnp.concatenate(
                        [jnp.where(inside, values[:, at], 0.0), jnp.where(inside, 1.0, 0.0)], axis=1
                    ).astype(bf16)
                )
            mixed = jnp.dot(
                jnp.concatenate(terms, axis=1), jnp.concatenate(mixing, axis=0),
                preferred_element_type=f32,
            )
            base = side * shard + tile * LANES
            context_ref[:, base : base + LANES] = (mixed[:, :LANES] / mixed[:, LANES:]).astype(bf16)


def out_far_weights(goal_ref, out_x_ref, out_y_ref, out_z_ref):
    group, parity = lax.axis_index(SONGS), lax.axis_index(FRAME) % 2
    goal_ref[2 * group + parity] = out_x_ref[...]
    goal_ref[2 * (1 - group) + parity] = out_y_ref[...]
    goal_ref[2 * group + 1 - parity] = out_z_ref[0]
    goal_ref[2 * (1 - group) + 1 - parity] = out_z_ref[1]


def out_term(context_ref, out_ref, far_ref, block):
    shard = out_ref.shape[0]
    at = pl.ds(pl.multiple_of(block * shard, shard), shard)
    value = jnp.dot(context_ref[:, :shard], out_ref[:, at], preferred_element_type=f32)
    return value + jnp.dot(context_ref[:, shard:], far_ref[block], preferred_element_type=f32)


def output_send_kernel(
    away, context_ref, out_ref, out_x_ref, out_y_ref, out_z_ref, send_ref, far_ref
):
    rows = send_ref.shape[0] // 2
    index = lax.axis_index(TENSOR)
    chip, core = index // 2, index % 2
    out_far_weights(far_ref, out_x_ref, out_y_ref, out_z_ref)
    goal = 1 - chip if away else chip
    value = out_term(context_ref, out_ref, far_ref, 2 * goal + 1 - core).astype(bf16)
    send_ref[:rows, :] = value[rows:]
    send_ref[rows:, :] = value[:rows]


def output_keep_kernel(
    away, context_ref, out_ref, out_x_ref, out_y_ref, out_z_ref, mine_ref, theirs_ref,
    keep_ref, far_ref,
):
    rows, shard = mine_ref.shape[0], out_ref.shape[0]
    index = lax.axis_index(TENSOR)
    chip, core = index // 2, index % 2
    out_far_weights(far_ref, out_x_ref, out_y_ref, out_z_ref)
    block = 2 * (1 - chip if away else chip) + core
    at = pl.ds(pl.multiple_of(block * shard, shard), shard)
    value = out_term(context_ref, out_ref, far_ref, block)
    keep_ref[:rows, :] = value[:rows] + mine_ref[:, at].astype(f32)
    keep_ref[rows:, :] = value[rows:] + theirs_ref[:, at].astype(f32)


def run_copies(pairs, sems):
    copies = [
        pltpu.make_async_copy(source, goal, sems.at[place])
        for place, (source, goal) in enumerate(pairs)
    ]
    for copy in copies:
        copy.start()
    for copy in copies:
        copy.wait()


def row_pieces(place, depth):
    step = depth // PIECES
    for piece in range(PIECES):
        start = pl.multiple_of(place * depth + piece * step, step)
        yield pl.ds(start, step), pl.ds(piece * step, step)


def pack_first_kernel(qkv_ref, out_ref, send_ref, sems):
    depth, shard = qkv_ref.shape[1] // 2, qkv_ref.shape[2]
    group, parity = lax.axis_index(SONGS), lax.axis_index(FRAME) % 2
    pairs = [
        (qkv_ref.at[1, rows, :], send_ref.at[goal, :]) for rows, goal in row_pieces(group, depth)
    ]
    block = pl.ds(pl.multiple_of((2 * group + parity) * shard, shard), shard)
    for piece in range(2):
        rows = pl.ds(piece * shard // 2, shard // 2)
        goal = pl.ds(depth + piece * shard // 2, shard // 2)
        pairs.append((out_ref.at[rows, block], send_ref.at[goal, :]))
    run_copies(pairs, sems)


def pack_rest_kernel(qkv_ref, send_ref, sems):
    depth = send_ref.shape[1]
    group, parity = lax.axis_index(SONGS), lax.axis_index(FRAME) % 2
    pairs = []
    for slot, which, place in ((0, 0, parity), (1, 2, group)):
        for rows, goal in row_pieces(place, depth):
            pairs.append((qkv_ref.at[which, rows, :], send_ref.at[slot, goal, :]))
    run_copies(pairs, sems)


def pack(kernel, shapes, copies, args):
    return pl.pallas_call(
        kernel,
        out_shape=[jax.ShapeDtypeStruct(shape, bf16) for shape in shapes],
        in_specs=[pl.BlockSpec(memory_space=pltpu.HBM)] * len(args),
        out_specs=[pl.BlockSpec(memory_space=VMEM)] * len(shapes),
        scratch_shapes=[pltpu.SemaphoreType.DMA((copies,))],
        compiler_params=pltpu.CompilerParams(vmem_limit_bytes=4 * 2**20),
        cost_estimate=pl.CostEstimate(flops=0, bytes_accessed=2**20, transcendentals=0),
    )(*[pltpu.with_memory_space_constraint(arg, pltpu.HBM) for arg in args])


def residual_kernel(latent_ref, keep_ref, far_ref, out_ref):
    stems = latent_ref.shape[0]
    index = lax.axis_index(TENSOR)
    chip, core = index // 2, index % 2
    start = pl.multiple_of(chip * WINDOW, WINDOW)
    for stem in range(stems // 2):
        rows = slice(stem * WINDOW, (stem + 1) * WINDOW)
        total = keep_ref[rows, :] + far_ref[rows, :].astype(f32)
        latent = latent_ref[core * (stems // 2) + stem, pl.ds(start, WINDOW), :]
        out_ref[rows, :] = (latent.astype(f32) + total).astype(bf16)


def place(value_ref, out_ref, window, sems):
    stems = out_ref.shape[0]
    core = lax.axis_index(TENSOR) % 2
    half = stems // 2
    at = pl.ds(pl.multiple_of(window * WINDOW, WINDOW), WINDOW)
    pairs = []
    for stem in range(stems):
        goal = (core if stem < half else 1 - core) * half + stem % half
        source = value_ref.at[pl.ds(stem * WINDOW, WINDOW), :]
        pairs.append((source, out_ref.at[goal, at, :]))
    run_copies(pairs, sems)


def place_near_kernel(keep_ref, got_ref, out_ref, value_ref, sems):
    value_ref[...] = (keep_ref[...] + got_ref[...].astype(f32)).astype(bf16)
    place(value_ref, out_ref, lax.axis_index(TENSOR) // 2, sems)


def place_far_kernel(value_ref, near_ref, out_ref, sems):
    del near_ref
    place(value_ref, out_ref, 1 - lax.axis_index(TENSOR) // 2, sems)


def call(kernel, outs, scratch, args, flops=0, moved=0, limit=16):
    return pl.pallas_call(
        kernel,
        out_shape=[jax.ShapeDtypeStruct(shape, dtype) for shape, dtype in outs],
        in_specs=[pl.BlockSpec(memory_space=VMEM)] * len(args),
        out_specs=[pl.BlockSpec(memory_space=VMEM)] * len(outs),
        scratch_shapes=[VMEM(shape, dtype) for shape, dtype in scratch],
        compiler_params=pltpu.CompilerParams(vmem_limit_bytes=limit * 2**20),
        cost_estimate=pl.CostEstimate(flops=flops, bytes_accessed=moved, transcendentals=0),
    )(*args)


def swap_cores(value):
    return lax.ppermute(value, TENSOR, [(0, 1), (1, 0), (2, 3), (3, 2)])


def swap_chips(value):
    return lax.ppermute(value, TENSOR, [(0, 2), (2, 0), (1, 3), (3, 1)])


def swap_groups(value):
    return lax.ppermute(value, SONGS, [(0, 1), (1, 0)])


ONE = ((0, 1), (1, 0), (2, 3), (3, 2))
TWO = ((0, 3), (3, 0), (1, 2), (2, 1))
FAR = ((0, 2), (2, 0), (1, 3), (3, 1))


def trade(value, pairs):
    return lax.ppermute(value, FRAME, pairs)


def trade_by_core(value):
    count = lax.axis_size(TENSOR)
    pairs = [
        (source * count + index, goal * count + index)
        for index in range(count)
        for source, goal in (TWO if index % 2 else ONE)
    ]
    return lax.ppermute(value, (FRAME, TENSOR), pairs)


def fast(
    latent, norm1_gain, conv1_weight, time_bias, norm2_gain, conv2_weight,
    attn_gain, qkv_weight, out_weight,
):
    stems, frames, channels = latent.shape
    frame_size = lax.axis_size(FRAME)
    shard = conv1_weight.shape[2]
    width = channels // GROUPS
    entries = frames * frame_size * width
    half_rows = stems // 2 * WINDOW
    qkv = jnp.transpose(qkv_weight, (1, 0, 2))
    depth = channels // 2
    (first,) = pack(pack_first_kernel, [(depth + shard, shard)], PIECES + 2, [qkv, out_weight])
    (rest,) = pack(pack_rest_kernel, [(2, depth, shard)], 2 * PIECES, [qkv])
    first_x = swap_chips(first)
    rest_x = swap_chips(rest)
    k_x, out_x = first_x[:depth], first_x[depth:]
    q_x, v_x = rest_x[0], rest_x[1]
    out_y = swap_groups(out_x)
    k_y = swap_groups(k_x)
    q_z = trade(q_x, ONE)
    v_y = swap_groups(v_x)
    out_z = trade(jnp.stack([out_x, out_y]), ONE)
    weight1 = swap_cores(conv1_weight)
    weight2 = swap_cores(conv2_weight).reshape(3 * shard, channels)
    bias_far = swap_cores(time_bias)
    gain_far = swap_cores(norm2_gain)
    gain2 = jnp.concatenate([norm2_gain, gain_far])[None]
    wide = channels + 2 * LANES
    near, own = call(
        functools.partial(stats_kernel, width),
        [((stems, wide), f32), ((stems, 2 * LANES), f32)],
        [((stems, channels), f32)] * 2,
        [latent],
    )
    far = trade(own, FAR)
    got = trade_by_core(near)
    swapped = swap_cores(got)
    half, span = stems // 2, 2 * shard
    narrow = span + 2 * LANES
    hid, one2, two2, own2 = call(
        functools.partial(first_kernel, entries, width, frame_size),
        [((half, frames, span), f32), ((half, narrow), f32), ((half, narrow), f32),
         ((half, 2 * LANES), f32)],
        [((half * frames, channels), bf16), ((16, channels), f32)] + [((half, span), f32)] * 2,
        [latent, got, swapped, far, own, norm1_gain[None], conv1_weight, weight1,
         time_bias[None], bias_far[None]],
        flops=6 * stems * frames * channels * shard, limit=24,
    )
    far2 = trade(own2, FAR)
    got_two = trade(two2, TWO)
    got_one = trade(one2, ONE)

    def second(other):
        return call(
            functools.partial(second_kernel, entries, width, frame_size, other),
            [((half_rows, channels), bf16 if other else f32)],
            [((half_rows, 6 * shard), bf16)],
            [hid, got_one, got_two, far2, own2, gain2,
             conv2_weight.reshape(3 * shard, channels), weight2],
            flops=12 * half_rows * channels * shard,
        )[0]

    summed = swap_chips(second(True))
    mine = call(
        residual_kernel, [((half_rows, channels), bf16)], [],
        [latent, second(False), summed],
    )[0]
    theirs = swap_cores(mine)
    weights = [attn_gain[None], qkv, k_x, k_y, q_x, q_z]
    projected = call(
        project_kernel,
        [((half_rows, shard), f32), ((half_rows, 2 * shard), f32), ((half_rows, channels), bf16)],
        [],
        [mine, *weights[:4]],
        flops=6 * half_rows * channels * shard,
    )
    context = call(
        attention_kernel, [((2 * half_rows, 2 * shard), bf16)],
        [((2 * half_rows, channels), bf16)],
        [theirs, *weights, v_x, v_y, *projected],
        flops=24 * half_rows * channels * shard, limit=24,
    )[0]
    inputs = [context, out_weight, out_x, out_y, out_z]
    whole, scratch = (2 * half_rows, shard), [((4, shard, shard), bf16)]
    flops = 2 * half_rows * channels * shard

    def output(away, kept):
        return call(
            functools.partial(output_keep_kernel if kept else output_send_kernel, away),
            [(whole, f32 if kept else bf16)], scratch,
            inputs + [mine, theirs] if kept else inputs, flops=flops,
        )[0]

    send_far, keep_far = output(True, False), output(True, True)
    send_near, keep_near = output(False, False), output(False, True)
    got_far = swap_cores(send_far)
    got_near = swap_cores(send_near)
    away = (keep_far + got_far.astype(f32)).astype(bf16)
    arrived = swap_chips(away)
    vmem, anywhere = pl.BlockSpec(memory_space=VMEM), pl.BlockSpec(memory_space=pl.ANY)
    shape = jax.ShapeDtypeStruct((stems, frames, shard), bf16)
    sems = pltpu.SemaphoreType.DMA((stems,))
    params = pltpu.CompilerParams(vmem_limit_bytes=4 * 2**20)
    near = pl.pallas_call(
        place_near_kernel, name="place_near", out_shape=shape,
        in_specs=[vmem, vmem], out_specs=anywhere, compiler_params=params,
        scratch_shapes=[VMEM((2 * half_rows, shard), bf16), sems],
    )(keep_near, got_near)
    return pl.pallas_call(
        place_far_kernel, name="place_far", out_shape=shape,
        in_specs=[vmem, anywhere], out_specs=anywhere, compiler_params=params,
        scratch_shapes=[sems], input_output_aliases={1: 0},
    )(arrived, near)


def local(*args):
    latent = args[0]
    stems, frames, channels = latent.shape
    tensor_size, frame_size = lax.axis_size(TENSOR), lax.axis_size(FRAME)
    shard = channels // tensor_size
    suits = (
        tensor_size == 4
        and frame_size == 4
        and lax.axis_size(SONGS) == 2
        and frames == 2 * WINDOW
        and stems % 2 == 0
        and stems <= 8
        and shard % (2 * LANES) == 0
    )
    if not suits:
        return generic(*args)
    return fast(*args)


def solution(mesh):
    return jax.shard_map(
        local,
        mesh=mesh,
        in_specs=(
            P(None, (SONGS, FRAME), None),
            P(),
            P(None, None, TENSOR),
            P(TENSOR),
            P(TENSOR),
            P(None, TENSOR, None),
            P(),
            P(None, None, TENSOR),
            P(TENSOR, None),
        ),
        out_specs=P(None, (SONGS, FRAME), TENSOR),
        check_vma=False,
    )
```

```python
import functools
import math

import jax
import jax.numpy as jnp
from jax import lax
from jax.experimental import pallas as pl
from jax.experimental.pallas import tpu as pltpu
from jax.sharding import PartitionSpec as P


TENSOR, FRAME, SONGS = "tensor", "frame", "groups"
GROUPS = 32
HEAD_DIM = 64
WINDOW = 64
LANES = 128
PIECES = 4
CHUNK = 2

norm_eps = 1e-05
rms_eps = 1e-06
HIGHEST = lax.Precision.HIGHEST
VMEM = pltpu.VMEM
bf16 = jnp.bfloat16
f32 = jnp.float32


def extended(block, sides, width):
    for axis, dim in sides:
        count = lax.axis_size(axis)
        forward = [(i, i + 1) for i in range(count - 1)]
        backward = [(target, source) for source, target in forward]
        low = lax.ppermute(
            lax.slice_in_dim(block, block.shape[dim] - width, None, axis=dim), axis, forward
        )
        high = lax.ppermute(lax.slice_in_dim(block, 0, width, axis=dim), axis, backward)
        block = jnp.concatenate([low, block, high], axis=dim)
    return block


def group_sums(hidden, group_count):
    stem_count, frame_count, channels = hidden.shape
    grouped = hidden.reshape(stem_count, frame_count, group_count, channels // group_count)
    return (jnp.sum(grouped, axis=(1, 3)), jnp.sum(grouped * grouped, axis=(1, 3)))


def apply_group(hidden, totals, squares, entries, gain_vec):
    stem_count, frame_count, channels = hidden.shape
    group_count = totals.shape[1]
    centre = totals / entries
    spread = squares / entries - centre * centre
    grouped = hidden.reshape(stem_count, frame_count, group_count, channels // group_count)
    scaled = (grouped - centre[:, None, :, None]) * lax.rsqrt(spread + norm_eps)[:, None, :, None]
    return scaled.reshape(stem_count, frame_count, channels) * gain_vec


def conv_padded(padded, kernel, frame_count):
    stem_count = padded.shape[0]
    channels = padded.shape[2]
    result = jnp.zeros((stem_count * frame_count, kernel.shape[2]), jnp.float32)
    for tap_index in range(3):
        tap_rows = padded[:, tap_index : tap_index + frame_count].reshape(
            stem_count * frame_count, channels
        )
        result = result + jnp.dot(tap_rows, kernel[tap_index], preferred_element_type=jnp.float32)
    return result.reshape(stem_count, frame_count, kernel.shape[2])


def attend(queries, keys_all, values):
    stem_count, frame_count, head_count, head_dim = queries.shape
    window_count = frame_count // WINDOW

    def arrange(source):
        shaped = source.reshape(stem_count, window_count, WINDOW, head_count, head_dim)
        return shaped.transpose(1, 3, 0, 2, 4).reshape(
            window_count, head_count, stem_count * WINDOW, head_dim
        )

    scores = jnp.einsum(
        "nhqd,nhkd->nhqk",
        arrange(queries),
        arrange(keys_all),
        precision=lax.Precision.HIGHEST,
        preferred_element_type=jnp.float32,
    ) / math.sqrt(head_dim)
    scores = scores - jnp.max(scores, axis=3, keepdims=True)
    exp_scores = jnp.exp(scores)
    attn_probs = (exp_scores / jnp.sum(exp_scores, axis=3, keepdims=True)).astype(jnp.bfloat16)
    context = jnp.einsum(
        "nhqk,nhkd->nhqd", attn_probs, arrange(values), preferred_element_type=jnp.float32
    ).astype(jnp.bfloat16)
    context = context.reshape(window_count, head_count, stem_count, WINDOW, head_dim).transpose(
        2, 0, 3, 1, 4
    )
    return context.reshape(stem_count * frame_count, head_count * head_dim)


def generic(
    latent,
    norm1_gain,
    conv1_weight,
    time_bias,
    norm2_gain,
    conv2_weight,
    attn_gain,
    qkv_weight,
    out_weight,
):
    stem_count, frame_count, channels = latent.shape
    tensor_size = lax.axis_size(TENSOR)
    shard_width = channels // tensor_size
    row_count = stem_count * frame_count
    group_entries = frame_count * lax.axis_size(FRAME) * (channels // GROUPS)
    latent_f = latent.astype(jnp.float32)
    sums_one, squares_one = group_sums(latent_f, GROUPS)
    sums_one, squares_one = lax.psum((sums_one, squares_one), FRAME)
    act_one = jax.nn.silu(
        apply_group(latent_f, sums_one, squares_one, group_entries, norm1_gain)
    ).astype(jnp.bfloat16)
    padded_one = extended(act_one, ((FRAME, 1),), 1)
    hid_one = conv_padded(padded_one, conv1_weight, frame_count)
    hid_one = hid_one + time_bias
    local_groups = GROUPS // tensor_size
    sums_two, squares_two = group_sums(hid_one, local_groups)
    sums_two, squares_two = lax.psum((sums_two, squares_two), FRAME)
    act_two = jax.nn.silu(
        apply_group(hid_one, sums_two, squares_two, group_entries, norm2_gain)
    ).astype(jnp.bfloat16)
    padded_two = extended(act_two, ((FRAME, 1),), 1)
    conv_term = conv_padded(padded_two, conv2_weight, frame_count)
    own_start = lax.axis_index(TENSOR) * shard_width
    qkv_flat = qkv_weight.reshape(channels, 3 * shard_width)
    conv_total = lax.psum(conv_term.astype(jnp.bfloat16), TENSOR).astype(jnp.float32)
    residual = (latent_f + conv_total).astype(jnp.bfloat16)
    res_f = residual.astype(jnp.float32)
    mean_sq = jnp.mean(res_f * res_f, axis=2, keepdims=True)
    normed = (res_f * lax.rsqrt(mean_sq + rms_eps) * attn_gain).astype(jnp.bfloat16)
    projected = jnp.dot(
        normed.reshape(row_count, channels), qkv_flat, preferred_element_type=jnp.float32
    )
    res_own = lax.dynamic_slice_in_dim(res_f, own_start, shard_width, 2)
    head_local = shard_width // HEAD_DIM
    projected = projected.reshape(stem_count, frame_count, 3, head_local, HEAD_DIM)
    values = projected[:, :, 2].astype(jnp.bfloat16)
    context = attend(projected[:, :, 0], projected[:, :, 1], values)
    out_term = jnp.dot(context, out_weight, preferred_element_type=jnp.float32).reshape(
        stem_count, frame_count, channels
    )
    attn_share = lax.psum_scatter(
        out_term.astype(jnp.bfloat16), TENSOR, scatter_dimension=2, tiled=True
    ).astype(jnp.float32)
    velocity = (res_own + attn_share).astype(jnp.bfloat16)
    return velocity


def silu_of_half(half):
    return half + half * jnp.tanh(half)


def one_hot(rows, columns, width, by_row):
    row = lax.broadcasted_iota(jnp.int32, (rows, columns), 0)
    column = lax.broadcasted_iota(jnp.int32, (rows, columns), 1)
    if by_row:
        return (row // width == column).astype(f32)
    return (row == column // width).astype(f32)


def f32_dot(a, b):
    return jnp.dot(a, b, precision=HIGHEST, preferred_element_type=f32)


def even_place():
    return lax.axis_index(FRAME) % 2 == 0


def group_totals(sums, squares, width):
    hot = one_hot(sums.shape[1], LANES, width, True)
    return f32_dot(sums, hot), f32_dot(squares, hot)


def channel_scale(refs, entries, channels, width):
    total = refs[0]
    for other in refs[1:]:
        total = total + other
    centre = total[:, :LANES] / entries
    spread = total[:, LANES:] / entries - centre * centre
    hot = one_hot(LANES, channels, width, False)
    return f32_dot(centre, hot), f32_dot(lax.rsqrt(spread + norm_eps), hot)


def stats_kernel(width, lat_ref, near_ref, own_ref, sum_ref, square_ref):
    stems, frames, channels = lat_ref.shape
    upward = even_place() == (lax.axis_index(TENSOR) % 2 == 0)
    for stem in range(stems):
        block = lat_ref[stem].astype(f32)
        sum_ref[stem : stem + 1, :] = jnp.sum(block, axis=0, keepdims=True)
        square_ref[stem : stem + 1, :] = jnp.sum(block * block, axis=0, keepdims=True)
        edge = jnp.where(upward, block[frames - 1 :], block[:1])
        near_ref[stem : stem + 1, :channels] = edge
    sums, squares = group_totals(sum_ref[...], square_ref[...], width)
    for ref, start in ((near_ref, channels), (own_ref, 0)):
        ref[:, start : start + LANES] = sums
        ref[:, start + LANES : start + 2 * LANES] = squares


def pick(value):
    half = value.shape[0] // 2
    return jnp.where(lax.axis_index(TENSOR) % 2 == 0, value[:half], value[half:])


def both_dots(rows, near, away):
    parts = [jnp.dot(rows, weight, preferred_element_type=f32) for weight in (near, away)]
    return jnp.concatenate(parts, axis=1)


def first_kernel(
    entries, width, frame_size,
    lat_ref, got_ref, swapped_ref, far_ref, own_ref, gain_ref, weight_ref, partner_ref,
    bias_ref, bias_far_ref,
    hid_ref, one_ref, two_ref, tot_ref, act_ref, edge_ref, sum_ref, square_ref,
):
    frames, channels = lat_ref.shape[1:]
    stems, _, span = hid_ref.shape
    place = lax.axis_index(FRAME)
    core = lax.axis_index(TENSOR) % 2
    centre, scale = channel_scale(
        [own_ref[...], got_ref[:, channels:], swapped_ref[:, channels:], far_ref[...]],
        entries, channels, width,
    )
    even = even_place()
    first_got = even == (core == 0)
    got, swapped = got_ref[:, :channels], swapped_ref[:, :channels]
    high, low = jnp.where(first_got, got, swapped), jnp.where(first_got, swapped, got)
    scale = scale * (0.5 * gain_ref[...])
    low, high = pick(silu_of_half((low - centre) * scale)), pick(silu_of_half((high - centre) * scale))
    centre, scale = pick(centre), pick(scale)
    edge_ref[...] = jnp.zeros_like(edge_ref)
    edge_ref[0:stems, :] = jnp.where(place > 0, low, 0.0)
    edge_ref[8 : 8 + stems, :] = jnp.where(place < frame_size - 1, high, 0.0)
    edge = edge_ref[...].astype(bf16)
    edge_low = both_dots(edge, weight_ref[0], partner_ref[0])
    edge_high = both_dots(edge, weight_ref[2], partner_ref[2])
    row = lax.broadcasted_iota(jnp.int32, (frames, span), 0)
    bias = jnp.concatenate([bias_ref[...], bias_far_ref[...]], axis=1)
    for stem in range(stems):
        if stem % CHUNK == 0:
            first, last = stem, min(stem + CHUNK, stems)
            for part in range(first, last):
                block = lat_ref[core * stems + part].astype(f32)
                block = (block - centre[part : part + 1]) * scale[part : part + 1]
                act_ref[part * frames : (part + 1) * frames, :] = silu_of_half(block).astype(bf16)
            rows = act_ref[first * frames : last * frames, :]
            taps = [both_dots(rows, weight_ref[tap], partner_ref[tap]) for tap in range(3)]
        lo = (stem - first) * frames
        before = pltpu.roll(taps[0][lo : lo + frames], 1, 0)
        after = pltpu.roll(taps[2][lo : lo + frames], frames - 1, 0)
        before = jnp.where(row == 0, edge_low[stem : stem + 1], before)
        after = jnp.where(row == frames - 1, edge_high[8 + stem : 9 + stem], after)
        hid = taps[1][lo : lo + frames] + before + after + bias
        hid_ref[stem] = hid
        sum_ref[stem : stem + 1, :] = jnp.sum(hid, axis=0, keepdims=True)
        square_ref[stem : stem + 1, :] = jnp.sum(hid * hid, axis=0, keepdims=True)
        down, up = hid[:1], hid[frames - 1 :]
        one_ref[stem : stem + 1, :span] = jnp.where(even, up, down)
        two_ref[stem : stem + 1, :span] = jnp.where(even, down, up)
    sums, squares = group_totals(sum_ref[...], square_ref[...], width)
    for ref, start in ((one_ref, span), (two_ref, span), (tot_ref, 0)):
        ref[:, start : start + LANES] = sums
        ref[:, start + LANES : start + 2 * LANES] = squares


def second_kernel(
    entries, width, frame_size, other,
    hid_ref, one_ref, two_ref, far_ref, own_ref, gain_ref, weight_ref, partner_ref,
    total_ref, act_ref,
):
    stems, _, span = hid_ref.shape
    shard = span // 2
    place = lax.axis_index(FRAME)
    chip = lax.axis_index(TENSOR) // 2
    window = 1 - chip if other else chip
    centre, scale = channel_scale(
        [own_ref[...], one_ref[:, span:], two_ref[:, span:], far_ref[...]],
        entries, span, width,
    )
    even = even_place()
    one, two = one_ref[:, :span], two_ref[:, :span]
    high, low = jnp.where(even, one, two), jnp.where(even, two, one)
    scale = scale * (0.5 * gain_ref[...])
    low = jnp.where(place > 0, silu_of_half((low - centre) * scale), 0.0)
    high = jnp.where(place < frame_size - 1, silu_of_half((high - centre) * scale), 0.0)
    row = lax.broadcasted_iota(jnp.int32, (WINDOW, span), 0)
    start = pl.multiple_of(window * WINDOW, WINDOW)
    for stem in range(stems):
        mean, factor = centre[stem : stem + 1], scale[stem : stem + 1]
        act = silu_of_half((hid_ref[stem, pl.ds(start, WINDOW), :] - mean) * factor)
        inner = silu_of_half((hid_ref[stem, WINDOW - 8 : WINDOW + 8, :] - mean) * factor)
        before = jnp.where(window == 0, low[stem : stem + 1], inner[7:8])
        after = jnp.where(window == 0, inner[8:9], high[stem : stem + 1])
        before = jnp.where(row == 0, before, pltpu.roll(act, 1, 0))
        after = jnp.where(row == WINDOW - 1, after, pltpu.roll(act, WINDOW - 1, 0))
        at = slice(stem * WINDOW, (stem + 1) * WINDOW)
        for tap, value in enumerate((before, act, after)):
            value = value.astype(bf16)
            act_ref[at, tap * shard : (tap + 1) * shard] = value[:, :shard]
            act_ref[at, (3 + tap) * shard : (4 + tap) * shard] = value[:, shard:]
    total = jnp.dot(act_ref[:, : 3 * shard], weight_ref[...], preferred_element_type=f32)
    total = total + jnp.dot(
        act_ref[:, 3 * shard :], partner_ref[...], preferred_element_type=f32
    )
    total_ref[...] = total.astype(total_ref.dtype)


def split2(value):
    high = value.astype(bf16)
    return high, (value - high.astype(f32)).astype(bf16)


def normed_rows(res, gain_ref):
    mean_sq = jnp.mean(res * res, axis=1, keepdims=True)
    return (res * lax.rsqrt(mean_sq + rms_eps) * gain_ref[...]).astype(bf16)


def projector(normed_ref, qkv_ref, k_x_ref, k_y_ref, q_x_ref, q_z_ref, v_refs=()):
    depth = normed_ref.shape[1] // 2
    group, parity = lax.axis_index(SONGS), lax.axis_index(FRAME) % 2

    def half(place):
        return normed_ref[:, pl.ds(pl.multiple_of(place * depth, depth), depth)]

    def project(side, which):
        if side == 0:
            return jnp.dot(normed_ref[...], qkv_ref[which], preferred_element_type=f32)
        if which == 0:
            place, near, away = parity, q_x_ref[...], q_z_ref[...]
        elif which == 1:
            place, near, away = group, k_x_ref[...], k_y_ref[...]
        else:
            place, near, away = group, v_refs[0][...], v_refs[1][...]
        value = jnp.dot(half(place), near, preferred_element_type=f32)
        return value + jnp.dot(half(1 - place), away, preferred_element_type=f32)

    return project


def project_kernel(
    mine_ref, gain_ref, qkv_ref, k_x_ref, k_y_ref, q_x_ref, q_z_ref,
    queries_ref, keys_ref, normed_ref,
):
    shard = qkv_ref.shape[2]
    normed_ref[...] = normed_rows(mine_ref[...].astype(f32), gain_ref)
    project = projector(normed_ref, qkv_ref, k_x_ref, k_y_ref, q_x_ref, q_z_ref)
    for side in range(2):
        at = slice(side * shard, (side + 1) * shard)
        queries_ref[:, at] = project(side, 0)
        keys_ref[:, at] = project(side, 1)


def attention_kernel(
    theirs_ref, gain_ref, qkv_ref, k_x_ref, k_y_ref, q_x_ref, q_z_ref, v_x_ref, v_y_ref,
    queries_ref, keys_ref, mine_ref,
    context_ref, normed_ref,
):
    rows = theirs_ref.shape[0]
    shard = qkv_ref.shape[2]
    normed_ref[:rows, :] = mine_ref[...]
    normed_ref[rows:, :] = normed_rows(theirs_ref[...].astype(f32), gain_ref)
    weights = qkv_ref, k_x_ref, k_y_ref, q_x_ref, q_z_ref
    project = projector(normed_ref.at[pl.ds(rows, rows), :], *weights)
    project_all = projector(normed_ref, *weights, (v_x_ref, v_y_ref))
    lane = lax.broadcasted_iota(jnp.int32, (2 * rows, LANES), 1)
    nt = (((1,), (1,)), ((), ()))
    for side in range(2):
        span = slice(side * shard, (side + 1) * shard)
        queries, keys = [
            jnp.concatenate([ref[:, span], project(side, which)], axis=0)
            for which, ref in enumerate((queries_ref, keys_ref))
        ]
        values = project_all(side, 2)
        queries = queries * (math.log2(math.e) / math.sqrt(HEAD_DIM))
        for tile in range(shard // LANES):
            at = slice(tile * LANES, (tile + 1) * LANES)
            q_high, q_low = split2(queries[:, at])
            q_low = pltpu.roll(q_low.astype(f32), HEAD_DIM, 1).astype(bf16)
            k_high, k_low = split2(keys[:, at])
            k_rolled = split2(pltpu.roll(keys[:, at], HEAD_DIM, 1))
            terms, mixing = [], []
            for head in range(LANES // HEAD_DIM):
                inside = lane // HEAD_DIM == head
                left = jnp.where(inside, q_high, q_low)
                left = jnp.concatenate([left, left], axis=1)
                right = [
                    jnp.where(inside, own, rolled)
                    for own, rolled in zip((k_high, k_low), k_rolled)
                ]
                right = jnp.concatenate(right, axis=1)
                scores = lax.dot_general(left, right, nt, preferred_element_type=f32)
                scores = jnp.exp2(scores - jnp.max(scores, axis=1, keepdims=True))
                terms.append(scores.astype(bf16))
                mixing.append(
                    jnp.concatenate(
                        [jnp.where(inside, values[:, at], 0.0), jnp.where(inside, 1.0, 0.0)], axis=1
                    ).astype(bf16)
                )
            mixed = jnp.dot(
                jnp.concatenate(terms, axis=1), jnp.concatenate(mixing, axis=0),
                preferred_element_type=f32,
            )
            base = side * shard + tile * LANES
            context_ref[:, base : base + LANES] = (mixed[:, :LANES] / mixed[:, LANES:]).astype(bf16)


def out_far_weights(goal_ref, out_x_ref, out_y_ref, out_z_ref):
    group, parity = lax.axis_index(SONGS), lax.axis_index(FRAME) % 2
    goal_ref[2 * group + parity] = out_x_ref[...]
    goal_ref[2 * (1 - group) + parity] = out_y_ref[...]
    goal_ref[2 * group + 1 - parity] = out_z_ref[0]
    goal_ref[2 * (1 - group) + 1 - parity] = out_z_ref[1]


def out_term(context_ref, out_ref, far_ref, block):
    shard = out_ref.shape[0]
    at = pl.ds(pl.multiple_of(block * shard, shard), shard)
    value = jnp.dot(context_ref[:, :shard], out_ref[:, at], preferred_element_type=f32)
    return value + jnp.dot(context_ref[:, shard:], far_ref[block], preferred_element_type=f32)


def output_send_kernel(
    away, context_ref, out_ref, out_x_ref, out_y_ref, out_z_ref, send_ref, far_ref
):
    rows = send_ref.shape[0] // 2
    index = lax.axis_index(TENSOR)
    chip, core = index // 2, index % 2
    out_far_weights(far_ref, out_x_ref, out_y_ref, out_z_ref)
    goal = 1 - chip if away else chip
    value = out_term(context_ref, out_ref, far_ref, 2 * goal + 1 - core).astype(bf16)
    send_ref[:rows, :] = value[rows:]
    send_ref[rows:, :] = value[:rows]


def output_keep_kernel(
    away, context_ref, out_ref, out_x_ref, out_y_ref, out_z_ref, mine_ref, theirs_ref,
    keep_ref, far_ref,
):
    rows, shard = mine_ref.shape[0], out_ref.shape[0]
    index = lax.axis_index(TENSOR)
    chip, core = index // 2, index % 2
    out_far_weights(far_ref, out_x_ref, out_y_ref, out_z_ref)
    block = 2 * (1 - chip if away else chip) + core
    at = pl.ds(pl.multiple_of(block * shard, shard), shard)
    value = out_term(context_ref, out_ref, far_ref, block)
    keep_ref[:rows, :] = value[:rows] + mine_ref[:, at].astype(f32)
    keep_ref[rows:, :] = value[rows:] + theirs_ref[:, at].astype(f32)


def run_copies(pairs, sems):
    copies = [
        pltpu.make_async_copy(source, goal, sems.at[place])
        for place, (source, goal) in enumerate(pairs)
    ]
    for copy in copies:
        copy.start()
    for copy in copies:
        copy.wait()


def row_pieces(place, depth):
    step = depth // PIECES
    for piece in range(PIECES):
        start = pl.multiple_of(place * depth + piece * step, step)
        yield pl.ds(start, step), pl.ds(piece * step, step)


def pack_first_kernel(qkv_ref, out_ref, send_ref, sems):
    depth, shard = qkv_ref.shape[1] // 2, qkv_ref.shape[2]
    group, parity = lax.axis_index(SONGS), lax.axis_index(FRAME) % 2
    pairs = [
        (qkv_ref.at[1, rows, :], send_ref.at[goal, :]) for rows, goal in row_pieces(group, depth)
    ]
    block = pl.ds(pl.multiple_of((2 * group + parity) * shard, shard), shard)
    for piece in range(2):
        rows = pl.ds(piece * shard // 2, shard // 2)
        goal = pl.ds(depth + piece * shard // 2, shard // 2)
        pairs.append((out_ref.at[rows, block], send_ref.at[goal, :]))
    run_copies(pairs, sems)


def pack_rest_kernel(qkv_ref, send_ref, sems):
    depth = send_ref.shape[1]
    group, parity = lax.axis_index(SONGS), lax.axis_index(FRAME) % 2
    pairs = []
    for slot, which, place in ((0, 0, parity), (1, 2, group)):
        for rows, goal in row_pieces(place, depth):
            pairs.append((qkv_ref.at[which, rows, :], send_ref.at[slot, goal, :]))
    run_copies(pairs, sems)


def pack(kernel, shapes, copies, args):
    return pl.pallas_call(
        kernel,
        out_shape=[jax.ShapeDtypeStruct(shape, bf16) for shape in shapes],
        in_specs=[pl.BlockSpec(memory_space=pltpu.HBM)] * len(args),
        out_specs=[pl.BlockSpec(memory_space=VMEM)] * len(shapes),
        scratch_shapes=[pltpu.SemaphoreType.DMA((copies,))],
        compiler_params=pltpu.CompilerParams(vmem_limit_bytes=4 * 2**20),
        cost_estimate=pl.CostEstimate(flops=0, bytes_accessed=2**20, transcendentals=0),
    )(*[pltpu.with_memory_space_constraint(arg, pltpu.HBM) for arg in args])


def residual_kernel(latent_ref, keep_ref, far_ref, out_ref):
    stems = latent_ref.shape[0]
    index = lax.axis_index(TENSOR)
    chip, core = index // 2, index % 2
    start = pl.multiple_of(chip * WINDOW, WINDOW)
    for stem in range(stems // 2):
        rows = slice(stem * WINDOW, (stem + 1) * WINDOW)
        total = keep_ref[rows, :] + far_ref[rows, :].astype(f32)
        latent = latent_ref[core * (stems // 2) + stem, pl.ds(start, WINDOW), :]
        out_ref[rows, :] = (latent.astype(f32) + total).astype(bf16)


def place(value_ref, out_ref, window, sems):
    stems = out_ref.shape[0]
    core = lax.axis_index(TENSOR) % 2
    half = stems // 2
    at = pl.ds(pl.multiple_of(window * WINDOW, WINDOW), WINDOW)
    pairs = []
    for stem in range(stems):
        goal = (core if stem < half else 1 - core) * half + stem % half
        source = value_ref.at[pl.ds(stem * WINDOW, WINDOW), :]
        pairs.append((source, out_ref.at[goal, at, :]))
    run_copies(pairs, sems)


def place_near_kernel(keep_ref, got_ref, out_ref, value_ref, sems):
    value_ref[...] = (keep_ref[...] + got_ref[...].astype(f32)).astype(bf16)
    place(value_ref, out_ref, lax.axis_index(TENSOR) // 2, sems)


def place_far_kernel(value_ref, near_ref, out_ref, sems):
    del near_ref
    place(value_ref, out_ref, 1 - lax.axis_index(TENSOR) // 2, sems)


def call(kernel, outs, scratch, args, flops=0, moved=0, limit=16):
    return pl.pallas_call(
        kernel,
        out_shape=[jax.ShapeDtypeStruct(shape, dtype) for shape, dtype in outs],
        in_specs=[pl.BlockSpec(memory_space=VMEM)] * len(args),
        out_specs=[pl.BlockSpec(memory_space=VMEM)] * len(outs),
        scratch_shapes=[VMEM(shape, dtype) for shape, dtype in scratch],
        compiler_params=pltpu.CompilerParams(vmem_limit_bytes=limit * 2**20),
        cost_estimate=pl.CostEstimate(flops=flops, bytes_accessed=moved, transcendentals=0),
    )(*args)


def swap_cores(value):
    return lax.ppermute(value, TENSOR, [(0, 1), (1, 0), (2, 3), (3, 2)])


def swap_chips(value):
    return lax.ppermute(value, TENSOR, [(0, 2), (2, 0), (1, 3), (3, 1)])


def swap_groups(value):
    return lax.ppermute(value, SONGS, [(0, 1), (1, 0)])


ONE = ((0, 1), (1, 0), (2, 3), (3, 2))
TWO = ((0, 3), (3, 0), (1, 2), (2, 1))
FAR = ((0, 2), (2, 0), (1, 3), (3, 1))


def trade(value, pairs):
    return lax.ppermute(value, FRAME, pairs)


def trade_by_core(value):
    count = lax.axis_size(TENSOR)
    pairs = [
        (source * count + index, goal * count + index)
        for index in range(count)
        for source, goal in (TWO if index % 2 else ONE)
    ]
    return lax.ppermute(value, (FRAME, TENSOR), pairs)


def fast(
    latent, norm1_gain, conv1_weight, time_bias, norm2_gain, conv2_weight,
    attn_gain, qkv_weight, out_weight,
):
    stems, frames, channels = latent.shape
    frame_size = lax.axis_size(FRAME)
    shard = conv1_weight.shape[2]
    width = channels // GROUPS
    entries = frames * frame_size * width
    half_rows = stems // 2 * WINDOW
    qkv = jnp.transpose(qkv_weight, (1, 0, 2))
    depth = channels // 2
    (first,) = pack(pack_first_kernel, [(depth + shard, shard)], PIECES + 2, [qkv, out_weight])
    (rest,) = pack(pack_rest_kernel, [(2, depth, shard)], 2 * PIECES, [qkv])
    first_x = swap_chips(first)
    rest_x = swap_chips(rest)
    k_x, out_x = first_x[:depth], first_x[depth:]
    q_x, v_x = rest_x[0], rest_x[1]
    out_y = swap_groups(out_x)
    k_y = swap_groups(k_x)
    q_z = trade(q_x, ONE)
    v_y = swap_groups(v_x)
    out_z = trade(jnp.stack([out_x, out_y]), ONE)
    weight1 = swap_cores(conv1_weight)
    weight2 = swap_cores(conv2_weight).reshape(3 * shard, channels)
    bias_far = swap_cores(time_bias)
    gain_far = swap_cores(norm2_gain)
    gain2 = jnp.concatenate([norm2_gain, gain_far])[None]
    wide = channels + 2 * LANES
    near, own = call(
        functools.partial(stats_kernel, width),
        [((stems, wide), f32), ((stems, 2 * LANES), f32)],
        [((stems, channels), f32)] * 2,
        [latent],
    )
    far = trade(own, FAR)
    got = trade_by_core(near)
    swapped = swap_cores(got)
    half, span = stems // 2, 2 * shard
    narrow = span + 2 * LANES
    hid, one2, two2, own2 = call(
        functools.partial(first_kernel, entries, width, frame_size),
        [((half, frames, span), f32), ((half, narrow), f32), ((half, narrow), f32),
         ((half, 2 * LANES), f32)],
        [((half * frames, channels), bf16), ((16, channels), f32)] + [((half, span), f32)] * 2,
        [latent, got, swapped, far, own, norm1_gain[None], conv1_weight, weight1,
         time_bias[None], bias_far[None]],
        flops=6 * stems * frames * channels * shard, limit=24,
    )
    far2 = trade(own2, FAR)
    got_two = trade(two2, TWO)
    got_one = trade(one2, ONE)

    def second(other):
        return call(
            functools.partial(second_kernel, entries, width, frame_size, other),
            [((half_rows, channels), bf16 if other else f32)],
            [((half_rows, 6 * shard), bf16)],
            [hid, got_one, got_two, far2, own2, gain2,
             conv2_weight.reshape(3 * shard, channels), weight2],
            flops=12 * half_rows * channels * shard,
        )[0]

    summed = swap_chips(second(True))
    mine = call(
        residual_kernel, [((half_rows, channels), bf16)], [],
        [latent, second(False), summed],
    )[0]
    theirs = swap_cores(mine)
    weights = [attn_gain[None], qkv, k_x, k_y, q_x, q_z]
    projected = call(
        project_kernel,
        [((half_rows, 2 * shard), f32)] * 2 + [((half_rows, channels), bf16)], [],
        [mine, *weights],
        flops=8 * half_rows * channels * shard,
    )
    context = call(
        attention_kernel, [((2 * half_rows, 2 * shard), bf16)],
        [((2 * half_rows, channels), bf16)],
        [theirs, *weights, v_x, v_y, *projected],
        flops=24 * half_rows * channels * shard, limit=24,
    )[0]
    inputs = [context, out_weight, out_x, out_y, out_z]
    whole, scratch = (2 * half_rows, shard), [((4, shard, shard), bf16)]
    flops = 2 * half_rows * channels * shard

    def output(away, kept):
        return call(
            functools.partial(output_keep_kernel if kept else output_send_kernel, away),
            [(whole, f32 if kept else bf16)], scratch,
            inputs + [mine, theirs] if kept else inputs, flops=flops,
        )[0]

    send_far, keep_far = output(True, False), output(True, True)
    send_near, keep_near = output(False, False), output(False, True)
    got_far = swap_cores(send_far)
    got_near = swap_cores(send_near)
    away = (keep_far + got_far.astype(f32)).astype(bf16)
    arrived = swap_chips(away)
    vmem, anywhere = pl.BlockSpec(memory_space=VMEM), pl.BlockSpec(memory_space=pl.ANY)
    shape = jax.ShapeDtypeStruct((stems, frames, shard), bf16)
    sems = pltpu.SemaphoreType.DMA((stems,))
    params = pltpu.CompilerParams(vmem_limit_bytes=4 * 2**20)
    near = pl.pallas_call(
        place_near_kernel, name="place_near", out_shape=shape,
        in_specs=[vmem, vmem], out_specs=anywhere, compiler_params=params,
        scratch_shapes=[VMEM((2 * half_rows, shard), bf16), sems],
    )(keep_near, got_near)
    return pl.pallas_call(
        place_far_kernel, name="place_far", out_shape=shape,
        in_specs=[vmem, anywhere], out_specs=anywhere, compiler_params=params,
        scratch_shapes=[sems], input_output_aliases={1: 0},
    )(arrived, near)


def local(*args):
    latent = args[0]
    stems, frames, channels = latent.shape
    tensor_size, frame_size = lax.axis_size(TENSOR), lax.axis_size(FRAME)
    shard = channels // tensor_size
    suits = (
        tensor_size == 4
        and frame_size == 4
        and lax.axis_size(SONGS) == 2
        and frames == 2 * WINDOW
        and stems % 2 == 0
        and stems <= 8
        and shard % (2 * LANES) == 0
    )
    if not suits:
        return generic(*args)
    return fast(*args)


def solution(mesh):
    return jax.shard_map(
        local,
        mesh=mesh,
        in_specs=(
            P(None, (SONGS, FRAME), None),
            P(),
            P(None, None, TENSOR),
            P(TENSOR),
            P(TENSOR),
            P(None, TENSOR, None),
            P(),
            P(None, None, TENSOR),
            P(TENSOR, None),
        ),
        out_specs=P(None, (SONGS, FRAME), TENSOR),
        check_vma=False,
    )
```
